32 devices in a mesh: nodes: 32 (over z, y, x, core).
Axes of the slice: x: 2, y: 2, z: 4, core: 2. Of those that a mesh axis runs over, the one named last changes fastest.
Arguments:
- features: bfloat16 [131072, 602], P('nodes'), may hold values from -6 to 6
- labels: int32 [131072, 121], P('nodes'), may hold values 0 or 1
- labelled: int32 [131072], P('nodes'), may hold values 0 or 1
- label_count: int32 [1], replicated, may hold values from 65536 to 131072
- need_blocks: int32 [32, 32, 2], P('nodes'), may hold values from 0 to 31
- need_count: int32 [32, 32], P('nodes'), may hold values from 1 to 2
- target_block: int32 [32, 32, 2], P('nodes'), may hold values from 0 to 31
- adjacency: bfloat16 [2048, 128, 128], P('nodes'), may hold values from 0 to 0.14355469
- embed_weight: float32 [602, 512], replicated, may hold values from -0.25 to 0.25
- pair_weight: float32 [1, 2, 512, 512], replicated, may hold values from -0.25 to 0.25
- merge_weight: float32 [1, 1024, 512], replicated, may hold values from -0.1875 to 0.1875
- head_weight: float32 [512, 121], replicated, may hold values from -0.25 to 0.25
- embed_moment: float32 [602, 512], replicated, may hold values from -2.9802322e-07 to 2.9802322e-07
- pair_moment: float32 [1, 2, 512, 512], replicated, may hold values from -2.9802322e-07 to 2.9802322e-07
- merge_moment: float32 [1, 1024, 512], replicated, may hold values from -2.9802322e-07 to 2.9802322e-07
- head_moment: float32 [512, 121], replicated, may hold values from -8.34465e-07 to 8.34465e-07
- embed_variance: float32 [602, 512], replicated, may hold values from 2.8863303e-17 to 1.1785848e-16
- pair_variance: float32 [1, 2, 512, 512], replicated, may hold values from 2.8863303e-17 to 1.1785848e-16
- merge_variance: float32 [1, 1024, 512], replicated, may hold values from 2.8863303e-17 to 1.1785848e-16
- head_variance: float32 [512, 121], replicated, may hold values from 2.5444234e-16 to 1.0177694e-15
Outputs:
- loss_value: float32 [1], replicated
- embed_updated: float32 [602, 512], replicated
- pair_updated: float32 [1, 2, 512, 512], replicated
- merge_updated: float32 [1, 1024, 512], replicated
- head_updated: float32 [512, 121], replicated
- embed_momentum: float32 [602, 512], replicated
- pair_momentum: float32 [1, 2, 512, 512], replicated
- merge_momentum: float32 [1, 1024, 512], replicated
- head_momentum: float32 [512, 121], replicated
- embed_squares: float32 [602, 512], replicated
- pair_squares: float32 [1, 2, 512, 512], replicated
- merge_squares: float32 [1, 1024, 512], replicated
- head_squares: float32 [512, 121], replicated
The draws below stay inside these ranges and needn't reach their ends.
Inputs may be any that keep to these rules, and one draw needn't show every extreme that they name: `need_blocks`: block indices within an owner's blocks. `need_count`: live slots per device pair. `target_block`: block indices within the taking device's blocks.
All inputs are finite; a program needn't handle non-finite values. No bound on the sum of `labels` or of `labelled` on one device may be relied on, other than what follows from the above.
Results may differ from the reference program's by a relative error of at most 0.008.
Values may be sent and summed in bfloat16 or wider, within the bound.
A program may use at most 448 MiB of HBM per device.

```python
import math
import jax
import jax.numpy as jnp
from jax import lax

FEATURES = 602
HIDDEN_SIZE = 512
LABELS = 121
LAYERS = 1
BLOCK = 128
SLOTS = 2
ROWS_DEV = 4096
BLOCKS_DEV = 32
NODES = 131072
N_NODES = 32


def place_ends(drawn, stream_key, low, largest):
    spot = [jax.random.randint(jax.random.fold_in(stream_key, axis), (), 0, length) for axis, length in enumerate(drawn.shape)]
    main_axis = drawn.shape.index(max(drawn.shape))
    beside = spot[:main_axis] + [(spot[main_axis] + 1) % drawn.shape[main_axis]] + spot[main_axis + 1:]
    return drawn.at[tuple(spot)].set(low).at[tuple(beside)].set(largest)


def shard_levels(stream_key, extent, cuts, low, largest):
    def one(axis_at, blocks):
        heights = jax.random.uniform(jax.random.fold_in(jax.random.fold_in(stream_key, 6), axis_at), (blocks,), jnp.float32, low / len(cuts), largest / len(cuts))
        return jnp.repeat(jnp.exp(heights), extent[axis_at] // blocks).reshape((-1,) + (1,) * (len(extent) - axis_at - 1))

    factor_of = one(*cuts[0])
    for cut in cuts[1:]:
        factor_of = factor_of * one(*cut)
    return factor_of


def centred(rng, shape, spread, limit, shards=(), kind=jnp.bfloat16):
    loudness = shard_levels(rng, shape, shards, -0.22, 0.18) if shards else 1.0
    result = jax.random.normal(rng, shape, jnp.float32) * spread * loudness
    return jnp.minimum(jnp.maximum(result, -limit), limit).astype(kind)


def setup_inputs(seed: int = 0) -> dict:
    key_list = jax.random.split(jax.random.key(seed), 21)
    features = centred(key_list[0], (NODES, FEATURES), 1.0, 6.0, ((0, 32),))
    labels = place_ends((jax.random.randint(key_list[1], (NODES, LABELS), 0, 2) < 1).astype(jnp.int32), jax.random.fold_in(key_list[1], 1), 0, 1)
    labelled = place_ends((jax.random.randint(key_list[2], (NODES,), 0, 3) < 2).astype(jnp.int32), jax.random.fold_in(key_list[2], 1), 0, 1)
    label_count = jax.random.randint(key_list[3], (1,), NODES // 2, NODES + 1).astype(jnp.int32)
    need_blocks = place_ends(jax.random.randint(key_list[4], (N_NODES, N_NODES, SLOTS), 0, BLOCKS_DEV), jax.random.fold_in(key_list[4], 1), 0, BLOCKS_DEV - 1).astype(jnp.int32)
    need_count = place_ends(jax.random.randint(key_list[5], (N_NODES, N_NODES), 1, SLOTS + 1), jax.random.fold_in(key_list[5], 1), 1, SLOTS).astype(jnp.int32)
    target_block = place_ends(jax.random.randint(key_list[6], (N_NODES, N_NODES, SLOTS), 0, BLOCKS_DEV), jax.random.fold_in(key_list[6], 1), 0, BLOCKS_DEV - 1).astype(jnp.int32)
    adjacency = jnp.clip(0.14355469 * jax.random.uniform(key_list[7], (N_NODES * N_NODES * SLOTS, BLOCK, BLOCK), jnp.float32) ** shard_levels(key_list[7], (N_NODES * N_NODES * SLOTS, BLOCK, BLOCK), ((0, 32),), -0.2, 0.2), 0.0, 0.14355469).astype(jnp.bfloat16)
    embed_weight = centred(key_list[8], (FEATURES, HIDDEN_SIZE), FEATURES ** -0.5, 0.25, (), jnp.float32)
    pair_weight = centred(key_list[9], (LAYERS, 2, HIDDEN_SIZE, HIDDEN_SIZE), HIDDEN_SIZE ** -0.5, 0.25, (), jnp.float32)
    merge_weight = centred(key_list[10], (LAYERS, 2 * HIDDEN_SIZE, HIDDEN_SIZE), (2 * HIDDEN_SIZE) ** -0.5, 0.1875, (), jnp.float32)
    head_weight = centred(key_list[11], (HIDDEN_SIZE, LABELS), HIDDEN_SIZE ** -0.5, 0.25, (), jnp.float32)
    embed_moment = centred(key_list[12], (FEATURES, HIDDEN_SIZE), (0.039 * (LABELS * NODES) ** -0.5 / HIDDEN_SIZE), 2.980232238769531e-07, (), jnp.float32)
    pair_moment = centred(key_list[13], (LAYERS, 2, HIDDEN_SIZE, HIDDEN_SIZE), (0.039 * (LABELS * NODES) ** -0.5 / HIDDEN_SIZE), 2.980232238769531e-07, (), jnp.float32)
    merge_moment = centred(key_list[14], (LAYERS, 2 * HIDDEN_SIZE, HIDDEN_SIZE), (0.039 * (LABELS * NODES) ** -0.5 / HIDDEN_SIZE), 2.980232238769531e-07, (), jnp.float32)
    head_moment = centred(key_list[15], (HIDDEN_SIZE, LABELS), (0.055 * (LABELS * LABELS * NODES * HIDDEN_SIZE) ** -0.5), 8.344650268554688e-07, (), jnp.float32)
    embed_variance = jnp.clip(jnp.exp(jax.random.uniform(key_list[16], (FEATURES, HIDDEN_SIZE), jnp.float32, math.log(2.8863302804735426e-17), math.log(1.178584803866785e-16))), 2.8863302804735426e-17, 1.178584803866785e-16)
    pair_variance = jnp.clip(jnp.exp(jax.random.uniform(key_list[17], (LAYERS, 2, HIDDEN_SIZE, HIDDEN_SIZE), jnp.float32, math.log(2.8863302804735426e-17), math.log(1.178584803866785e-16))), 2.8863302804735426e-17, 1.178584803866785e-16)
    merge_variance = jnp.clip(jnp.exp(jax.random.uniform(key_list[18], (LAYERS, 2 * HIDDEN_SIZE, HIDDEN_SIZE), jnp.float32, math.log(2.8863302804735426e-17), math.log(1.178584803866785e-16))), 2.8863302804735426e-17, 1.178584803866785e-16)
    head_variance = jnp.clip(jnp.exp(jax.random.uniform(key_list[19], (HIDDEN_SIZE, LABELS), jnp.float32, math.log(2.544423446080874e-16), math.log(1.0177693784323497e-15))), 2.544423446080874e-16, 1.0177693784323497e-15)
    return dict(features=features, labels=labels, labelled=labelled, label_count=label_count, need_blocks=need_blocks, need_count=need_count, target_block=target_block, adjacency=adjacency, embed_weight=embed_weight, pair_weight=pair_weight, merge_weight=merge_weight, head_weight=head_weight, embed_moment=embed_moment, pair_moment=pair_moment, merge_moment=merge_moment, head_moment=head_moment, embed_variance=embed_variance, pair_variance=pair_variance, merge_variance=merge_variance, head_variance=head_variance)


@jax.custom_vjp
def low(v):
    return lax.optimization_barrier(v.astype(jnp.bfloat16)).astype(jnp.float32)

@jax.custom_vjp
def low_back(v):
    return v

def low_keep(v):
    return (low(v), None)

def low_pass(kept, grad):
    return (grad,)

def back_keep(v):
    return (v, None)

def back_low(kept, grad):
    return (low(grad),)
low.defvjp(low_keep, low_pass)
low_back.defvjp(back_keep, back_low)
norm_eps = 1e-06
learn_rate = 0.03
beta_one = 0.9
beta_two = 0.999
adam_eps = 1e-08
decay_rate = 0.01
adam_step = 10.0

def dense(former, latter):
    return jnp.dot(former, latter, precision=lax.Precision.HIGHEST, preferred_element_type=jnp.float32)

def adam_update(weight, grad, first, second):
    first_new = beta_one * first + (1.0 - beta_one) * grad
    second_new = beta_two * second + (1.0 - beta_two) * grad * grad
    first_hat = first_new / (1.0 - beta_one ** adam_step)
    second_hat = second_new / (1.0 - beta_two ** adam_step)
    weight_new = weight - learn_rate * (first_hat / (jnp.sqrt(second_hat) + adam_eps) + decay_rate * weight)
    return (weight_new, first_new, second_new)

def reference(features, labels, labelled, label_count, need_blocks, need_count, target_block, adjacency, embed_weight, pair_weight, merge_weight, head_weight, embed_moment, pair_moment, merge_moment, head_moment, embed_variance, pair_variance, merge_variance, head_variance):
    device_count = N_NODES
    slot_count = device_count * SLOTS
    inputs = features.astype(jnp.float32)
    truth = labels.astype(jnp.float32)
    row_mask = labelled.astype(jnp.float32)[:, None]
    live = jnp.arange(SLOTS, dtype=jnp.int32)[None, None, :] < need_count[:, :, None]
    edge_weights = adjacency.astype(jnp.float32).reshape(device_count, slot_count, BLOCK, BLOCK)
    edge_weights = edge_weights * live.reshape(device_count, slot_count)[:, :, None, None].astype(jnp.float32)
    owners = jnp.arange(device_count, dtype=jnp.int32)[None, :, None] * BLOCKS_DEV
    sources = (owners + need_blocks.astype(jnp.int32)).reshape(device_count, slot_count)
    sinks = target_block.astype(jnp.int32).reshape(device_count, slot_count)
    denom = label_count[0].astype(jnp.float32) * LABELS

    def aggregate(hidden_half):
        table = hidden_half.reshape(device_count * BLOCKS_DEV, BLOCK, HIDDEN_SIZE)

        def one_device(pieces):
            block_weights, block_sources, block_sinks = pieces
            received = low_back(table[block_sources])
            products = jnp.einsum('kab,kbh->kah', block_weights, received, precision=lax.Precision.HIGHEST)
            summed = jax.ops.segment_sum(products, block_sinks, num_segments=BLOCKS_DEV)
            return summed.reshape(ROWS_DEV, HIDDEN_SIZE)
        return lax.map(jax.checkpoint(one_device), (edge_weights, sources, sinks)).reshape(NODES, HIDDEN_SIZE)

    def forward(params):
        embed_full, pair_full, merge_full, head_full = params
        hidden = low_back(dense(inputs, low(embed_full)))
        for layer in range(LAYERS):
            hidden_half = low(hidden)
            gathered = low(low_back(aggregate(hidden_half)))
            self_part = dense(hidden_half, low(pair_full[layer, 0]))
            neigh_part = dense(gathered, low(pair_full[layer, 1]))
            joined = low(low_back(jnp.concatenate([self_part, neigh_part], axis=1)))
            linear = low_back(dense(joined, low(merge_full[layer])))
            active = linear * jax.nn.sigmoid(linear)
            hidden = active * lax.rsqrt(lax.optimization_barrier(jnp.sum(active * active, axis=1, keepdims=True)) + norm_eps)
        logits = low_back(dense(low(hidden), low(head_full)))
        per_entry = jnp.maximum(logits, 0.0) - logits * truth + jnp.log1p(jnp.exp(-jnp.abs(logits)))
        return jnp.sum(per_entry * row_mask) / denom
    params = (embed_weight, pair_weight, merge_weight, head_weight)
    loss, pull = jax.vjp(forward, params)
    grads = pull(jnp.ones_like(loss))[0]
    firsts = (embed_moment, pair_moment, merge_moment, head_moment)
    seconds = (embed_variance, pair_variance, merge_variance, head_variance)
    results = [adam_update(params[index], grads[index], firsts[index], seconds[index]) for index in range(4)]
    return (loss.reshape(1), results[0][0], results[1][0], results[2][0], results[3][0], results[0][1], results[1][1], results[2][1], results[3][1], results[0][2], results[1][2], results[2][2], results[3][2])
```

```python
import functools

import jax
import jax.numpy as jnp
from jax import lax
from jax.experimental import pallas as pl
from jax.experimental.pallas import tpu as pltpu
from jax.sharding import PartitionSpec as P

norm_eps = 1e-06
learn_rate = 0.03
beta_one = 0.9
beta_two = 0.999
adam_eps = 1e-08
decay_rate = 0.01
adam_step = 10.0

PLANES = 4
KINDS = 4
CHUNKS = 8
MESH = pl.DeviceIdType.MESH


def to_half(value):
    return value.astype(jnp.bfloat16)


def mat_product(former, latter):
    return jnp.dot(former, latter, preferred_element_type=jnp.float32)


def left_product(former, latter):
    return lax.dot_general(
        former, latter, (((0,), (0,)), ((), ())), preferred_element_type=jnp.float32
    )


def right_product(former, latter):
    return lax.dot_general(
        former, latter, (((1,), (1,)), ((), ())), preferred_element_type=jnp.float32
    )


def adam_update(weight, grad, first, second):
    first_new = beta_one * first + (1.0 - beta_one) * grad
    second_new = beta_two * second + (1.0 - beta_two) * grad * grad
    first_hat = first_new / (1.0 - beta_one**adam_step)
    second_hat = second_new / (1.0 - beta_two**adam_step)
    weight_new = weight - learn_rate * (
        first_hat / (jnp.sqrt(second_hat) + adam_eps) + decay_rate * weight
    )
    return (weight_new, first_new, second_new)


def place(me, plane_size):
    z = me // plane_size
    spot = me % plane_size
    inner = (z % 2 + z // 2) % 2
    near = z + 1 - 2 * (z % 2)
    far_in = 2 - z // 2
    far_out = 3 * (1 - z // 2)
    return z, spot, inner, near, far_in, far_out


def exchange_kernel(n, slots, far_cap, near_cap, ring, *refs):
    far_list, near_list, pass_list, serve = refs[:4]
    table = refs[4]
    out = refs[5]
    rest = list(refs[6:])
    far_stage = [rest.pop(0) for _ in range(CHUNKS)]
    near_stage = [rest.pop(0) for _ in range(CHUNKS)]
    near_got = [rest.pop(0) for _ in range(CHUNKS)]
    far_got = [[rest.pop(0) for _ in range(CHUNKS)] for _ in range(2)]
    pass_stage = [[rest.pop(0) for _ in range(CHUNKS)] for _ in range(2)]
    serve_stage = [rest.pop(0) for _ in range(ring)]
    far_sent, near_sent, near_recv, far_recv, pass_sent, serve_sent, serve_recv = rest

    size = n // PLANES
    rows = table.shape[1] // CHUNKS
    me = lax.axis_index("nodes")
    z, spot, inner, near, far_in, far_out = place(me, size)
    near_dev = near * size + spot
    relay_dev = far_in * size + spot
    outer_dev = far_out * size + spot
    is_inner = inner == 1

    barrier = pltpu.get_barrier_semaphore()

    def greet(step, carry):
        pl.semaphore_signal(
            barrier,
            inc=1,
            device_id=(z * size + lax.rem(spot + step, size),),
            device_id_type=MESH,
        )
        return carry

    lax.fori_loop(1, size, greet, 0)
    pl.semaphore_signal(barrier, inc=1, device_id=(near_dev,), device_id_type=MESH)

    @pl.when(is_inner)
    def _():
        pl.semaphore_signal(barrier, inc=1, device_id=(relay_dev,), device_id_type=MESH)
        pl.semaphore_signal(barrier, inc=1, device_id=(outer_dev,), device_id_type=MESH)

    pl.semaphore_wait(barrier, size + 1)

    def far_copy(step, lane):
        return pltpu.make_async_remote_copy(
            src_ref=far_stage[step],
            dst_ref=far_got[lane][step],
            send_sem=far_sent.at[step],
            recv_sem=far_recv.at[lane, step],
            device_id=(relay_dev,),
            device_id_type=MESH,
        )

    def near_copy(step):
        return pltpu.make_async_remote_copy(
            src_ref=near_stage[step],
            dst_ref=near_got[step],
            send_sem=near_sent.at[step],
            recv_sem=near_recv.at[step],
            device_id=(near_dev,),
            device_id_type=MESH,
        )

    def pass_copy(step, lane):
        return pltpu.make_async_remote_copy(
            src_ref=pass_stage[lane][step],
            dst_ref=far_got[lane][step].at[pl.ds(0, near_cap)],
            send_sem=pass_sent.at[lane, step],
            recv_sem=far_recv.at[lane, step],
            device_id=(near_dev,),
            device_id_type=MESH,
        )

    for step in range(CHUNKS):
        window = pl.ds(step * rows, rows)

        def fill_far(at, carry):
            far_stage[step][at] = table[far_list[at], window, :]
            return carry

        lax.fori_loop(0, far_cap, fill_far, 0)

        @pl.when(is_inner)
        def _():
            far_copy(step, 0).start()

        @pl.when(inner == 0)
        def _():
            far_copy(step, 1).start()

        def fill_near(at, carry):
            near_stage[step][at] = table[near_list[at], window, :]
            return carry

        lax.fori_loop(0, near_cap, fill_near, 0)
        near_copy(step).start()

    def serve_copy(step, peer):
        return pltpu.make_async_remote_copy(
            src_ref=serve_stage[step % ring].at[peer],
            dst_ref=out.at[step, spot],
            send_sem=serve_sent.at[step % ring],
            recv_sem=serve_recv.at[step],
            device_id=(z * size + peer,),
            device_id_type=MESH,
        )

    def serve_drain(step):
        held = serve_stage[step % ring].at[pl.ds(0, size - 1)]
        pltpu.make_async_copy(held, held, serve_sent.at[step % ring]).wait()

    for step in range(CHUNKS):
        window = pl.ds(step * rows, rows)

        @pl.when(is_inner)
        def _():
            for lane in range(2):
                pltpu.make_async_copy(
                    far_got[lane][step], far_got[lane][step], far_recv.at[lane, step]
                ).wait()

                def fill_pass(at, carry):
                    pass_stage[lane][step][at] = far_got[lane][step][pass_list[lane, at]]
                    return carry

                lax.fori_loop(0, near_cap, fill_pass, 0)
                pass_copy(step, lane).start()

        @pl.when(inner == 0)
        def _():
            for lane in range(2):
                part = far_got[lane][step].at[pl.ds(0, near_cap)]
                pltpu.make_async_copy(part, part, far_recv.at[lane, step]).wait()

        pltpu.make_async_copy(near_got[step], near_got[step], near_recv.at[step]).wait()
        if step >= ring:
            serve_drain(step - ring)

        def fill_serve(peer, carry):
            stage = serve_stage[step % ring]
            for slot in range(slots):
                stage[peer, 0, slot] = table[serve[peer, 0, slot], window, :]
                stage[peer, 1, slot] = near_got[step][serve[peer, 1, slot]]
                stage[peer, 2, slot] = far_got[0][step][serve[peer, 2, slot]]
                stage[peer, 3, slot] = far_got[1][step][serve[peer, 3, slot]]
            return carry

        lax.fori_loop(0, size, fill_serve, 0)
        pltpu.make_async_copy(
            serve_stage[step % ring].at[spot], out.at[step, spot], serve_recv.at[step]
        ).start()

        def send(hop, carry):
            serve_copy(step, lax.rem(spot + hop, size)).start()
            return carry

        lax.fori_loop(1, size, send, 0)

    for step in range(CHUNKS):
        pltpu.make_async_copy(out.at[step], out.at[step], serve_recv.at[step]).wait()
    for step in range(max(0, CHUNKS - ring), CHUNKS):
        serve_drain(step)
    for step in range(CHUNKS):
        pltpu.make_async_copy(far_stage[step], far_stage[step], far_sent.at[step]).wait()
        pltpu.make_async_copy(near_stage[step], near_stage[step], near_sent.at[step]).wait()

    @pl.when(is_inner)
    def _():
        for step in range(CHUNKS):
            for lane in range(2):
                held = pass_stage[lane][step]
                pltpu.make_async_copy(held, held, pass_sent.at[lane, step]).wait()


def exchange(n, slots, far_cap, near_cap, collective, lists, table):
    size = n // PLANES
    blocks, depth, width = table.shape
    rows = depth // CHUNKS
    kind = table.dtype
    ring = CHUNKS if size <= 8 else 2

    def rows_of(*lead):
        return pltpu.VMEM(lead + (rows, width), kind)

    scratch = (
        [rows_of(far_cap) for _ in range(CHUNKS)]
        + [rows_of(near_cap) for _ in range(2 * CHUNKS)]
        + [rows_of(far_cap) for _ in range(2 * CHUNKS)]
        + [rows_of(near_cap) for _ in range(2 * CHUNKS)]
        + [rows_of(size, KINDS, slots) for _ in range(ring)]
        + [
            pltpu.SemaphoreType.DMA((CHUNKS,)),
            pltpu.SemaphoreType.DMA((CHUNKS,)),
            pltpu.SemaphoreType.DMA((CHUNKS,)),
            pltpu.SemaphoreType.DMA((2, CHUNKS)),
            pltpu.SemaphoreType.DMA((2, CHUNKS)),
            pltpu.SemaphoreType.DMA((ring,)),
            pltpu.SemaphoreType.DMA((CHUNKS,)),
        ]
    )
    far_list, near_list, pass_list, serve = lists
    smem = pl.BlockSpec(memory_space=pltpu.SMEM)
    return pl.pallas_call(
        functools.partial(exchange_kernel, n, slots, far_cap, near_cap, ring),
        out_shape=jax.ShapeDtypeStruct((CHUNKS, size, KINDS, slots, rows, width), kind),
        in_specs=[smem, smem, smem, smem, pl.BlockSpec(memory_space=pltpu.VMEM)],
        out_specs=pl.BlockSpec(memory_space=pl.ANY),
        scratch_shapes=scratch,
        compiler_params=pltpu.CompilerParams(
            collective_id=collective, has_side_effects=True, vmem_limit_bytes=60 * 2**20
        ),
        name="exchange",
    )(far_list[:far_cap], near_list[:near_cap], pass_list[:, :near_cap], serve, table)


def gather_sum_kernel(flip, slots, order, sinks, weights, got, out, total):
    at = pl.program_id(0)

    @pl.when(at == 0)
    def _():
        total[...] = jnp.zeros_like(total)

    blocks, depth, width = total.shape
    for kind in range(KINDS):
        for slot in range(slots):
            sink = sinks[at, kind, slot]

            @pl.when(sink < blocks)
            def _():
                edge = weights[order[kind], 0, slot]
                rows = got[:, 0, kind, slot].reshape(depth, width)
                dims = (((0,), (0,)), ((), ())) if flip else (((1,), (0,)), ((), ()))
                total[sink] += lax.dot_general(
                    edge, rows, dims, preferred_element_type=jnp.float32
                )

    @pl.when(at == pl.num_programs(0) - 1)
    def _():
        out[...] = total[...].astype(out.dtype)


def gather_sum(flip, kind, order, sinks, weights, got, blocks):
    size, _, slots = sinks.shape
    chunks, _, _, _, rows, width = got.shape
    depth = chunks * rows
    edges = weights.reshape(PLANES, size, slots, depth, depth)
    return pl.pallas_call(
        functools.partial(gather_sum_kernel, flip, slots),
        out_shape=jax.ShapeDtypeStruct((blocks, depth, width), kind),
        grid_spec=pltpu.PrefetchScalarGridSpec(
            num_scalar_prefetch=2,
            grid=(size,),
            in_specs=[
                pl.BlockSpec(
                    (PLANES, 1, slots, depth, depth), lambda at, order, sinks: (0, at, 0, 0, 0)
                ),
                pl.BlockSpec(
                    (chunks, 1, KINDS, slots, rows, width),
                    lambda at, order, sinks: (0, at, 0, 0, 0, 0),
                ),
            ],
            out_specs=pl.BlockSpec((blocks, depth, width), lambda at, order, sinks: (0, 0, 0)),
            scratch_shapes=[pltpu.VMEM((blocks, depth, width), jnp.float32)],
        ),
        compiler_params=pltpu.CompilerParams(vmem_limit_bytes=40 * 2**20),
        name="gather_sum",
    )(order, sinks, edges, got)


def pick(values, hot, axis):
    shape = [1] * values.ndim
    shape[axis] = values.shape[axis]
    return jnp.sum(jnp.where(hot.reshape(shape), values, 0), axis=axis)


def by_kind(values, order, axis):
    planes = jnp.arange(PLANES, dtype=jnp.int32)
    return jnp.stack([pick(values, planes == order[kind], axis) for kind in range(KINDS)], axis)


def index_tables(n, blocks, taken, me):
    size = n // PLANES
    ways, slots = taken.shape[0], taken.shape[3]
    z, spot, inner, near, far_in, far_out = place(me, size)
    planes = jnp.arange(PLANES, dtype=jnp.int32)
    block_ids = jnp.arange(blocks, dtype=jnp.int32)
    split = taken.reshape(ways, PLANES, size, PLANES, size, slots)
    every = jnp.any(
        split[..., None] == block_ids, axis=(2, 5)
    )
    every_far = every.reshape(ways, 2, 2, PLANES, size, blocks).any(axis=2)
    own_plane = (planes[:, None] == planes[None, :])[None, :, :, None]
    own_half = (jnp.arange(2)[:, None] == planes[None, :] // 2)[None, :, :, None]
    near_need = jnp.max(
        jnp.where(own_plane, 0, jnp.sum(every.astype(jnp.int32), axis=-1)), axis=(1, 2, 3)
    )
    far_need = jnp.max(
        jnp.where(own_half, 0, jnp.sum(every_far.astype(jnp.int32), axis=-1)), axis=(1, 2, 3)
    )

    order = jnp.stack([z, near, far_in, far_out])
    mine = lax.dynamic_index_in_dim(split, spot, 4, keepdims=False)
    mine = by_kind(mine, order, 3)
    hit = jnp.any(
        mine[..., None] == block_ids, axis=(2, 4)
    )
    hit_half = hit.reshape(ways, 2, 2, KINDS, blocks).any(axis=2)
    below = (block_ids[:, None] > block_ids[None, :]).astype(jnp.int32)

    def ranks(present):
        return jnp.sum(present[..., None, :].astype(jnp.int32) * below, axis=-1)

    rank = ranks(hit)
    rank_half = ranks(hit_half)
    half = z // 2
    outer_plane = 3 * half
    here = planes == z
    pos_here = pick(rank, here, 1)
    hit_outer = jnp.any(hit & (planes == outer_plane).reshape(1, PLANES, 1, 1), axis=1)
    pos_outer = pick(rank, planes == outer_plane, 1)
    hit_near = jnp.any(hit & (planes == near).reshape(1, PLANES, 1, 1), axis=1)
    pos_near = pick(rank, planes == near, 1)
    halves = jnp.arange(2)
    pos_half = pick(rank_half, halves == half, 1)
    hit_far = jnp.any(hit_half & (halves == 1 - half).reshape(1, 2, 1, 1), axis=1)
    pos_far = pick(rank_half, halves == 1 - half, 1)

    def compact(present, pos, value):
        spots = block_ids[:, None]
        return jnp.sum(
            jnp.where(present[..., None, :] & (pos[..., None, :] == spots), value[..., None, :], 0),
            axis=-1,
        )

    ids = jnp.broadcast_to(block_ids, (ways, blocks))
    far_list = compact(hit_far[:, 0], pos_far[:, 0], ids)
    near_list = compact(hit_near[:, 0], pos_near[:, 0], ids)
    pass_list = compact(hit_outer[:, 2:], pos_outer[:, 2:], pos_half[:, 2:])
    kinds = jnp.arange(KINDS)[None, :, None]
    spot_map = jnp.where(
        kinds == 0, block_ids, jnp.where((kinds >= 2) & (inner == 1), pos_half, pos_here)
    )
    wanted = pick(mine, here, 1)
    serve = jnp.sum(
        jnp.where(wanted[..., None] == block_ids, spot_map[:, None, :, None, :], 0), axis=-1
    )
    return order, far_list, near_list, pass_list, serve, near_need, far_need


def my_slots(n, table, order):
    size = n // PLANES
    return by_kind(table.reshape(PLANES, size, -1), order, 0).transpose(1, 0, 2)


def shards(
    features,
    labels,
    labelled,
    label_count,
    need_blocks,
    need_count,
    target_block,
    adjacency,
    embed_weight,
    pair_weight,
    merge_weight,
    head_weight,
    embed_moment,
    pair_moment,
    merge_moment,
    head_moment,
    embed_variance,
    pair_variance,
    merge_variance,
    head_variance,
):
    row_count = features.shape[0]
    hidden_width = embed_weight.shape[1]
    block_rows = adjacency.shape[1]
    slots = need_blocks.shape[2]
    n = lax.axis_size("nodes")
    size = n // PLANES
    block_count = row_count // block_rows
    me = lax.axis_index("nodes")

    alive = lax.broadcasted_iota(jnp.int32, need_blocks.shape[1:], 1) < need_count[0][:, None]
    wanted = jnp.where(alive, need_blocks[0], block_count)
    sunk = jnp.where(alive, target_block[0], block_count)
    tables = lax.all_gather(jnp.stack([wanted, sunk]), "nodes", axis=0, tiled=False)
    taken = jnp.stack([tables[:, 0], tables[:, 1].transpose(1, 0, 2)])
    order, far_list, near_list, pass_list, serve, near_need, far_need = index_tables(
        n, block_count, taken, me
    )
    near_full = min(block_count, size * slots)
    rungs = [(min(23, block_count), min(15, near_full)), (block_count, near_full)]
    if near_full > 16:
        rungs = rungs[1:]

    def swap(way, table):
        lists = (far_list[way], near_list[way], pass_list[way], serve[way])

        def at(rung):
            far_cap, near_cap = rungs[rung]
            return lambda *held: exchange(
                n, slots, far_cap, near_cap, 1 + way * len(rungs) + rung, held[:4], held[4]
            )

        if len(rungs) == 1:
            return at(0)(*lists, table)
        fits = (far_need[way] <= rungs[0][0]) & (near_need[way] <= rungs[0][1])
        return lax.cond(fits, at(0), at(1), *lists, table)

    pair_half = to_half(pair_weight)
    merge_half = to_half(merge_weight)
    head_half = to_half(head_weight)
    hidden_half = to_half(mat_product(features, to_half(embed_weight)))
    got = swap(0, hidden_half.reshape(block_count, block_rows, hidden_width))
    gathered = gather_sum(
        False, jnp.bfloat16, order, my_slots(n, sunk, order), adjacency, got, block_count
    ).reshape(row_count, hidden_width)
    adjacency_later, gathered = lax.optimization_barrier((adjacency, gathered))
    edges_back = lax.all_to_all(adjacency_later, "nodes", split_axis=0, concat_axis=0, tiled=True)

    self_part = mat_product(hidden_half, pair_half[0, 0])
    neigh_part = mat_product(gathered, pair_half[0, 1])
    joined = to_half(jnp.concatenate([self_part, neigh_part], axis=1))
    linear = mat_product(joined, merge_half[0])
    active = linear * jax.nn.sigmoid(linear)
    scale = lax.rsqrt(jnp.sum(active * active, axis=1, keepdims=True) + norm_eps)
    output = active * scale
    final_half = to_half(output)
    logits = mat_product(final_half, head_half)
    truth = labels.astype(jnp.float32)
    row_mask = labelled.astype(jnp.float32)[:, None]
    denom = label_count[0].astype(jnp.float32) * logits.shape[1]
    per_entry = jnp.maximum(logits, 0.0) - logits * truth + jnp.log1p(jnp.exp(-jnp.abs(logits)))
    loss_part = jnp.sum(per_entry * row_mask) / denom
    grad_logits = to_half((jax.nn.sigmoid(logits) - truth) * row_mask / denom)
    head_grad = left_product(final_half, grad_logits)
    grad_out = right_product(grad_logits, head_half)
    grad_active = scale * (grad_out - output * jnp.sum(grad_out * output, axis=1, keepdims=True))
    sig_value = jax.nn.sigmoid(linear)
    grad_linear = to_half(grad_active * sig_value * (1.0 + linear * (1.0 - sig_value)))
    merge_grad = left_product(joined, grad_linear)
    grad_joined = to_half(right_product(grad_linear, merge_half[0]))
    grad_self_out = grad_joined[:, :hidden_width]
    grad_neigh_out = grad_joined[:, hidden_width:]
    grad_self = left_product(hidden_half, grad_self_out)
    grad_neigh = left_product(gathered, grad_neigh_out)
    grad_gathered = to_half(right_product(grad_neigh_out, pair_half[0, 1]))
    pair_grad = jnp.stack([grad_self, grad_neigh])[None]
    merge_grad = merge_grad[None]
    spread = jnp.zeros((head_grad.shape[0], 128 - head_grad.shape[1]), jnp.float32)
    spread = spread.at[0, 0].set(loss_part)
    head_wide = jnp.concatenate([head_grad, spread], axis=1)
    pair_grad, merge_grad, head_wide = lax.psum((pair_grad, merge_grad, head_wide), "nodes")
    labels_width = head_grad.shape[1]
    head_grad = head_wide[:, :labels_width]
    loss_total = head_wide[0, labels_width]

    back = swap(1, grad_gathered.reshape(block_count, block_rows, hidden_width))
    summed = gather_sum(
        True,
        jnp.float32,
        order,
        my_slots(n, taken[0][:, me], order),
        edges_back,
        back,
        block_count,
    ).reshape(row_count, hidden_width)
    grad_hidden = right_product(grad_self_out, pair_half[0, 0]) + summed
    embed_grad = lax.psum(left_product(features, to_half(grad_hidden)), "nodes")
    pair_next = adam_update(pair_weight, pair_grad, pair_moment, pair_variance)
    merge_next = adam_update(merge_weight, merge_grad, merge_moment, merge_variance)
    head_next = adam_update(head_weight, head_grad, head_moment, head_variance)
    embed_next = adam_update(embed_weight, embed_grad, embed_moment, embed_variance)
    return (
        loss_total.reshape(1),
        embed_next[0],
        pair_next[0],
        merge_next[0],
        head_next[0],
        embed_next[1],
        pair_next[1],
        merge_next[1],
        head_next[1],
        embed_next[2],
        pair_next[2],
        merge_next[2],
        head_next[2],
    )


def solution(mesh):
    split = ("nodes",)
    return jax.shard_map(
        shards,
        mesh=mesh,
        in_specs=(
            P("nodes", None),
            P("nodes", None),
            P("nodes"),
            P(),
            P("nodes", None, None),
            P("nodes", None),
            P("nodes", None, None),
            P("nodes", None, None),
        )
        + (P(),) * 12,
        out_specs=(P(),) * 13,
        check_vma=False,
    )
```

```python
import functools

import jax
import jax.numpy as jnp
from jax import lax
from jax.experimental import pallas as pl
from jax.experimental.pallas import tpu as pltpu
from jax.sharding import PartitionSpec as P

norm_eps = 1e-06
learn_rate = 0.03
beta_one = 0.9
beta_two = 0.999
adam_eps = 1e-08
decay_rate = 0.01
adam_step = 10.0

PLANES = 4
KINDS = 4
CHUNKS = 8
PARTS = 2
AHEAD = 3
LEAD = 1
UNROLL = False
LANES = 128
MESH = pl.DeviceIdType.MESH


def to_half(value):
    return value.astype(jnp.bfloat16)


def mat_product(former, latter):
    return jnp.dot(former, latter, preferred_element_type=jnp.float32)


def left_product(former, latter):
    return lax.dot_general(
        former, latter, (((0,), (0,)), ((), ())), preferred_element_type=jnp.float32
    )


def right_product(former, latter):
    return lax.dot_general(
        former, latter, (((1,), (1,)), ((), ())), preferred_element_type=jnp.float32
    )


def adam_update(weight, grad, first, second):
    first_new = beta_one * first + (1.0 - beta_one) * grad
    second_new = beta_two * second + (1.0 - beta_two) * grad * grad
    first_hat = first_new / (1.0 - beta_one**adam_step)
    second_hat = second_new / (1.0 - beta_two**adam_step)
    weight_new = weight - learn_rate * (
        first_hat / (jnp.sqrt(second_hat) + adam_eps) + decay_rate * weight
    )
    return (weight_new, first_new, second_new)


def place(me, plane_size):
    z = me // plane_size
    spot = me % plane_size
    inner = (z % 2 + z // 2) % 2
    near = z + 1 - 2 * (z % 2)
    far_in = 2 - z // 2
    far_out = 3 * (1 - z // 2)
    return z, spot, inner, near, far_in, far_out


class Summer:
    STEPS = 7

    def __init__(self, n, shape):
        self.n, (self.rows, self.width) = n, shape
        self.size = n // PLANES
        self.chips = self.size // 2
        self.half = self.width // 2
        self.cuts = min(self.half // LANES, self.chips)
        self.cut = self.half // self.cuts
        self.bands = self.chips // self.cuts
        self.band = self.rows // self.bands
        self.shard = self.band // PLANES

    @staticmethod
    def padded(n, rows, width):
        summer = Summer(n, (rows, width))
        unit = summer.bands * PLANES * 8
        return -(-rows // unit) * unit

    def scratch(self):
        f32 = jnp.float32
        return [
            pltpu.VMEM((self.rows, self.half), f32),
            pltpu.VMEM((self.chips - 1, self.band, self.cut), f32),
            pltpu.VMEM((PLANES - 1, self.shard, self.cut), f32),
            pltpu.SemaphoreType.DMA((6,)),
            pltpu.SemaphoreType.DMA((6,)),
        ]

    def bind(self, part, total, refs):
        self.part, self.total = part, total
        self.from_core, self.from_chip, self.from_plane, self.sent, self.got = refs
        me = lax.axis_index("nodes")
        self.z, spot = me // self.size, me % self.size
        self.chip, self.core = spot // 2, spot % 2
        self.mine = pl.ds(pl.multiple_of(self.core * self.half, LANES), self.half)
        self.other = pl.ds(pl.multiple_of((1 - self.core) * self.half, LANES), self.half)

    def device(self, z, chip, core):
        return z * self.size + chip * 2 + core

    def plane_peers(self):
        found = [self.device(self.z, self.chip, 1 - self.core)]
        for hop in range(1, self.chips):
            found.append(self.device(self.z, lax.rem(self.chip + hop, self.chips), self.core))
        return found

    def column_peers(self):
        return [
            self.device(lax.rem(self.z + hop, PLANES), self.chip, self.core)
            for hop in range(1, PLANES)
        ]

    def patch(self, chip):
        row = pl.multiple_of((chip // self.cuts) * self.band, 8)
        col = self.core * self.half + (chip % self.cuts) * self.cut
        return row, pl.ds(pl.multiple_of(col, LANES), self.cut)

    def copy(self, hop, src, dst, device):
        return pltpu.make_async_remote_copy(
            src_ref=src,
            dst_ref=dst,
            send_sem=self.sent.at[hop],
            recv_sem=self.got.at[hop],
            device_id=(device,),
            device_id_type=MESH,
        )

    @staticmethod
    def settle(sem, held):
        pltpu.make_async_copy(held, held, sem).wait()

    def step(self, at):
        part, total = self.part, self.total
        across = self.device(self.z, self.chip, 1 - self.core)
        row, cols = self.patch(self.chip)
        band = pl.ds(row, self.band)
        rows = pl.ds(pl.multiple_of(row + self.z * self.shard, 8), self.shard)
        if at == 0:
            self.copy(0, part.at[:, self.other], self.from_core, across).start()
        elif at == 1:
            self.settle(self.got.at[0], self.from_core)
            part[:, self.mine] += self.from_core[...]
            for hop in range(1, self.chips):
                chip = lax.rem(self.chip + hop, self.chips)
                there, cut = self.patch(chip)
                src = part.at[pl.ds(there, self.band), cut]
                dst = self.from_chip.at[hop - 1]
                self.copy(1, src, dst, self.device(self.z, chip, self.core)).start()
        elif at == 2:
            self.settle(self.got.at[1], self.from_chip)
            held = part[band, cols]
            for hop in range(1, self.chips):
                held = held + self.from_chip[hop - 1]
            part[band, cols] = held
            for hop in range(1, PLANES):
                z = lax.rem(self.z + hop, PLANES)
                there = pl.multiple_of(row + z * self.shard, 8)
                src = part.at[pl.ds(there, self.shard), cols]
                dst = self.from_plane.at[hop - 1]
                self.copy(2, src, dst, self.device(z, self.chip, self.core)).start()
        elif at == 3:
            self.settle(self.got.at[2], self.from_plane)
            held = part[rows, cols]
            for hop in range(1, PLANES):
                held = held + self.from_plane[hop - 1]
            total[rows, cols] = held
            for hop in range(1, PLANES):
                z = lax.rem(self.z + hop, PLANES)
                held = total.at[rows, cols]
                self.copy(3, held, held, self.device(z, self.chip, self.core)).start()
        elif at == 4:
            self.settle(self.got.at[3], self.from_plane)
            for hop in range(1, self.chips):
                chip = lax.rem(self.chip + hop, self.chips)
                held = total.at[band, cols]
                self.copy(4, held, held, self.device(self.z, chip, self.core)).start()
        elif at == 5:
            self.settle(self.got.at[4], self.from_chip)
            held = total.at[:, self.mine]
            self.copy(5, held, held, across).start()
        else:
            self.settle(self.got.at[5], self.from_core)
            self.settle(self.sent.at[0], self.from_core)
            self.settle(self.sent.at[1], self.from_chip)
            self.settle(self.sent.at[2], self.from_plane)
            self.settle(self.sent.at[3], self.from_plane)
            self.settle(self.sent.at[4], self.from_chip)
            self.settle(self.sent.at[5], self.from_core)


def finish_kernel(n, tile, rows, grads, total, part, *refs):
    summer = Summer(n, part.shape)
    summer.bind(part, total, refs)
    barrier = pltpu.get_barrier_semaphore()
    peers = summer.plane_peers() + summer.column_peers()
    for peer in peers:
        pl.semaphore_signal(barrier, inc=1, device_id=(peer,), device_id_type=MESH)
    count, depth = rows.shape

    def multiply(cols):
        part[:, cols] = jnp.zeros((part.shape[0], summer.half), jnp.float32)

        def add(at, carry):
            window = pl.ds(pl.multiple_of(at * tile, tile), tile)
            part[:count, cols] += mat_product(rows[:, window], grads[window, cols])
            return carry

        lax.fori_loop(0, depth // tile, add, 0)

    multiply(summer.other)
    pl.semaphore_wait(barrier, len(peers))
    summer.step(0)
    multiply(summer.mine)
    for at in range(1, Summer.STEPS):
        summer.step(at)


def finish(n, rows, grads, collective):
    shape = (Summer.padded(n, rows.shape[0], grads.shape[1]), grads.shape[1])
    vmem = pl.BlockSpec(memory_space=pltpu.VMEM)
    return pl.pallas_call(
        functools.partial(finish_kernel, n, 1024),
        out_shape=jax.ShapeDtypeStruct(shape, jnp.float32),
        in_specs=[vmem, vmem],
        out_specs=vmem,
        scratch_shapes=[pltpu.VMEM(shape, jnp.float32)] + Summer(n, shape).scratch(),
        compiler_params=pltpu.CompilerParams(
            collective_id=collective, has_side_effects=True, vmem_limit_bytes=40 * 2**20
        ),
        name="finish",
    )(rows, grads)


class Exchange:
    def __init__(self, n, slots, far_cap, near_cap, shape, kind):
        self.n, self.slots = n, slots
        self.far_cap, self.near_cap = far_cap, near_cap
        self.size = n // PLANES
        self.blocks, self.depth, self.width = shape
        self.kind = kind
        self.rows = self.depth // CHUNKS
        self.cols = self.width // PARTS
        self.steps = CHUNKS * PARTS
        self.ring = self.steps if self.size <= 8 else 2

    def out_shape(self):
        return jax.ShapeDtypeStruct(
            (CHUNKS, self.size, KINDS, self.slots, self.rows, self.width), self.kind
        )

    def scratch(self):
        def piece(*lead):
            return pltpu.VMEM(lead + (self.rows, self.cols), self.kind)

        steps, ring = self.steps, self.ring
        dma = pltpu.SemaphoreType.DMA
        return (
            [piece(self.far_cap) for _ in range(steps)]
            + [piece(self.near_cap) for _ in range(2 * steps)]
            + [piece(self.far_cap) for _ in range(2 * steps)]
            + [piece(self.near_cap) for _ in range(2 * steps)]
            + [piece(self.size, 2, self.slots) for _ in range(2 * ring)]
            + [dma((steps,)), dma((steps,)), dma((steps,)), dma((2, steps)), dma((2, steps))]
            + [dma((2, ring)), dma((CHUNKS,))]
        )

    def bind(self, plan, table, out, refs):
        self.plan, self.table, self.out = plan, table, out
        rest = list(refs)
        steps = self.steps

        def take(count):
            found = rest[:count]
            del rest[:count]
            return found

        self.far_stage = take(steps)
        self.near_stage = take(steps)
        self.near_got = take(steps)
        self.far_got = [take(steps), take(steps)]
        self.pass_stage = [take(steps), take(steps)]
        self.serve_stage = [take(self.ring), take(self.ring)]
        (
            self.far_sent,
            self.near_sent,
            self.near_recv,
            self.far_recv,
            self.pass_sent,
            self.serve_sent,
            self.serve_recv,
        ) = rest
        me = lax.axis_index("nodes")
        self.z, self.spot, self.inner, near, far_in, far_out = place(me, self.size)
        self.near_dev = near * self.size + self.spot
        self.relay_dev = far_in * self.size + self.spot
        self.outer_dev = far_out * self.size + self.spot

    def greet(self, column=False):
        barrier = pltpu.get_barrier_semaphore()

        def hello(device):
            pl.semaphore_signal(barrier, inc=1, device_id=(device,), device_id_type=MESH)

        def in_plane(step, carry):
            hello(self.z * self.size + lax.rem(self.spot + step, self.size))
            return carry

        lax.fori_loop(1, self.size, in_plane, 0)
        if column:
            for hop in range(1, PLANES):
                hello(lax.rem(self.z + hop, PLANES) * self.size + self.spot)
            pl.semaphore_wait(barrier, self.size - 1 + PLANES - 1)
            return
        hello(self.near_dev)

        @pl.when(self.inner == 1)
        def _():
            hello(self.relay_dev)
            hello(self.outer_dev)

        pl.semaphore_wait(barrier, self.size + 1)

    def window(self, step):
        return pl.ds((step // PARTS) * self.rows, self.rows), pl.ds(
            (step % PARTS) * self.cols, self.cols
        )

    def remote(self, src, dst, sent, got, device):
        return pltpu.make_async_remote_copy(
            src_ref=src,
            dst_ref=dst,
            send_sem=sent,
            recv_sem=got,
            device_id=(device,),
            device_id_type=MESH,
        )

    @staticmethod
    def settle(sem, held):
        pltpu.make_async_copy(held, held, sem).wait()

    def launch(self, step):
        rows, cols = self.window(step)
        plan, table = self.plan, self.table
        far_stage, near_stage = self.far_stage[step], self.near_stage[step]

        def fill_far(at, carry):
            far_stage[at] = table[plan[ROW_FAR, at], rows, cols]
            return carry

        def fill_near(at, carry):
            near_stage[at] = table[plan[ROW_NEAR, at], rows, cols]
            return carry

        lax.fori_loop(0, self.far_cap, fill_far, 0, unroll=UNROLL)
        for lane in range(2):

            @pl.when(self.inner == 1 - lane)
            def _():
                self.remote(
                    far_stage,
                    self.far_got[lane][step],
                    self.far_sent.at[step],
                    self.far_recv.at[lane, step],
                    self.relay_dev,
                ).start()

        lax.fori_loop(0, self.near_cap, fill_near, 0, unroll=UNROLL)
        self.remote(
            near_stage,
            self.near_got[step],
            self.near_sent.at[step],
            self.near_recv.at[step],
            self.near_dev,
        ).start()

    def relay(self, step):
        plan = self.plan

        @pl.when(self.inner == 1)
        def _():
            for lane in range(2):
                got, stage = self.far_got[lane][step], self.pass_stage[lane][step]
                self.settle(self.far_recv.at[lane, step], got)

                def fill(at, carry):
                    stage[at] = got[plan[ROW_PASS + lane, at]]
                    return carry

                lax.fori_loop(0, self.near_cap, fill, 0, unroll=UNROLL)
                self.remote(
                    stage,
                    got.at[pl.ds(0, self.near_cap)],
                    self.pass_sent.at[lane, step],
                    self.far_recv.at[lane, step],
                    self.near_dev,
                ).start()

        @pl.when(self.inner == 0)
        def _():
            for lane in range(2):
                got = self.far_got[lane][step].at[pl.ds(0, self.near_cap)]
                self.settle(self.far_recv.at[lane, step], got)

    def serve(self, step, pair):
        rows, cols = self.window(step)
        plan, table, slots, size = self.plan, self.table, self.slots, self.size
        chunk, slot_at = step // PARTS, step % self.ring
        if pair == 0:
            self.settle(self.near_recv.at[step], self.near_got[step])
        if step >= self.ring:
            self.drain(step - self.ring, pair)
        stage = self.serve_stage[pair][slot_at]

        def fill(peer, carry):
            taker = self.z * size + peer
            for slot in range(slots):
                first = plan[ROW_SERVE + 2 * pair * slots + slot, taker]
                second = plan[ROW_SERVE + (2 * pair + 1) * slots + slot, taker]
                if pair == 0:
                    stage[peer, 0, slot] = table[first, rows, cols]
                    stage[peer, 1, slot] = self.near_got[step][second]
                else:
                    stage[peer, 0, slot] = self.far_got[0][step][first]
                    stage[peer, 1, slot] = self.far_got[1][step][second]
            return carry

        lax.fori_loop(0, size, fill, 0)
        there = self.out.at[chunk, self.spot, pl.ds(2 * pair, 2), :, :, cols]
        pltpu.make_async_copy(stage.at[self.spot], there, self.serve_recv.at[chunk]).start()

        def send(hop, carry):
            peer = lax.rem(self.spot + hop, size)
            self.remote(
                stage.at[peer],
                there,
                self.serve_sent.at[pair, slot_at],
                self.serve_recv.at[chunk],
                self.z * size + peer,
            ).start()
            return carry

        lax.fori_loop(1, size, send, 0)

    def drain(self, step, pair):
        slot_at = step % self.ring
        held = self.serve_stage[pair][slot_at].at[pl.ds(0, self.size - 1)]
        self.settle(self.serve_sent.at[pair, slot_at], held)

    def run(self, side=None):
        steps = self.steps
        for step in range(min(AHEAD, steps)):
            self.launch(step)
        for step in range(min(LEAD, steps)):
            self.serve(step, 0)
        for step in range(steps):
            if step + AHEAD < steps:
                self.launch(step + AHEAD)
            self.relay(step)
            self.serve(step, 1)
            if step + LEAD < steps:
                self.serve(step + LEAD, 0)
            if side is not None:
                side(step)
        for chunk in range(CHUNKS):
            self.settle(self.serve_recv.at[chunk], self.out.at[chunk])
        for step in range(max(0, steps - self.ring), steps):
            self.drain(step, 0)
            self.drain(step, 1)
        for step in range(steps):
            self.settle(self.far_sent.at[step], self.far_stage[step])
            self.settle(self.near_sent.at[step], self.near_stage[step])

        @pl.when(self.inner == 1)
        def _():
            for step in range(steps):
                for lane in range(2):
                    self.settle(self.pass_sent.at[lane, step], self.pass_stage[lane][step])


def exchange_kernel(moves, plan, table, out, *refs):
    moves.bind(plan, table, out, refs)
    moves.greet()
    moves.run()


def exchange_sum_kernel(moves, summer, plan, table, part, out, total, held, sem, *refs):
    moves.bind(plan, table, out, refs[5:])
    summer.bind(held, total, refs[:5])
    fetch = pltpu.make_async_copy(part, held, sem)
    fetch.start()
    moves.greet(column=True)

    def side(step):
        if step == 0:
            fetch.wait()
        at = step // PARTS
        if step % PARTS == 0 and at < Summer.STEPS:
            summer.step(at)

    moves.run(side)


def exchange(n, slots, far_cap, near_cap, collective, plan, table, part=None):
    moves = Exchange(n, slots, far_cap, near_cap, table.shape, table.dtype)
    hbm = pl.BlockSpec(memory_space=pl.ANY)
    vmem = pl.BlockSpec(memory_space=pltpu.VMEM)
    in_specs = [pl.BlockSpec(memory_space=pltpu.SMEM), vmem]
    params = pltpu.CompilerParams(
        collective_id=collective, has_side_effects=True, vmem_limit_bytes=60 * 2**20
    )
    if part is None:
        return pl.pallas_call(
            functools.partial(exchange_kernel, moves),
            out_shape=moves.out_shape(),
            in_specs=in_specs,
            out_specs=hbm,
            scratch_shapes=moves.scratch(),
            compiler_params=params,
            name="exchange",
        )(plan, table)
    summer = Summer(n, part.shape)
    return pl.pallas_call(
        functools.partial(exchange_sum_kernel, moves, summer),
        out_shape=(moves.out_shape(), jax.ShapeDtypeStruct(part.shape, jnp.float32)),
        in_specs=in_specs + [hbm],
        out_specs=(hbm, vmem),
        scratch_shapes=[pltpu.VMEM(part.shape, jnp.float32), pltpu.SemaphoreType.DMA]
        + summer.scratch()
        + moves.scratch(),
        compiler_params=params,
        name="exchange_sum",
    )(plan, table, part)


def gather_sum_kernel(flip, slots, first_row, sinks, weights, got, *refs):
    out, total = refs[-2:]
    at = pl.program_id(0)
    size = pl.num_programs(0)
    z, _, _, near, far_in, far_out = place(lax.axis_index("nodes"), size)

    @pl.when(at == 0)
    def _():
        total[...] = jnp.zeros_like(total)

    blocks, depth, width = total.shape
    if flip:
        own, mixer = refs[:2]
        span = own.shape[0] // depth
        base = right_product(own[...], mixer[...]).reshape(span, depth, width)
        total[pl.ds(at * span, span)] += base
    for kind, owner_z in enumerate((z, near, far_in, far_out)):
        for slot in range(slots):
            sink = sinks[first_row + slot, owner_z * size + at]

            @pl.when(sink < blocks)
            def _():
                edge = weights[owner_z, 0, slot]
                rows = got[:, 0, kind, slot].reshape(depth, width)
                dims = (((0,), (0,)), ((), ())) if flip else (((1,), (0,)), ((), ()))
                total[sink] += lax.dot_general(
                    edge, rows, dims, preferred_element_type=jnp.float32
                )

    @pl.when(at == pl.num_programs(0) - 1)
    def _():
        out[...] = total[...].astype(out.dtype)


def gather_sum(flip, first_row, sinks, weights, got, blocks, *base):
    chunks, size, _, slots, rows, width = got.shape
    depth = chunks * rows
    edges = weights.reshape(PLANES, size, slots, depth, depth)
    tile = blocks * depth // size
    base_specs = [
        pl.BlockSpec((tile, width), lambda at, sinks: (at, 0)),
        pl.BlockSpec((width, width), lambda at, sinks: (0, 0)),
    ]
    return pl.pallas_call(
        functools.partial(gather_sum_kernel, flip, slots, first_row),
        out_shape=jax.ShapeDtypeStruct((blocks, depth, width), jnp.bfloat16),
        grid_spec=pltpu.PrefetchScalarGridSpec(
            num_scalar_prefetch=1,
            grid=(size,),
            in_specs=[
                pl.BlockSpec(
                    (PLANES, 1, slots, depth, depth), lambda at, sinks: (0, at, 0, 0, 0)
                ),
                pl.BlockSpec(
                    (chunks, 1, KINDS, slots, rows, width),
                    lambda at, sinks: (0, at, 0, 0, 0, 0),
                ),
            ]
            + base_specs[: len(base)],
            out_specs=pl.BlockSpec((blocks, depth, width), lambda at, sinks: (0, 0, 0)),
            scratch_shapes=[pltpu.VMEM((blocks, depth, width), jnp.float32)],
        ),
        compiler_params=pltpu.CompilerParams(vmem_limit_bytes=40 * 2**20),
        name="gather_sum",
    )(sinks, edges, got, *base)


ROW_FAR, ROW_NEAR, ROW_PASS, ROW_SERVE = 0, 1, 2, 4


def plan_rows(slots):
    wishes = ROW_SERVE + KINDS * slots
    return wishes, wishes + slots, -(-(wishes + slots + 1) // 8) * 8


def column(values, lane):
    lanes = lax.broadcasted_iota(jnp.int32, values.shape, 1)
    return jnp.sum(jnp.where(lanes == lane, values, 0.0), axis=1, keepdims=True)


def lay_plan(n, slots, blocks, rungs, way, wishes_of, plan, present):
    size = n // PLANES
    me = lax.axis_index("nodes")
    z, spot, inner, near, far_in, far_out = place(me, size)
    half = z // 2
    row_wish, row_rung, _ = plan_rows(slots)

    taker = lax.broadcasted_iota(jnp.int32, (LANES, LANES), 0)
    group = lax.broadcasted_iota(jnp.int32, (LANES, LANES), 1)
    plane_of = taker // size
    member = (taker < n) & ((plane_of == group) | (plane_of // 2 + PLANES == group))
    member = jnp.where(member, 1.0, 0.0).astype(jnp.bfloat16)
    hits = jnp.zeros((n * blocks, LANES), jnp.float32)
    for slot in range(slots):
        wish = wishes_of[slot][...]
        ids = lax.broadcasted_iota(jnp.int32, (n, blocks, LANES), 1)
        hot = jnp.where(wish[:, None, :] == ids, 1.0, 0.0).astype(jnp.bfloat16)
        hits = hits + mat_product(hot.reshape(n * blocks, LANES), member)
    here = jnp.where(hits > 0.0, 1.0, 0.0)
    present[...] = here
    counts = jnp.sum(here.reshape(n, blocks, LANES), axis=1)
    owner_plane = lax.broadcasted_iota(jnp.int32, (n, LANES), 0) // size
    lane = lax.broadcasted_iota(jnp.int32, (n, LANES), 1)
    is_near = (lane < PLANES) & (lane != owner_plane)
    is_far = (lane >= PLANES) & (lane < PLANES + 2) & (lane - PLANES != owner_plane // 2)
    near_most = jnp.max(jnp.where(is_near, counts, 0.0), axis=(0, 1), keepdims=True)
    far_most = jnp.max(jnp.where(is_far, counts, 0.0), axis=(0, 1), keepdims=True)
    rung = jnp.zeros((1, 1), jnp.float32)
    for far_cap, near_cap in rungs[:-1]:
        over = (far_most > float(far_cap)) | (near_most > float(near_cap))
        rung = rung + jnp.where(over, 1.0, 0.0)

    def put(row, values):
        plan[way, pl.ds(row, 1), :] = values.astype(jnp.int32)

    put(row_rung, jnp.broadcast_to(rung, (1, LANES)))
    block_id = lax.broadcasted_iota(jnp.int32, (blocks, LANES), 0)
    block_lane = lax.broadcasted_iota(jnp.int32, (blocks, LANES), 1)
    ids = block_id.astype(jnp.float32)
    below = lax.broadcasted_iota(jnp.int32, (blocks, blocks), 0) > lax.broadcasted_iota(
        jnp.int32, (blocks, blocks), 1
    )
    below = jnp.where(below, 1.0, 0.0).astype(jnp.bfloat16)

    def listed(chosen, pos, values):
        at = (chosen > 0.0) & (pos.astype(jnp.int32) == block_lane)
        return jnp.sum(jnp.where(at, values, 0.0), axis=0, keepdims=True)

    for kind, owner_z in enumerate((z, near, far_in, far_out)):
        owner = owner_z * size + spot
        mine = present[pl.ds(pl.multiple_of(owner * blocks, 8), blocks), :]
        rank = mat_product(below, mine.astype(jnp.bfloat16))
        if kind == 0:
            where_held = ids
            far = PLANES + 1 - half
            put(ROW_FAR, listed(column(mine, far), column(rank, far), ids))
            put(ROW_NEAR, listed(column(mine, near), column(rank, near), ids))
        elif kind == 1:
            where_held = column(rank, z)
        else:
            where_held = column(rank, z + inner * (PLANES + half - z))
            edge = 3 * half
            put(
                ROW_PASS + kind - 2,
                listed(column(mine, edge), column(rank, edge), column(rank, PLANES + half)),
            )
        for slot in range(slots):
            wish = wishes_of[slot][pl.ds(owner, 1), :]
            held = jnp.where(wish == block_id, where_held, 0.0)
            put(ROW_SERVE + kind * slots + slot, jnp.sum(held, axis=0, keepdims=True))
            if kind == 0:
                put(row_wish + slot, wish)


def prelude_kernel(n, slots, blocks, rungs, tile, *refs):
    mine, rows, weight, hidden, plan, taken = refs[:6]
    wishes = refs[6 : 6 + 2 * slots]
    present, send_sem, recv_sem = refs[6 + 2 * slots :]
    me = lax.axis_index("nodes")
    barrier = pltpu.get_barrier_semaphore()

    def greet(step, carry):
        pl.semaphore_signal(
            barrier, inc=1, device_id=(lax.rem(me + step, n),), device_id_type=MESH
        )
        return carry

    lax.fori_loop(1, n, greet, 0)
    taken[me] = mine[...]
    pl.semaphore_wait(barrier, n - 1)

    def send(step, carry):
        pltpu.make_async_remote_copy(
            src_ref=mine,
            dst_ref=taken.at[me],
            send_sem=send_sem,
            recv_sem=recv_sem,
            device_id=(lax.rem(me + step, n),),
            device_id_type=MESH,
        ).start()
        return carry

    lax.fori_loop(1, n, send, 0)
    half_weight = to_half(weight[...])

    def project(at, carry):
        window = pl.ds(pl.multiple_of(at * tile, tile), tile)
        hidden[window, :] = to_half(left_product(rows[:, window], half_weight))
        return carry

    lax.fori_loop(0, rows.shape[1] // tile, project, 0)
    others = taken.at[pl.ds(0, n - 1)]
    pltpu.make_async_copy(others, others, recv_sem).wait()
    pltpu.make_async_copy(others, others, send_sem).wait()

    every = taken[...].reshape(n, 2 * slots * LANES)
    unit = lax.broadcasted_iota(jnp.int32, (n, LANES), 0) == lax.broadcasted_iota(
        jnp.int32, (n, LANES), 1
    )
    unit = jnp.where(unit, 1.0, 0.0).astype(jnp.bfloat16)
    for slot in range(slots):
        part = every[:, slot * LANES : (slot + 1) * LANES]
        turned = left_product(part.astype(jnp.float32).astype(jnp.bfloat16), unit)
        wishes[slot][...] = turned[:n].astype(jnp.int32)
        wishes[slots + slot][...] = every[:, (slots + slot) * LANES : (slots + slot + 1) * LANES]
    for way in range(2):
        lay_plan(
            n,
            slots,
            blocks,
            rungs,
            way,
            wishes[way * slots : (way + 1) * slots],
            plan,
            present,
        )


def prelude(n, slots, blocks, rungs, mine, rows, weight):
    count, width = rows.shape[1], weight.shape[1]
    vmem = pl.BlockSpec(memory_space=pltpu.VMEM)
    plan_shape = (2, plan_rows(slots)[2], LANES)
    return pl.pallas_call(
        functools.partial(prelude_kernel, n, slots, blocks, rungs, 512),
        out_shape=(
            jax.ShapeDtypeStruct((count, width), jnp.bfloat16),
            jax.ShapeDtypeStruct(plan_shape, jnp.int32),
        ),
        in_specs=[vmem, vmem, vmem],
        out_specs=(vmem, vmem),
        scratch_shapes=[pltpu.VMEM((n,) + mine.shape, jnp.int32)]
        + [pltpu.VMEM((n, LANES), jnp.int32) for _ in range(2 * slots)]
        + [
            pltpu.VMEM((n * blocks, LANES), jnp.float32),
            pltpu.SemaphoreType.DMA,
            pltpu.SemaphoreType.DMA,
        ],
        compiler_params=pltpu.CompilerParams(
            collective_id=0, has_side_effects=True, vmem_limit_bytes=40 * 2**20
        ),
        name="prelude",
    )(mine, rows, weight)


def shards(
    features,
    labels,
    labelled,
    label_count,
    need_blocks,
    need_count,
    target_block,
    adjacency,
    embed_weight,
    pair_weight,
    merge_weight,
    head_weight,
    embed_moment,
    pair_moment,
    merge_moment,
    head_moment,
    embed_variance,
    pair_variance,
    merge_variance,
    head_variance,
):
    row_count = features.shape[0]
    hidden_width = embed_weight.shape[1]
    block_rows = adjacency.shape[1]
    slots = need_blocks.shape[2]
    n = lax.axis_size("nodes")
    size = n // PLANES
    block_count = row_count // block_rows
    alive = lax.broadcasted_iota(jnp.int32, need_blocks.shape[1:], 1) < need_count[0][:, None]
    raw = jnp.stack([need_blocks[0], target_block[0]])
    raw = jnp.where(alive, raw, block_count).transpose(0, 2, 1).reshape(2 * slots, n)
    raw = jnp.pad(raw, ((0, 0), (0, LANES - n)), constant_values=block_count)
    near_full = min(block_count, size * slots)
    rungs = [(min(23, block_count), min(15, near_full)), (block_count, near_full)]
    if near_full > 16:
        rungs = rungs[1:]
    hidden_half, plan = prelude(
        n, slots, block_count, rungs, raw.reshape(1, 2 * slots * LANES), features.T, embed_weight
    )
    row_wish, row_rung, _ = plan_rows(slots)

    def swap(way, *held):
        def at(rung):
            far_cap, near_cap = rungs[rung]
            return lambda *held: exchange(
                n, slots, far_cap, near_cap, 2 + way * len(rungs) + rung, *held
            )

        if len(rungs) == 1:
            return at(0)(plan[way], *held)
        branches = [at(rung) for rung in range(len(rungs))]
        return lax.switch(plan[way, row_rung, 0], branches, plan[way], *held)

    pair_half = to_half(pair_weight)
    merge_half = to_half(merge_weight)
    head_half = to_half(head_weight)
    got = swap(0, hidden_half.reshape(block_count, block_rows, hidden_width))
    gathered = gather_sum(
        False, slots, raw, adjacency, got, block_count
    ).reshape(row_count, hidden_width)
    adjacency_later, gathered = lax.optimization_barrier((adjacency, gathered))
    edges_back = lax.all_to_all(adjacency_later, "nodes", split_axis=0, concat_axis=0, tiled=True)

    self_part = mat_product(hidden_half, pair_half[0, 0])
    neigh_part = mat_product(gathered, pair_half[0, 1])
    joined = to_half(jnp.concatenate([self_part, neigh_part], axis=1))
    linear = mat_product(joined, merge_half[0])
    active = linear * jax.nn.sigmoid(linear)
    scale = lax.rsqrt(jnp.sum(active * active, axis=1, keepdims=True) + norm_eps)
    output = active * scale
    final_half = to_half(output)
    logits = mat_product(final_half, head_half)
    truth = labels.astype(jnp.float32)
    row_mask = labelled.astype(jnp.float32)[:, None]
    denom = label_count[0].astype(jnp.float32) * logits.shape[1]
    per_entry = jnp.maximum(logits, 0.0) - logits * truth + jnp.log1p(jnp.exp(-jnp.abs(logits)))
    loss_part = jnp.sum(per_entry * row_mask) / denom
    grad_logits = to_half((jax.nn.sigmoid(logits) - truth) * row_mask / denom)
    head_grad = left_product(final_half, grad_logits)
    grad_out = right_product(grad_logits, head_half)
    grad_active = scale * (grad_out - output * jnp.sum(grad_out * output, axis=1, keepdims=True))
    sig_value = jax.nn.sigmoid(linear)
    grad_linear = to_half(grad_active * sig_value * (1.0 + linear * (1.0 - sig_value)))
    merge_grad = left_product(joined, grad_linear)
    grad_joined = to_half(right_product(grad_linear, merge_half[0]))
    grad_self_out = grad_joined[:, :hidden_width]
    grad_neigh_out = grad_joined[:, hidden_width:]
    grad_self = left_product(hidden_half, grad_self_out)
    grad_neigh = left_product(gathered, grad_neigh_out)
    grad_gathered = to_half(right_product(grad_neigh_out, pair_half[0, 1]))
    label_width = head_grad.shape[1]
    spread = jnp.zeros((hidden_width, LANES - label_width), jnp.float32)
    spread = spread.at[0, 0].set(loss_part)
    head_wide = jnp.concatenate([head_grad, spread], axis=1).reshape(-1, hidden_width)
    part = jnp.concatenate([grad_self, grad_neigh, merge_grad, head_wide], axis=0)
    part_rows = Summer.padded(n, part.shape[0], hidden_width)
    part = jnp.pad(part, ((0, part_rows - part.shape[0]), (0, 0)))
    back, total = swap(1, grad_gathered.reshape(block_count, block_rows, hidden_width), part)
    pair_grad = total[: 2 * hidden_width].reshape(pair_weight.shape)
    merge_grad = total[2 * hidden_width : 4 * hidden_width].reshape(merge_weight.shape)
    head_wide = total[4 * hidden_width : 4 * hidden_width + head_wide.shape[0]]
    head_wide = head_wide.reshape(hidden_width, LANES)
    head_grad = head_wide[:, :label_width]
    loss_total = head_wide[0, label_width]

    grad_hidden = gather_sum(
        True, row_wish, plan[0], edges_back, back, block_count, grad_joined, pair_half[0, 0]
    ).reshape(row_count, hidden_width)
    embed_grad = finish(n, features.T, grad_hidden, 1)[: features.shape[1]]
    pair_next = adam_update(pair_weight, pair_grad, pair_moment, pair_variance)
    merge_next = adam_update(merge_weight, merge_grad, merge_moment, merge_variance)
    head_next = adam_update(head_weight, head_grad, head_moment, head_variance)
    embed_next = adam_update(embed_weight, embed_grad, embed_moment, embed_variance)
    return (
        loss_total.reshape(1),
        embed_next[0],
        pair_next[0],
        merge_next[0],
        head_next[0],
        embed_next[1],
        pair_next[1],
        merge_next[1],
        head_next[1],
        embed_next[2],
        pair_next[2],
        merge_next[2],
        head_next[2],
    )


def solution(mesh):
    split = ("nodes",)
    return jax.shard_map(
        shards,
        mesh=mesh,
        in_specs=(
            P("nodes", None),
            P("nodes", None),
            P("nodes"),
            P(),
            P("nodes", None, None),
            P("nodes", None),
            P("nodes", None, None),
            P("nodes", None, None),
        )
        + (P(),) * 12,
        out_specs=(P(),) * 13,
        check_vma=False,
    )
```

```python
import functools

import jax
import jax.numpy as jnp
from jax import lax
from jax.experimental import pallas as pl
from jax.experimental.pallas import tpu as pltpu
from jax.sharding import PartitionSpec as P

norm_eps = 1e-06
learn_rate = 0.03
beta_one = 0.9
beta_two = 0.999
adam_eps = 1e-08
decay_rate = 0.01
adam_step = 10.0

PLANES = 4
KINDS = 4
CHUNKS = 8
PARTS = 4
AHEAD = 3
NEAR_AHEAD = 3
LEAD = 2
UNROLL = False
LANES = 128
VMEM_MOST = 60 * 2**20
TILE = 1024
PIECES = 2
SUM_AT = (0, 2, 9, 13, 17, 20, 24, 30, 32)
MESH = pl.DeviceIdType.MESH


def to_half(value):
    return value.astype(jnp.bfloat16)


def mat_product(former, latter):
    return jnp.dot(former, latter, preferred_element_type=jnp.float32)


def left_product(former, latter):
    return lax.dot_general(
        former, latter, (((0,), (0,)), ((), ())), preferred_element_type=jnp.float32
    )


def right_product(former, latter):
    return lax.dot_general(
        former, latter, (((1,), (1,)), ((), ())), preferred_element_type=jnp.float32
    )


def adam_update(weight, grad, first, second):
    first_new = beta_one * first + (1.0 - beta_one) * grad
    second_new = beta_two * second + (1.0 - beta_two) * grad * grad
    first_hat = first_new * (1.0 / (1.0 - beta_one**adam_step))
    second_hat = second_new * (1.0 / (1.0 - beta_two**adam_step))
    weight_new = weight - learn_rate * (
        first_hat / (jnp.sqrt(second_hat) + adam_eps) + decay_rate * weight
    )
    return (weight_new, first_new, second_new)


def place(me, plane_size):
    z = me // plane_size
    spot = me % plane_size
    inner = (z % 2 + z // 2) % 2
    near = z + 1 - 2 * (z % 2)
    far_in = 2 - z // 2
    far_out = 3 * (1 - z // 2)
    return z, spot, inner, near, far_in, far_out


class Summer:
    STEPS = 9

    def __init__(self, n, shape, split_row=None, direct=False):
        self.n, (self.rows, self.width) = n, shape
        self.split_row, self.direct = split_row, direct
        self.size = n // PLANES
        self.chips = self.size // 2
        self.half = self.width // 2
        self.cuts = min(self.half // LANES, self.chips)
        self.cut = self.half // self.cuts
        self.bands = self.chips // self.cuts
        self.band = self.rows // self.bands
        self.shard = self.band // PLANES

    @staticmethod
    def padded(n, rows, width):
        summer = Summer(n, (rows, width))
        unit = summer.bands * PLANES * 16
        return -(-rows // unit) * unit

    def scratch(self):
        f32 = jnp.float32
        return [
            pltpu.VMEM((self.rows, self.half), f32),
            pltpu.VMEM((self.chips - 1, self.band, self.cut), f32),
            pltpu.VMEM(((1 if self.direct else 2) * self.shard, self.cut), f32),
            pltpu.VMEM(((PLANES - 1 if self.direct else 1) * self.shard, self.cut), f32),
            pltpu.SemaphoreType.DMA((8,)),
            pltpu.SemaphoreType.DMA((8,)),
        ]

    def bind(self, part, total, refs):
        self.part, self.total = part, total
        self.from_core, self.from_chip, self.from_pair, self.from_far, self.sent, self.got = refs
        me = lax.axis_index("nodes")
        self.z, spot = me // self.size, me % self.size
        self.chip, self.core = spot // 2, spot % 2
        self.low, self.high = self.z % 2, self.z // 2
        self.mine = pl.ds(pl.multiple_of(self.core * self.half, LANES), self.half)
        self.other = pl.ds(pl.multiple_of((1 - self.core) * self.half, LANES), self.half)
        self.across = self.device(self.z, self.chip, 1 - self.core)
        self.pair = self.device(self.high * 2 + 1 - self.low, self.chip, self.core)
        self.far = self.device((1 - self.high) * 2 + self.low, self.chip, self.core)

    def device(self, z, chip, core):
        return z * self.size + chip * 2 + core

    def column(self, hop):
        return self.device(lax.rem(self.z + hop, PLANES), self.chip, self.core)

    def peers(self):
        found = [self.across, self.pair, self.far]
        if self.direct:
            found = [self.across] + [self.column(hop) for hop in range(1, PLANES)]
        for hop in range(1, self.chips):
            found.append(self.device(self.z, lax.rem(self.chip + hop, self.chips), self.core))
        return found

    def patch(self, chip):
        row = pl.multiple_of((chip // self.cuts) * self.band, 8)
        col = self.core * self.half + (chip % self.cuts) * self.cut
        return row, pl.ds(pl.multiple_of(col, LANES), self.cut)

    def copy(self, hop, src, dst, device):
        pltpu.make_async_remote_copy(
            src_ref=src,
            dst_ref=dst,
            send_sem=self.sent.at[hop],
            recv_sem=self.got.at[hop],
            device_id=(device,),
            device_id_type=MESH,
        ).start()

    @staticmethod
    def settle(sem, held):
        pltpu.make_async_copy(held, held, sem).wait()

    def split(self, values, first_row):
        high = values.astype(self.total.dtype).astype(jnp.float32)
        middle = (values - high).astype(self.total.dtype).astype(jnp.float32)
        at = lax.broadcasted_iota(jnp.int32, values.shape, 0) + first_row - self.split_row
        rest = jnp.where(at == 1, values - high, values - high - middle)
        return jnp.where((at == 1) | (at == 2), rest, values)

    def column_step(self, at, band, cols, plane_shard, amount):
        part, total, shard = self.part, self.total, self.shard
        if at == 2:
            self.settle(self.got.at[1], self.from_chip)
            held = part[band, cols]
            for hop in range(1, self.chips):
                held = held + self.from_chip[hop - 1]
            part[band, cols] = held
            for hop in range(1, PLANES):
                src = part.at[plane_shard(lax.rem(self.z + hop, PLANES)), cols]
                dst = self.from_far.at[pl.ds((hop - 1) * shard, shard)]
                self.copy(3, src, dst, self.column(hop))
        elif at == 3:
            self.settle(self.got.at[3], self.from_far)
            held = part[plane_shard(self.z), cols]
            for hop in range(1, PLANES):
                held = held + self.from_far[pl.ds((hop - 1) * shard, shard), :]
            if self.split_row is not None:
                held = self.split(held, self.patch(self.chip)[0] + self.z * shard)
            total[plane_shard(self.z), cols] = held.astype(total.dtype)
            held = total.at[plane_shard(self.z), cols]
            for hop in range(1, PLANES):
                self.copy(4, held, held, self.column(hop))

    def step(self, at):
        part, total, shard = self.part, self.total, self.shard
        row, cols = self.patch(self.chip)
        band = pl.ds(row, self.band)

        def pairs(low):
            return pl.ds(pl.multiple_of(row + low * 2 * shard, 16), 2 * shard)

        def shards(high):
            return pl.ds(pl.multiple_of(row + (self.low * 2 + high) * shard, 16), shard)

        def amount(*shape):
            return total.at[pl.ds(0, shape[0]), pl.ds(0, shape[1])]

        short = self.band * total.dtype.itemsize // part.dtype.itemsize
        every_chip = self.from_chip.at[:, pl.ds(0, short)]

        def chips(hop):
            chip = lax.rem(self.chip + hop, self.chips)
            return chip, self.device(self.z, chip, self.core)

        def plane_shard(z):
            return pl.ds(pl.multiple_of(row + z * shard, 16), shard)

        if self.direct and 2 <= at <= 5:
            self.column_step(at, band, cols, plane_shard, amount)
        elif at == 0:
            self.copy(0, part.at[:, self.other], self.from_core, self.across)
        elif at == 1:
            self.settle(self.got.at[0], self.from_core)
            part[:, self.mine] += self.from_core[...]
            for hop in range(1, self.chips):
                chip, device = chips(hop)
                there, cut = self.patch(chip)
                src = part.at[pl.ds(there, self.band), cut]
                self.copy(1, src, self.from_chip.at[hop - 1], device)
        elif at == 2:
            self.settle(self.got.at[1], self.from_chip)
            held = part[band, cols]
            for hop in range(1, self.chips):
                held = held + self.from_chip[hop - 1]
            part[band, cols] = held
            self.copy(2, part.at[pairs(1 - self.low), cols], self.from_pair, self.pair)
        elif at == 3:
            self.settle(self.got.at[2], self.from_pair)
            part[pairs(self.low), cols] += self.from_pair[...]
            self.copy(3, part.at[shards(1 - self.high), cols], self.from_far, self.far)
        elif at == 4:
            self.settle(self.got.at[3], self.from_far)
            held = part[shards(self.high), cols] + self.from_far[...]
            if self.split_row is not None:
                held = self.split(held, row + (self.low * 2 + self.high) * shard)
            total[shards(self.high), cols] = held.astype(total.dtype)
            held = total.at[shards(self.high), cols]
            self.copy(4, held, held, self.far)
        elif at == 5:
            self.settle(self.got.at[4], amount(shard, self.cut))
            held = total.at[pairs(self.low), cols]
            self.copy(5, held, held, self.pair)
        elif at == 6:
            if self.direct:
                self.settle(self.got.at[4], amount((PLANES - 1) * shard, self.cut))
            else:
                self.settle(self.got.at[5], amount(2 * shard, self.cut))
            held = total.at[band, cols]
            for hop in range(1, self.chips):
                self.copy(6, held, held, chips(hop)[1])
        elif at == 7:
            self.settle(self.got.at[6], every_chip)
            held = total.at[:, self.mine]
            self.copy(7, held, held, self.across)
        else:
            self.settle(self.got.at[7], amount(self.rows, self.half))
            self.settle(self.sent.at[0], self.from_core)
            self.settle(self.sent.at[1], self.from_chip)
            self.settle(self.sent.at[3], self.from_far)
            if self.direct:
                self.settle(self.sent.at[4], amount((PLANES - 1) * shard, self.cut))
            else:
                self.settle(self.sent.at[2], self.from_pair)
                self.settle(self.sent.at[4], amount(shard, self.cut))
                self.settle(self.sent.at[5], amount(2 * shard, self.cut))
            self.settle(self.sent.at[6], every_chip)
            self.settle(self.sent.at[7], amount(self.rows, self.half))


def finish_kernel(n, tile, rows_there, grads, loss, total, part, rows, held, sem, *refs):
    fetches = [
        pltpu.make_async_copy(grads, held, sem.at[0]),
        pltpu.make_async_copy(rows_there, rows, sem.at[1]),
    ]
    for fetch in fetches:
        fetch.start()
    below = -(-rows.shape[0] // 8) * 8
    summer = Summer(n, part.shape, below, direct=True)
    summer.bind(part, total, refs)
    barrier = pltpu.get_barrier_semaphore()
    peers = summer.peers()
    for peer in peers:
        pl.semaphore_signal(barrier, inc=1, device_id=(peer,), device_id_type=MESH)
    count, depth = rows.shape

    def multiply(cols):
        part[:, cols] = jnp.zeros((part.shape[0], summer.half), jnp.float32)

        def add(at, carry):
            window = pl.ds(pl.multiple_of(at * tile, tile), tile)
            part[:count, cols] += mat_product(rows[:, window], held[window, cols])
            return carry

        lax.fori_loop(0, depth // tile, add, 0)
        part[pl.ds(below, 8), cols] = jnp.broadcast_to(loss[...], (8, summer.half))

    for fetch in fetches:
        fetch.wait()
    multiply(summer.other)
    pl.semaphore_wait(barrier, len(peers))
    summer.step(0)
    multiply(summer.mine)
    for at in range(1, Summer.STEPS):
        summer.step(at)


def finish(n, rows, grads, loss, collective):
    count = -(-rows.shape[0] // 8) * 8
    shape = (Summer.padded(n, count + 8, grads.shape[1]), grads.shape[1])
    vmem = pl.BlockSpec(memory_space=pltpu.VMEM)
    total = pl.pallas_call(
        functools.partial(finish_kernel, n, 1024),
        out_shape=jax.ShapeDtypeStruct(shape, jnp.bfloat16),
        in_specs=[
            pl.BlockSpec(memory_space=pltpu.HBM),
            pl.BlockSpec(memory_space=pltpu.HBM),
            vmem,
        ],
        out_specs=vmem,
        scratch_shapes=[
            pltpu.VMEM(shape, jnp.float32),
            pltpu.VMEM(rows.shape, rows.dtype),
            pltpu.VMEM(grads.shape, grads.dtype),
            pltpu.SemaphoreType.DMA((2,)),
        ]
        + Summer(n, shape, direct=True).scratch(),
        compiler_params=pltpu.CompilerParams(
            collective_id=collective, has_side_effects=True, vmem_limit_bytes=VMEM_MOST
        ),
        name="finish",
    )(rows, grads, loss)
    total = total.astype(jnp.float32)
    return total[: rows.shape[0]], jnp.sum(total[count : count + 3, 0])


class Exchange:
    def __init__(self, n, slots, way, far_cap, near_cap, shape, kind):
        self.n, self.slots, self.way = n, slots, way
        self.far_cap, self.near_cap = far_cap, near_cap
        self.size = n // PLANES
        self.blocks, self.depth, self.width = shape
        self.kind = kind
        self.rows = self.depth // CHUNKS
        self.cols = self.width // PARTS
        self.steps = CHUNKS * PARTS
        self.ring = self.steps if self.size <= 8 else 2

    def out_shape(self):
        return jax.ShapeDtypeStruct(
            (CHUNKS, self.size, KINDS, self.slots, self.rows, self.width), self.kind
        )

    def scratch(self):
        def piece(*lead):
            return pltpu.VMEM(lead + (self.rows, self.cols), self.kind)

        steps, ring = self.steps, self.ring
        dma = pltpu.SemaphoreType.DMA
        return (
            [piece(self.far_cap) for _ in range(steps)]
            + [piece(self.near_cap) for _ in range(2 * steps)]
            + [piece(self.far_cap) for _ in range(2 * steps)]
            + [piece(self.near_cap) for _ in range(2 * steps)]
            + [piece(self.size, 2, self.slots) for _ in range(2 * ring)]
            + [dma((steps,)), dma((steps,)), dma((steps,)), dma((2, steps)), dma((2, steps))]
            + [dma((2, ring)), dma((CHUNKS,))]
        )

    def bind(self, plan, table, out, refs):
        self.plan, self.table, self.out = plan.at[self.way], table, out
        rest = list(refs)
        steps = self.steps

        def take(count):
            found = rest[:count]
            del rest[:count]
            return found

        self.far_stage = take(steps)
        self.near_stage = take(steps)
        self.near_got = take(steps)
        self.far_got = [take(steps), take(steps)]
        self.pass_stage = [take(steps), take(steps)]
        self.serve_stage = [take(self.ring), take(self.ring)]
        (
            self.far_sent,
            self.near_sent,
            self.near_recv,
            self.far_recv,
            self.pass_sent,
            self.serve_sent,
            self.serve_recv,
        ) = rest
        me = lax.axis_index("nodes")
        self.z, self.spot, self.inner, near, far_in, far_out = place(me, self.size)
        self.near_dev = near * self.size + self.spot
        self.relay_dev = far_in * self.size + self.spot
        self.outer_dev = far_out * self.size + self.spot

    def greet(self, column=False):
        barrier = pltpu.get_barrier_semaphore()

        def hello(device):
            pl.semaphore_signal(barrier, inc=1, device_id=(device,), device_id_type=MESH)

        def in_plane(step, carry):
            hello(self.z * self.size + lax.rem(self.spot + step, self.size))
            return carry

        lax.fori_loop(1, self.size, in_plane, 0)
        hello(self.near_dev)
        if column:
            hello(((1 - self.z // 2) * 2 + self.z % 2) * self.size + self.spot)

            @pl.when(self.inner == 1)
            def _():
                hello(self.relay_dev)

            pl.semaphore_wait(barrier, self.size + 1 + self.inner)
            return

        @pl.when(self.inner == 1)
        def _():
            hello(self.relay_dev)
            hello(self.outer_dev)

        pl.semaphore_wait(barrier, self.size + 1)

    def window(self, step):
        return pl.ds((step // PARTS) * self.rows, self.rows), pl.ds(
            (step % PARTS) * self.cols, self.cols
        )

    def remote(self, src, dst, sent, got, device):
        return pltpu.make_async_remote_copy(
            src_ref=src,
            dst_ref=dst,
            send_sem=sent,
            recv_sem=got,
            device_id=(device,),
            device_id_type=MESH,
        )

    @staticmethod
    def settle(sem, held):
        pltpu.make_async_copy(held, held, sem).wait()

    def launch_far(self, step):
        rows, cols = self.window(step)
        plan, table, far_stage = self.plan, self.table, self.far_stage[step]

        def fill_far(at, carry):
            far_stage[at] = table[plan[ROW_FAR, at], rows, cols]
            return carry

        lax.fori_loop(0, self.far_cap, fill_far, 0, unroll=UNROLL)
        for lane in range(2):

            @pl.when(self.inner == 1 - lane)
            def _():
                self.remote(
                    far_stage,
                    self.far_got[lane][step],
                    self.far_sent.at[step],
                    self.far_recv.at[lane, step],
                    self.relay_dev,
                ).start()

    def launch_near(self, step):
        rows, cols = self.window(step)
        plan, table, near_stage = self.plan, self.table, self.near_stage[step]

        def fill_near(at, carry):
            near_stage[at] = table[plan[ROW_NEAR, at], rows, cols]
            return carry

        lax.fori_loop(0, self.near_cap, fill_near, 0, unroll=UNROLL)
        self.remote(
            near_stage,
            self.near_got[step],
            self.near_sent.at[step],
            self.near_recv.at[step],
            self.near_dev,
        ).start()

    def relay(self, step):
        plan = self.plan

        @pl.when(self.inner == 1)
        def _():
            for lane in range(2):
                got, stage = self.far_got[lane][step], self.pass_stage[lane][step]
                self.settle(self.far_recv.at[lane, step], got)

                def fill(at, carry):
                    stage[at] = got[plan[ROW_PASS + lane, at]]
                    return carry

                lax.fori_loop(0, self.near_cap, fill, 0, unroll=UNROLL)
                self.remote(
                    stage,
                    got.at[pl.ds(0, self.near_cap)],
                    self.pass_sent.at[lane, step],
                    self.far_recv.at[lane, step],
                    self.near_dev,
                ).start()

        @pl.when(self.inner == 0)
        def _():
            for lane in range(2):
                got = self.far_got[lane][step].at[pl.ds(0, self.near_cap)]
                self.settle(self.far_recv.at[lane, step], got)

    def serve(self, step, pair):
        rows, cols = self.window(step)
        plan, table, slots, size = self.plan, self.table, self.slots, self.size
        chunk, slot_at = step // PARTS, step % self.ring
        if pair == 0:
            self.settle(self.near_recv.at[step], self.near_got[step])
        if step >= self.ring:
            self.drain(step - self.ring, pair)
        stage = self.serve_stage[pair][slot_at]

        def fill(peer, carry):
            taker = self.z * size + peer
            for slot in range(slots):
                first = plan[ROW_SERVE + 2 * pair * slots + slot, taker]
                second = plan[ROW_SERVE + (2 * pair + 1) * slots + slot, taker]
                if pair == 0:
                    stage[peer, 0, slot] = table[first, rows, cols]
                    stage[peer, 1, slot] = self.near_got[step][second]
                else:
                    stage[peer, 0, slot] = self.far_got[0][step][first]
                    stage[peer, 1, slot] = self.far_got[1][step][second]
            return carry

        lax.fori_loop(0, size, fill, 0)
        there = self.out.at[chunk, self.spot, pl.ds(2 * pair, 2), :, :, cols]
        pltpu.make_async_copy(stage.at[self.spot], there, self.serve_recv.at[chunk]).start()

        def send(hop, carry):
            peer = lax.rem(self.spot + hop, size)
            self.remote(
                stage.at[peer],
                there,
                self.serve_sent.at[pair, slot_at],
                self.serve_recv.at[chunk],
                self.z * size + peer,
            ).start()
            return carry

        lax.fori_loop(1, size, send, 0)

    def drain(self, step, pair):
        slot_at = step % self.ring
        held = self.serve_stage[pair][slot_at].at[pl.ds(0, self.size - 1)]
        self.settle(self.serve_sent.at[pair, slot_at], held)

    def run(self, side=None):
        steps = self.steps
        for step in range(min(AHEAD, steps)):
            self.launch_far(step)
            self.launch_near(step)

        @pl.when(self.inner == 1)
        def _():
            for step in range(AHEAD, min(NEAR_AHEAD, steps)):
                self.launch_near(step)

        for step in range(min(LEAD, steps)):
            self.serve(step, 0)
        for step in range(steps):
            if step + AHEAD < steps:
                self.launch_far(step + AHEAD)
                if NEAR_AHEAD == AHEAD:
                    self.launch_near(step + AHEAD)
                else:

                    @pl.when(self.inner == 0)
                    def _():
                        self.launch_near(step + AHEAD)

            if NEAR_AHEAD > AHEAD and step + NEAR_AHEAD < steps:

                @pl.when(self.inner == 1)
                def _():
                    self.launch_near(step + NEAR_AHEAD)

            self.relay(step)
            self.serve(step, 1)
            if step + LEAD < steps:
                self.serve(step + LEAD, 0)
            if side is not None:
                side(step)
        if side is not None:
            side(steps)
        for chunk in range(CHUNKS):
            self.settle(self.serve_recv.at[chunk], self.out.at[chunk])
        for step in range(max(0, steps - self.ring), steps):
            self.drain(step, 0)
            self.drain(step, 1)
        for step in range(steps):
            self.settle(self.far_sent.at[step], self.far_stage[step])
            self.settle(self.near_sent.at[step], self.near_stage[step])

        @pl.when(self.inner == 1)
        def _():
            for step in range(steps):
                for lane in range(2):
                    self.settle(self.pass_sent.at[lane, step], self.pass_stage[lane][step])


def exchange_kernel(moves, plan, table, out, held_table, table_sem, *refs):
    moves.bind(plan, held_table, out, refs)
    fetch = pltpu.make_async_copy(table, held_table, table_sem)
    fetch.start()
    moves.greet()
    fetch.wait()
    moves.run()


def exchange_sum_kernel(
    moves, summer, plan, table, part, out, total, held_table, table_sem, held, sem, *refs
):
    moves.bind(plan, held_table, out, refs[6:])
    fetch_table = pltpu.make_async_copy(table, held_table, table_sem)
    fetch_table.start()
    summer.bind(held, total, refs[:6])
    fetch = pltpu.make_async_copy(part, held, sem)
    fetch.start()
    moves.greet(column=True)
    fetch_table.wait()

    def side(step):
        if step == 0:
            fetch.wait()
        if step in SUM_AT:
            summer.step(SUM_AT.index(step))

    moves.run(side)


def exchange(n, slots, way, far_cap, near_cap, collective, plan, table, part=None):
    moves = Exchange(n, slots, way, far_cap, near_cap, table.shape, table.dtype)
    hbm = pl.BlockSpec(memory_space=pl.ANY)
    vmem = pl.BlockSpec(memory_space=pltpu.VMEM)
    in_specs = [pl.BlockSpec(memory_space=pltpu.SMEM), hbm]
    table_held = [pltpu.VMEM(table.shape, table.dtype), pltpu.SemaphoreType.DMA]
    params = pltpu.CompilerParams(
        collective_id=collective, has_side_effects=True, vmem_limit_bytes=VMEM_MOST
    )
    if part is None:
        return pl.pallas_call(
            functools.partial(exchange_kernel, moves),
            out_shape=moves.out_shape(),
            in_specs=in_specs,
            out_specs=hbm,
            scratch_shapes=table_held + moves.scratch(),
            compiler_params=params,
            name="exchange",
        )(plan, table)
    summer = Summer(n, part.shape)
    return pl.pallas_call(
        functools.partial(exchange_sum_kernel, moves, summer),
        out_shape=(moves.out_shape(), jax.ShapeDtypeStruct(part.shape, jnp.bfloat16)),
        in_specs=in_specs + [hbm],
        out_specs=(hbm, vmem),
        scratch_shapes=table_held
        + [pltpu.VMEM(part.shape, jnp.float32), pltpu.SemaphoreType.DMA]
        + summer.scratch()
        + moves.scratch(),
        compiler_params=params,
        name="exchange_sum",
    )(plan, table, part)


def add_products(flip, slots, first_row, sinks, weights, got, total, at, size):
    z, _, _, near, far_in, far_out = place(lax.axis_index("nodes"), size)
    depth, width = total.shape[1:]
    dims = (((0,), (0,)), ((), ())) if flip else (((1,), (0,)), ((), ()))
    for kind, owner_z in enumerate((z, near, far_in, far_out)):
        for slot in range(slots):
            sink = sinks[first_row + slot, owner_z * size + at]
            rows = got[:, 0, kind, slot].reshape(depth, width)
            total[sink] += lax.dot_general(
                weights[owner_z, 0, slot], rows, dims, preferred_element_type=jnp.float32
            )


def return_sum_kernel(slots, first_row, *refs):
    sinks, weights, got, own, mixer = refs[:5]
    states, head_state, out = refs[5:13], refs[13:17], refs[17]
    updates, head_update, total = refs[18:24], refs[24:27], refs[27]
    at = pl.program_id(0)
    blocks, depth, width = out.shape

    @pl.when(at == 0)
    def _():
        total[...] = jnp.zeros_like(total)
        label_width = head_state[0].shape[1]
        head_grad = head_state[1][...].astype(jnp.float32).T[:, :label_width]
        fresh = adam_update(head_state[0][...], head_grad, head_state[2][...], head_state[3][...])
        for to, values in zip(head_update, fresh):
            to[...] = values

    span = own.shape[0] // depth
    base = right_product(own[...], mixer[...]).reshape(span, depth, width)
    total[pl.ds(at * span, span)] += base
    for state, update in ((states[:4], updates[:3]), (states[4:], updates[3:])):
        grad = state[1][...].astype(jnp.float32)
        fresh = adam_update(state[0][...], grad, state[2][...], state[3][...])
        for to, values in zip(update, fresh):
            to[...] = values
    size = pl.num_programs(0)
    add_products(True, slots, first_row, sinks, weights, got, total, at, size)

    @pl.when(at == pl.num_programs(0) - 1)
    def _():
        out[...] = to_half(total[:blocks])


def block_specs(weights, got):
    chunks, size, kinds, slots, rows, width = got.shape
    depth = chunks * rows
    edges = weights.reshape(PLANES, size, slots, depth, depth)

    def clip(at):
        return jnp.minimum(at, size - 1)

    specs = [
        pl.BlockSpec((PLANES, 1, slots, depth, depth), lambda at, *_: (0, clip(at), 0, 0, 0)),
        pl.BlockSpec(
            (chunks, 1, kinds, slots, rows, width), lambda at, *_: (0, clip(at), 0, 0, 0, 0)
        ),
    ]
    return edges, specs


def return_sum(first_row, sinks, weights, got, blocks, own, mixer, grads, groups, head):
    chunks, size, _, slots, rows, width = got.shape
    depth = chunks * rows
    edges, specs = block_specs(weights, got)
    tile = blocks * depth // size
    specs = specs + [
        pl.BlockSpec((tile, width), lambda at, sinks: (at, 0)),
        pl.BlockSpec((width, width), lambda at, sinks: (0, 0)),
    ]
    states, shapes, out_specs = [], [], []
    for place_at, (weight, first, second) in enumerate(groups):
        part = weight.shape[0] // size
        spec = pl.BlockSpec((part, width), lambda at, sinks: (at, 0))
        moved = pl.BlockSpec((part, width), lambda at, sinks, p=place_at: (at + p * size, 0))
        states += [weight, grads, first, second]
        specs = specs + [spec, moved, spec, spec]
        shapes += [jax.ShapeDtypeStruct(weight.shape, jnp.float32)] * 3
        out_specs += [spec] * 3
    head_at = 2 * groups[0][0].shape[0] // LANES
    still = pl.BlockSpec(head[0].shape, lambda at, sinks: (0, 0))
    states += [head[0], grads, head[1], head[2]]
    specs = specs + [still, pl.BlockSpec((LANES, width), lambda at, sinks: (head_at, 0)), still, still]
    shapes += [jax.ShapeDtypeStruct(head[0].shape, jnp.float32)] * 3
    out_specs += [still] * 3
    found = pl.pallas_call(
        functools.partial(return_sum_kernel, slots, first_row),
        out_shape=[jax.ShapeDtypeStruct((blocks, depth, width), jnp.bfloat16)] + shapes,
        grid_spec=pltpu.PrefetchScalarGridSpec(
            num_scalar_prefetch=1,
            grid=(size,),
            in_specs=specs,
            out_specs=[pl.BlockSpec((blocks, depth, width), lambda at, sinks: (0, 0, 0))]
            + out_specs,
            scratch_shapes=[pltpu.VMEM((blocks + 1, depth, width), jnp.float32)],
        ),
        compiler_params=pltpu.CompilerParams(vmem_limit_bytes=48 * 2**20),
        name="return_sum",
    )(sinks, edges, got, own, mixer, *states)
    return found[0], found[1:4], found[4:7], found[7:10]


ROW_FAR, ROW_NEAR, ROW_PASS, ROW_SERVE = 0, 1, 2, 4


def plan_rows(slots):
    wishes = ROW_SERVE + KINDS * slots
    return wishes, -(-(wishes + slots) // 8) * 8


def column(values, lane):
    lanes = lax.broadcasted_iota(jnp.int32, values.shape, 1)
    return jnp.sum(jnp.where(lanes == lane, values, 0.0), axis=1, keepdims=True)


def lay_plan(n, slots, blocks, rungs, way, wishes_of, plan, chosen, present):
    size = n // PLANES
    me = lax.axis_index("nodes")
    z, spot, inner, near, far_in, far_out = place(me, size)
    half = z // 2
    row_wish, _ = plan_rows(slots)

    taker = lax.broadcasted_iota(jnp.int32, (LANES, LANES), 0)
    group = lax.broadcasted_iota(jnp.int32, (LANES, LANES), 1)
    plane_of = taker // size
    member = (taker < n) & ((plane_of == group) | (plane_of // 2 + PLANES == group))
    member = jnp.where(member, 1.0, 0.0).astype(jnp.bfloat16)
    hits = jnp.zeros((n * blocks, LANES), jnp.float32)
    for slot in range(slots):
        wish = wishes_of[slot][...]
        ids = lax.broadcasted_iota(jnp.int32, (n, blocks, LANES), 1)
        hot = jnp.where(wish[:, None, :] == ids, 1.0, 0.0).astype(jnp.bfloat16)
        hits = hits + mat_product(hot.reshape(n * blocks, LANES), member)
    here = jnp.where(hits > 0.0, 1.0, 0.0)
    present[...] = here
    counts = jnp.sum(here.reshape(n, blocks, LANES), axis=1)
    owner_plane = lax.broadcasted_iota(jnp.int32, (n, LANES), 0) // size
    lane = lax.broadcasted_iota(jnp.int32, (n, LANES), 1)
    is_near = (lane < PLANES) & (lane != owner_plane)
    is_far = (lane >= PLANES) & (lane < PLANES + 2) & (lane - PLANES != owner_plane // 2)
    near_most = jnp.max(jnp.where(is_near, counts, 0.0), axis=(0, 1), keepdims=True)
    far_most = jnp.max(jnp.where(is_far, counts, 0.0), axis=(0, 1), keepdims=True)
    rung = jnp.zeros((1, 1), jnp.float32)
    for far_cap, near_cap in rungs[:-1]:
        over = (far_most > float(far_cap)) | (near_most > float(near_cap))
        rung = rung + jnp.where(over, 1.0, 0.0)

    def put(row, values):
        plan[way, pl.ds(row, 1), :] = values.astype(jnp.int32)

    chosen[...] = rung.astype(jnp.int32)
    block_id = lax.broadcasted_iota(jnp.int32, (blocks, LANES), 0)
    block_lane = lax.broadcasted_iota(jnp.int32, (blocks, LANES), 1)
    ids = block_id.astype(jnp.float32)
    below = lax.broadcasted_iota(jnp.int32, (blocks, blocks), 0) > lax.broadcasted_iota(
        jnp.int32, (blocks, blocks), 1
    )
    below = jnp.where(below, 1.0, 0.0).astype(jnp.bfloat16)

    def listed(chosen, pos, values):
        at = (chosen > 0.0) & (pos.astype(jnp.int32) == block_lane)
        return jnp.sum(jnp.where(at, values, 0.0), axis=0, keepdims=True)

    for kind, owner_z in enumerate((z, near, far_in, far_out)):
        owner = owner_z * size + spot
        mine = present[pl.ds(pl.multiple_of(owner * blocks, 8), blocks), :]
        rank = mat_product(below, mine.astype(jnp.bfloat16))
        if kind == 0:
            where_held = ids
            far = PLANES + 1 - half
            put(ROW_FAR, listed(column(mine, far), column(rank, far), ids))
            put(ROW_NEAR, listed(column(mine, near), column(rank, near), ids))
        elif kind == 1:
            where_held = column(rank, z)
        else:
            where_held = column(rank, z + inner * (PLANES + half - z))
            edge = 3 * half
            put(
                ROW_PASS + kind - 2,
                listed(column(mine, edge), column(rank, edge), column(rank, PLANES + half)),
            )
        for slot in range(slots):
            wish = wishes_of[slot][pl.ds(owner, 1), :]
            held = jnp.where(wish == block_id, where_held, 0.0)
            put(ROW_SERVE + kind * slots + slot, jnp.sum(held, axis=0, keepdims=True))
            if kind == 0:
                put(row_wish + slot, wish)


def prelude_kernel(n, slots, blocks, rungs, tile, *refs):
    mine, rows, weight, hidden, plan = refs[:5]
    chosen, taken = refs[5:7], refs[7]
    wishes = refs[8 : 8 + 2 * slots]
    present, held, held_weight, row_sem, weight_sem, send_sem, recv_sem = refs[8 + 2 * slots :]
    tiles = rows.shape[1] // tile

    def window(at):
        return pl.ds(pl.multiple_of(at * tile, tile), tile)

    def fetch(at):
        part = window(at)
        return pltpu.make_async_copy(rows.at[:, part], held.at[:, part], row_sem.at[at])

    fetch_weight = pltpu.make_async_copy(weight, held_weight, weight_sem)
    fetch_weight.start()
    for at in range(tiles):
        fetch(at).start()
    me = lax.axis_index("nodes")
    barrier = pltpu.get_barrier_semaphore()

    def greet(step, carry):
        pl.semaphore_signal(
            barrier, inc=1, device_id=(lax.rem(me + step, n),), device_id_type=MESH
        )
        return carry

    lax.fori_loop(1, n, greet, 0)
    taken[me] = mine[...]
    fetch_weight.wait()
    half_weight = to_half(held_weight[...])

    def project(at):
        fetch(at).wait()
        hidden[window(at), :] = to_half(left_product(held[:, window(at)], half_weight))

    for at in range(tiles // 2):
        project(at)
    pl.semaphore_wait(barrier, n - 1)

    def send(step, carry):
        pltpu.make_async_remote_copy(
            src_ref=mine,
            dst_ref=taken.at[me],
            send_sem=send_sem,
            recv_sem=recv_sem,
            device_id=(lax.rem(me + step, n),),
            device_id_type=MESH,
        ).start()
        return carry

    lax.fori_loop(1, n, send, 0)
    for at in range(tiles // 2, tiles):
        project(at)
    others = taken.at[pl.ds(0, n - 1)]
    pltpu.make_async_copy(others, others, recv_sem).wait()
    pltpu.make_async_copy(others, others, send_sem).wait()

    every = taken[...].reshape(n, 2 * slots * LANES)
    unit = lax.broadcasted_iota(jnp.int32, (n, LANES), 0) == lax.broadcasted_iota(
        jnp.int32, (n, LANES), 1
    )
    unit = jnp.where(unit, 1.0, 0.0).astype(jnp.bfloat16)
    for slot in range(slots):
        part = every[:, slot * LANES : (slot + 1) * LANES]
        turned = left_product(part.astype(jnp.float32).astype(jnp.bfloat16), unit)
        wishes[slot][...] = turned[:n].astype(jnp.int32)
        wishes[slots + slot][...] = every[:, (slots + slot) * LANES : (slots + slot + 1) * LANES]
    for way in range(2):
        lay_plan(
            n,
            slots,
            blocks,
            rungs,
            way,
            wishes[way * slots : (way + 1) * slots],
            plan,
            chosen[way],
            present,
        )


def prelude(n, slots, blocks, rungs, mine, rows, weight):
    count, width = rows.shape[1], weight.shape[1]
    vmem = pl.BlockSpec(memory_space=pltpu.VMEM)
    plan_shape = (2, plan_rows(slots)[1], LANES)
    return pl.pallas_call(
        functools.partial(prelude_kernel, n, slots, blocks, rungs, 512),
        out_shape=(
            jax.ShapeDtypeStruct((count, width), jnp.bfloat16),
            jax.ShapeDtypeStruct(plan_shape, jnp.int32),
            jax.ShapeDtypeStruct((1, 1), jnp.int32),
            jax.ShapeDtypeStruct((1, 1), jnp.int32),
        ),
        in_specs=[vmem, pl.BlockSpec(memory_space=pltpu.HBM), pl.BlockSpec(memory_space=pltpu.HBM)],
        out_specs=(vmem, vmem, vmem, vmem),
        scratch_shapes=[pltpu.VMEM((n,) + mine.shape, jnp.int32)]
        + [pltpu.VMEM((n, LANES), jnp.int32) for _ in range(2 * slots)]
        + [
            pltpu.VMEM((n * blocks, LANES), jnp.float32),
            pltpu.VMEM(rows.shape, rows.dtype),
            pltpu.VMEM(weight.shape, weight.dtype),
            pltpu.SemaphoreType.DMA((count // 512,)),
            pltpu.SemaphoreType.DMA,
            pltpu.SemaphoreType.DMA,
            pltpu.SemaphoreType.DMA,
        ],
        compiler_params=pltpu.CompilerParams(
            collective_id=0, has_side_effects=True, vmem_limit_bytes=VMEM_MOST
        ),
        name="prelude",
    )(mine, rows, weight)


def sigmoid(values):
    return 1.0 / (1.0 + jnp.exp(-values))


def dense_kernel(label_width, pieces, slots, first_row, count, sinks, edges, got, *refs):
    marks, truth, own, pair, merge, head = refs[:6]
    grad_own, grad_taken, part, loss, total = refs[6:]
    at = pl.program_id(0)
    gathers = pl.num_programs(0) - total.shape[0] * total.shape[1] // own.shape[0]

    @pl.when(at == 0)
    def _():
        total[...] = jnp.zeros_like(total)
        part[...] = jnp.zeros_like(part)
        loss[...] = jnp.zeros_like(loss)

    @pl.when(at < gathers)
    def _():
        add_products(False, slots, first_row, sinks, edges, got, total, at, gathers)

    @pl.when(at >= gathers)
    def _():
        span = own.shape[0] // total.shape[1]
        taken = total.at[pl.ds((at - gathers) * span, span)]
        dense_tile(
            label_width,
            pieces,
            (count, marks, truth, own, taken, pair, merge, head),
            (grad_own, grad_taken, part, loss),
        )


def dense_tile(label_width, pieces, given, made):
    count, marks, truth, own, taken, pair, merge, head = given
    grad_own, grad_taken, part, loss = made
    width = own.shape[1]
    tile = own.shape[0] // pieces
    span = taken.shape[0] // pieces
    denom = count[0].astype(jnp.float32) * float(label_width)
    for piece in range(pieces):
        rows = pl.ds(piece * tile, tile)
        hidden = own[rows, :]
        gathered = to_half(taken[pl.ds(piece * span, span)]).reshape(tile, width)
        self_part = to_half(mat_product(hidden, pair[0]))
        neigh_part = to_half(mat_product(gathered, pair[1]))
        linear = mat_product(self_part, merge[:width]) + mat_product(neigh_part, merge[width:])
        sig = sigmoid(linear)
        active = linear * sig
        scale = lax.rsqrt(jnp.sum(active * active, axis=1, keepdims=True) + norm_eps)
        output = active * scale
        final = to_half(output)
        logits = mat_product(final, head[...])
        labels = truth[rows, :].astype(jnp.float32)
        labels = jnp.pad(labels, ((0, 0), (0, LANES - label_width)))
        marked = marks[0, :, rows].astype(jnp.float32)
        marked = jnp.broadcast_to(marked, (LANES, tile)).T
        column_id = lax.broadcasted_iota(jnp.int32, (tile, LANES), 1)
        marked = jnp.where(column_id < label_width, marked, 0.0)
        decay = jnp.exp(-jnp.abs(logits))
        entry = jnp.maximum(logits, 0.0) - logits * labels + jnp.log1p(decay)
        loss[...] += jnp.sum(entry * marked, axis=(0, 1), keepdims=True) / denom
        grad_logits = to_half((sigmoid(logits) - labels) * marked / denom)
        part[pl.ds(4 * width, LANES), :] += left_product(grad_logits, final)
        grad_out = right_product(grad_logits, head[...])
        along = jnp.sum(grad_out * output, axis=1, keepdims=True)
        grad_active = scale * (grad_out - output * along)
        grad_linear = to_half(grad_active * sig * (1.0 + linear * (1.0 - sig)))
        part[pl.ds(2 * width, width), :] += left_product(self_part, grad_linear)
        part[pl.ds(3 * width, width), :] += left_product(neigh_part, grad_linear)
        grad_self = to_half(right_product(grad_linear, merge[:width]))
        grad_neigh = to_half(right_product(grad_linear, merge[width:]))
        grad_own[rows, :] = grad_self
        part[pl.ds(0, width), :] += left_product(hidden, grad_self)
        part[pl.ds(width, width), :] += left_product(gathered, grad_neigh)
        grad_taken[rows, :] = to_half(right_product(grad_neigh, pair[1]))


def dense(tile, pieces, part_rows, first_row, scalars, edges, got, marks, truth, own, weights):
    rows, width = own.shape
    label_width = truth.shape[1]
    size, slots = got.shape[1], got.shape[3]
    edges, specs = block_specs(edges, got)
    depth = edges.shape[-1]

    def later(at):
        return jnp.maximum(at - size, 0)

    by_rows = pl.BlockSpec((tile, width), lambda at, *_: (later(at), 0))

    def whole(values):
        return pl.BlockSpec(values.shape, lambda at, *_: (0,) * values.ndim)

    return pl.pallas_call(
        functools.partial(dense_kernel, label_width, pieces, slots, first_row),
        out_shape=(
            jax.ShapeDtypeStruct((rows, width), jnp.bfloat16),
            jax.ShapeDtypeStruct((rows, width), jnp.bfloat16),
            jax.ShapeDtypeStruct((part_rows, width), jnp.float32),
            jax.ShapeDtypeStruct((1, 1), jnp.float32),
        ),
        grid_spec=pltpu.PrefetchScalarGridSpec(
            num_scalar_prefetch=2,
            grid=(size + rows // tile,),
            in_specs=specs
            + [
                pl.BlockSpec((1, 1, tile), lambda at, *_: (later(at), 0, 0)),
                pl.BlockSpec((tile, label_width), lambda at, *_: (later(at), 0)),
                by_rows,
            ]
            + [whole(values) for values in weights],
            out_specs=(
                by_rows,
                by_rows,
                pl.BlockSpec((part_rows, width), lambda at, *_: (0, 0)),
                pl.BlockSpec((1, 1), lambda at, *_: (0, 0)),
            ),
            scratch_shapes=[pltpu.VMEM((rows // depth + 1, depth, width), jnp.float32)],
        ),
        compiler_params=pltpu.CompilerParams(vmem_limit_bytes=VMEM_MOST),
        name="dense",
    )(*scalars, edges, got, marks.reshape(rows // tile, 1, tile), truth, own, *weights)


def shards(
    features,
    labels,
    labelled,
    label_count,
    need_blocks,
    need_count,
    target_block,
    adjacency,
    embed_weight,
    pair_weight,
    merge_weight,
    head_weight,
    embed_moment,
    pair_moment,
    merge_moment,
    head_moment,
    embed_variance,
    pair_variance,
    merge_variance,
    head_variance,
):
    row_count = features.shape[0]
    hidden_width = embed_weight.shape[1]
    block_rows = adjacency.shape[1]
    slots = need_blocks.shape[2]
    n = lax.axis_size("nodes")
    size = n // PLANES
    block_count = row_count // block_rows
    alive = lax.broadcasted_iota(jnp.int32, need_blocks.shape[1:], 1) < need_count[0][:, None]
    raw = jnp.stack([need_blocks[0], target_block[0]])
    raw = jnp.where(alive, raw, block_count).transpose(0, 2, 1).reshape(2 * slots, n)
    raw = jnp.pad(raw, ((0, 0), (0, LANES - n)), constant_values=block_count)
    near_full = min(block_count, size * slots)
    rungs = [(21, 14), (23, 15), (block_count, near_full)]
    if near_full > 16 or block_count < 24:
        rungs = rungs[-1:]
    hidden_half, plan, *rung_of = prelude(
        n, slots, block_count, rungs, raw.reshape(1, 2 * slots * LANES), features.T, embed_weight
    )
    row_wish, _ = plan_rows(slots)

    def swap(way, *held):
        def at(rung):
            far_cap, near_cap = rungs[rung]
            return lambda *held: exchange(
                n, slots, way, far_cap, near_cap, 2 + way * len(rungs) + rung, *held
            )

        if len(rungs) == 1:
            return at(0)(plan, *held)
        branches = [at(rung) for rung in range(len(rungs))]
        return lax.switch(rung_of[way].reshape(()), branches, plan, *held)

    pair_half = to_half(pair_weight)
    merge_half = to_half(merge_weight)
    head_half = to_half(head_weight)
    got = swap(0, hidden_half.reshape(block_count, block_rows, hidden_width))
    later, got = lax.optimization_barrier((adjacency, got))
    edges_back = lax.all_to_all(later, "nodes", split_axis=0, concat_axis=0, tiled=True)
    label_width = labels.shape[1]
    head_wide = jnp.pad(head_half, ((0, 0), (0, LANES - label_width)))
    part_rows = Summer.padded(n, 4 * hidden_width + LANES, hidden_width)
    grad_self, grad_gathered, part, loss_part = dense(
        min(TILE, row_count),
        PIECES,
        part_rows,
        slots,
        (label_count, raw),
        adjacency,
        got,
        labelled,
        labels,
        hidden_half,
        (pair_half[0], merge_half[0], head_wide),
    )
    back, total = swap(1, grad_gathered.reshape(block_count, block_rows, hidden_width), part)
    def flat(values):
        return values.reshape(-1, hidden_width)

    grad_hidden, pair_next, merge_next, head_next = return_sum(
        row_wish,
        plan.reshape(-1, LANES),
        edges_back,
        back,
        block_count,
        grad_self,
        pair_half[0, 0],
        total,
        (
            (flat(pair_weight), flat(pair_moment), flat(pair_variance)),
            (flat(merge_weight), flat(merge_moment), flat(merge_variance)),
        ),
        (head_weight, head_moment, head_variance),
    )
    pair_next = [values.reshape(pair_weight.shape) for values in pair_next]
    merge_next = [values.reshape(merge_weight.shape) for values in merge_next]
    grad_hidden = grad_hidden.reshape(row_count, hidden_width)
    embed_grad, loss_total = finish(n, features.T, grad_hidden, loss_part, 1)
    embed_next = adam_update(embed_weight, embed_grad, embed_moment, embed_variance)
    return (
        loss_total.reshape(1),
        embed_next[0],
        pair_next[0],
        merge_next[0],
        head_next[0],
        embed_next[1],
        pair_next[1],
        merge_next[1],
        head_next[1],
        embed_next[2],
        pair_next[2],
        merge_next[2],
        head_next[2],
    )


def solution(mesh):
    split = ("nodes",)
    return jax.shard_map(
        shards,
        mesh=mesh,
        in_specs=(
            P("nodes", None),
            P("nodes", None),
            P("nodes"),
            P(),
            P("nodes", None, None),
            P("nodes", None),
            P("nodes", None, None),
            P("nodes", None, None),
        )
        + (P(),) * 12,
        out_specs=(P(),) * 13,
        check_vma=False,
    )
```

```python
import functools

import jax
import jax.numpy as jnp
from jax import lax
from jax.experimental import pallas as pl
from jax.experimental.pallas import tpu as pltpu
from jax.sharding import PartitionSpec as P

norm_eps = 1e-06
learn_rate = 0.03
beta_one = 0.9
beta_two = 0.999
adam_eps = 1e-08
decay_rate = 0.01
adam_step = 10.0

PLANES = 4
KINDS = 4
CHUNKS = 8
PARTS = 4
AHEAD = 3
NEAR_AHEAD = 3
LEAD = 2
LANES = 128
VMEM_MOST = 60 * 2**20
TILE = 1024
PIECES = 2
STAGES = 9
SKEW = 2
SUM_AT = (0, 2, 9, 13, 17, 20, 24, 30, 32)
MESH = pl.DeviceIdType.MESH


def to_half(value):
    return value.astype(jnp.bfloat16)


def mat_product(former, latter):
    return jnp.dot(former, latter, preferred_element_type=jnp.float32)


def left_product(former, latter):
    return lax.dot_general(
        former, latter, (((0,), (0,)), ((), ())), preferred_element_type=jnp.float32
    )


def right_product(former, latter):
    return lax.dot_general(
        former, latter, (((1,), (1,)), ((), ())), preferred_element_type=jnp.float32
    )


def adam_update(weight, grad, first, second):
    first_new = beta_one * first + (1.0 - beta_one) * grad
    second_new = beta_two * second + (1.0 - beta_two) * grad * grad
    first_hat = first_new * (1.0 / (1.0 - beta_one**adam_step))
    second_hat = second_new * (1.0 / (1.0 - beta_two**adam_step))
    weight_new = weight - learn_rate * (
        first_hat / (jnp.sqrt(second_hat) + adam_eps) + decay_rate * weight
    )
    return (weight_new, first_new, second_new)


def place(me, plane_size):
    z = me // plane_size
    spot = me % plane_size
    inner = (z % 2 + z // 2) % 2
    near = z + 1 - 2 * (z % 2)
    far_in = 2 - z // 2
    far_out = 3 * (1 - z // 2)
    return z, spot, inner, near, far_in, far_out


class Summer:
    STEPS = 9

    def __init__(self, n, shape, split_row=None, direct=False):
        self.n, (self.rows, self.width) = n, shape
        self.split_row, self.direct = split_row, direct
        self.size = n // PLANES
        self.chips = self.size // 2
        self.half = self.width // 2
        self.cuts = min(self.half // LANES, self.chips)
        self.cut = self.half // self.cuts
        self.bands = self.chips // self.cuts
        self.band = self.rows // self.bands
        self.shard = self.band // PLANES

    @staticmethod
    def padded(n, rows, width):
        summer = Summer(n, (rows, width))
        unit = summer.bands * PLANES * 16
        return -(-rows // unit) * unit

    def scratch(self):
        f32 = jnp.float32
        return [
            pltpu.VMEM((self.rows, self.half), f32),
            pltpu.VMEM((self.chips - 1, self.band, self.cut), f32),
            pltpu.VMEM(((1 if self.direct else 2) * self.shard, self.cut), f32),
            pltpu.VMEM(((PLANES - 1 if self.direct else 1) * self.shard, self.cut), f32),
            pltpu.SemaphoreType.DMA((8,)),
            pltpu.SemaphoreType.DMA((8,)),
        ]

    def bind(self, part, total, refs):
        self.part, self.total = part, total
        self.from_core, self.from_chip, self.from_pair, self.from_far, self.sent, self.got = refs
        me = lax.axis_index("nodes")
        self.z, spot = me // self.size, me % self.size
        self.chip, self.core = spot // 2, spot % 2
        self.low, self.high = self.z % 2, self.z // 2
        self.mine = pl.ds(pl.multiple_of(self.core * self.half, LANES), self.half)
        self.other = pl.ds(pl.multiple_of((1 - self.core) * self.half, LANES), self.half)
        self.across = self.device(self.z, self.chip, 1 - self.core)
        self.pair = self.device(self.high * 2 + 1 - self.low, self.chip, self.core)
        self.far = self.device((1 - self.high) * 2 + self.low, self.chip, self.core)

    def device(self, z, chip, core):
        return z * self.size + chip * 2 + core

    def column(self, hop):
        return self.device(lax.rem(self.z + hop, PLANES), self.chip, self.core)

    def peers(self):
        found = [self.across, self.pair, self.far]
        if self.direct:
            found = [self.across] + [self.column(hop) for hop in range(1, PLANES)]
        for hop in range(1, self.chips):
            found.append(self.device(self.z, lax.rem(self.chip + hop, self.chips), self.core))
        return found

    def patch(self, chip):
        row = pl.multiple_of((chip // self.cuts) * self.band, 8)
        col = self.core * self.half + (chip % self.cuts) * self.cut
        return row, pl.ds(pl.multiple_of(col, LANES), self.cut)

    def copy(self, hop, src, dst, device):
        pltpu.make_async_remote_copy(
            src_ref=src,
            dst_ref=dst,
            send_sem=self.sent.at[hop],
            recv_sem=self.got.at[hop],
            device_id=(device,),
            device_id_type=MESH,
        ).start()

    @staticmethod
    def settle(sem, held):
        pltpu.make_async_copy(held, held, sem).wait()

    def split(self, values, first_row):
        high = values.astype(self.total.dtype).astype(jnp.float32)
        middle = (values - high).astype(self.total.dtype).astype(jnp.float32)
        at = lax.broadcasted_iota(jnp.int32, values.shape, 0) + first_row - self.split_row
        rest = jnp.where(at == 1, values - high, values - high - middle)
        return jnp.where((at == 1) | (at == 2), rest, values)

    def column_step(self, at, band, cols, plane_shard, amount):
        part, total, shard = self.part, self.total, self.shard
        if at == 2:
            self.settle(self.got.at[1], self.from_chip)
            held = part[band, cols]
            for hop in range(1, self.chips):
                held = held + self.from_chip[hop - 1]
            part[band, cols] = held
            for hop in range(1, PLANES):
                src = part.at[plane_shard(lax.rem(self.z + hop, PLANES)), cols]
                dst = self.from_far.at[pl.ds((hop - 1) * shard, shard)]
                self.copy(3, src, dst, self.column(hop))
        elif at == 3:
            self.settle(self.got.at[3], self.from_far)
            held = part[plane_shard(self.z), cols]
            for hop in range(1, PLANES):
                held = held + self.from_far[pl.ds((hop - 1) * shard, shard), :]
            if self.split_row is not None:
                held = self.split(held, self.patch(self.chip)[0] + self.z * shard)
            total[plane_shard(self.z), cols] = held.astype(total.dtype)
            held = total.at[plane_shard(self.z), cols]
            for hop in range(1, PLANES):
                self.copy(4, held, held, self.column(hop))

    def step(self, at):
        part, total, shard = self.part, self.total, self.shard
        row, cols = self.patch(self.chip)
        band = pl.ds(row, self.band)

        def pairs(low):
            return pl.ds(pl.multiple_of(row + low * 2 * shard, 16), 2 * shard)

        def shards(high):
            return pl.ds(pl.multiple_of(row + (self.low * 2 + high) * shard, 16), shard)

        def amount(*shape):
            return total.at[pl.ds(0, shape[0]), pl.ds(0, shape[1])]

        short = self.band * total.dtype.itemsize // part.dtype.itemsize
        every_chip = self.from_chip.at[:, pl.ds(0, short)]

        def chips(hop):
            chip = lax.rem(self.chip + hop, self.chips)
            return chip, self.device(self.z, chip, self.core)

        def plane_shard(z):
            return pl.ds(pl.multiple_of(row + z * shard, 16), shard)

        if self.direct and 2 <= at <= 5:
            self.column_step(at, band, cols, plane_shard, amount)
        elif at == 0:
            self.copy(0, part.at[:, self.other], self.from_core, self.across)
        elif at == 1:
            self.settle(self.got.at[0], self.from_core)
            part[:, self.mine] += self.from_core[...]
            for hop in range(1, self.chips):
                chip, device = chips(hop)
                there, cut = self.patch(chip)
                src = part.at[pl.ds(there, self.band), cut]
                self.copy(1, src, self.from_chip.at[hop - 1], device)
        elif at == 2:
            self.settle(self.got.at[1], self.from_chip)
            held = part[band, cols]
            for hop in range(1, self.chips):
                held = held + self.from_chip[hop - 1]
            part[band, cols] = held
            self.copy(2, part.at[pairs(1 - self.low), cols], self.from_pair, self.pair)
        elif at == 3:
            self.settle(self.got.at[2], self.from_pair)
            part[pairs(self.low), cols] += self.from_pair[...]
            self.copy(3, part.at[shards(1 - self.high), cols], self.from_far, self.far)
        elif at == 4:
            self.settle(self.got.at[3], self.from_far)
            held = part[shards(self.high), cols] + self.from_far[...]
            if self.split_row is not None:
                held = self.split(held, row + (self.low * 2 + self.high) * shard)
            total[shards(self.high), cols] = held.astype(total.dtype)
            held = total.at[shards(self.high), cols]
            self.copy(4, held, held, self.far)
        elif at == 5:
            self.settle(self.got.at[4], amount(shard, self.cut))
            held = total.at[pairs(self.low), cols]
            self.copy(5, held, held, self.pair)
        elif at == 6:
            if self.direct:
                self.settle(self.got.at[4], amount((PLANES - 1) * shard, self.cut))
            else:
                self.settle(self.got.at[5], amount(2 * shard, self.cut))
            held = total.at[band, cols]
            for hop in range(1, self.chips):
                self.copy(6, held, held, chips(hop)[1])
        elif at == 7:
            self.settle(self.got.at[6], every_chip)
            held = total.at[:, self.mine]
            self.copy(7, held, held, self.across)
        else:
            self.settle(self.got.at[7], amount(self.rows, self.half))
            self.settle(self.sent.at[0], self.from_core)
            self.settle(self.sent.at[1], self.from_chip)
            self.settle(self.sent.at[3], self.from_far)
            if self.direct:
                self.settle(self.sent.at[4], amount((PLANES - 1) * shard, self.cut))
            else:
                self.settle(self.sent.at[2], self.from_pair)
                self.settle(self.sent.at[4], amount(shard, self.cut))
                self.settle(self.sent.at[5], amount(2 * shard, self.cut))
            self.settle(self.sent.at[6], every_chip)
            self.settle(self.sent.at[7], amount(self.rows, self.half))


def finish_kernel(n, tile, rows_there, grads, loss, total, part, rows, held, sem, *refs):
    fetches = [
        pltpu.make_async_copy(grads, held, sem.at[0]),
        pltpu.make_async_copy(rows_there, rows, sem.at[1]),
    ]
    for fetch in fetches:
        fetch.start()
    below = -(-rows.shape[0] // 8) * 8
    summer = Summer(n, part.shape, below, direct=True)
    summer.bind(part, total, refs)
    barrier = pltpu.get_barrier_semaphore()
    peers = summer.peers()
    for peer in peers:
        pl.semaphore_signal(barrier, inc=1, device_id=(peer,), device_id_type=MESH)
    count, depth = rows.shape

    def multiply(cols):
        part[:, cols] = jnp.zeros((part.shape[0], summer.half), jnp.float32)

        def add(at, carry):
            window = pl.ds(pl.multiple_of(at * tile, tile), tile)
            part[:count, cols] += mat_product(rows[:, window], held[window, cols])
            return carry

        lax.fori_loop(0, depth // tile, add, 0)
        part[pl.ds(below, 8), cols] = jnp.broadcast_to(loss[...], (8, summer.half))

    for fetch in fetches:
        fetch.wait()
    multiply(summer.other)
    pl.semaphore_wait(barrier, len(peers))
    summer.step(0)
    multiply(summer.mine)
    for at in range(1, Summer.STEPS):
        summer.step(at)


def finish(n, rows, grads, loss, collective):
    count = -(-rows.shape[0] // 8) * 8
    shape = (Summer.padded(n, count + 8, grads.shape[1]), grads.shape[1])
    vmem = pl.BlockSpec(memory_space=pltpu.VMEM)
    total = pl.pallas_call(
        functools.partial(finish_kernel, n, 1024),
        out_shape=jax.ShapeDtypeStruct(shape, jnp.bfloat16),
        in_specs=[
            pl.BlockSpec(memory_space=pltpu.HBM),
            pl.BlockSpec(memory_space=pltpu.HBM),
            vmem,
        ],
        out_specs=vmem,
        scratch_shapes=[
            pltpu.VMEM(shape, jnp.float32),
            pltpu.VMEM(rows.shape, rows.dtype),
            pltpu.VMEM(grads.shape, grads.dtype),
            pltpu.SemaphoreType.DMA((2,)),
        ]
        + Summer(n, shape, direct=True).scratch(),
        compiler_params=pltpu.CompilerParams(
            collective_id=collective, has_side_effects=True, vmem_limit_bytes=VMEM_MOST
        ),
        name="finish",
    )(rows, grads, loss)
    loss = jnp.sum(total[count : count + 3, 0].astype(jnp.float32))
    return total[: rows.shape[0]].astype(jnp.float32), loss


class Exchange:
    def __init__(self, n, slots, way, far_cap, near_cap, shape, kind):
        self.n, self.slots, self.way = n, slots, way
        self.far_cap, self.near_cap = far_cap, near_cap
        self.size = n // PLANES
        self.blocks, self.depth, self.width = shape
        self.kind = kind
        self.rows = self.depth // CHUNKS
        self.cols = self.width // PARTS
        self.steps = CHUNKS * PARTS
        self.ring = self.steps if self.size <= 8 else 2

    def out_shape(self):
        return jax.ShapeDtypeStruct(
            (CHUNKS, self.size, KINDS, self.slots, self.rows, self.width), self.kind
        )

    def scratch(self):
        def piece(*lead):
            return pltpu.VMEM(lead + (self.rows, self.cols), self.kind)

        steps, ring = self.steps, self.ring
        dma = pltpu.SemaphoreType.DMA
        return (
            [piece(self.near_cap) for _ in range(steps)]
            + [piece(2, self.far_cap) for _ in range(steps)]
            + [piece(steps, self.far_cap), piece(steps, self.near_cap)]
            + [piece(steps, 2, self.near_cap)]
            + [piece(ring, self.size, 2, self.slots) for _ in range(2)]
            + [dma, dma, dma, dma((steps,)), dma((steps,)), dma((2, ring)), dma((CHUNKS,))]
        )

    def bind(self, plan, table, out, refs):
        self.plan, self.table, self.out = plan.at[self.way], table, out
        steps = self.steps
        self.near_got, self.far_got = refs[:steps], refs[steps : 2 * steps]
        (
            self.far_stage,
            self.near_stage,
            self.pass_stage,
            first_stage,
            second_stage,
            self.far_sent,
            self.near_sent,
            self.pass_sent,
            self.near_recv,
            self.far_recv,
            self.serve_sent,
            self.serve_recv,
        ) = refs[2 * steps :]
        self.serve_stage = (first_stage, second_stage)
        me = lax.axis_index("nodes")
        self.z, self.spot, self.inner, near, far_in, far_out = place(me, self.size)
        self.near_dev = near * self.size + self.spot
        self.relay_dev = far_in * self.size + self.spot
        self.outer_dev = far_out * self.size + self.spot

    def greet(self, column=False):
        barrier = pltpu.get_barrier_semaphore()

        def hello(device):
            pl.semaphore_signal(barrier, inc=1, device_id=(device,), device_id_type=MESH)

        def in_plane(step, carry):
            hello(self.z * self.size + lax.rem(self.spot + step, self.size))
            return carry

        lax.fori_loop(1, self.size, in_plane, 0)
        hello(self.near_dev)
        if column:
            hello(((1 - self.z // 2) * 2 + self.z % 2) * self.size + self.spot)

            @pl.when(self.inner == 1)
            def _():
                hello(self.relay_dev)

            pl.semaphore_wait(barrier, self.size + 1 + self.inner)
            return

        @pl.when(self.inner == 1)
        def _():
            hello(self.relay_dev)
            hello(self.outer_dev)

        pl.semaphore_wait(barrier, self.size + 1)

    def window(self, step):
        return pl.ds((step // PARTS) * self.rows, self.rows), pl.ds(
            (step % PARTS) * self.cols, self.cols
        )

    def remote(self, src, dst, sent, got, device):
        return pltpu.make_async_remote_copy(
            src_ref=src,
            dst_ref=dst,
            send_sem=sent,
            recv_sem=got,
            device_id=(device,),
            device_id_type=MESH,
        )

    @staticmethod
    def settle(sem, held):
        pltpu.make_async_copy(held, held, sem).wait()

    def launch_far(self, step):
        rows, cols = self.window(step)
        plan, table, stage = self.plan, self.table, self.far_stage.at[step]

        def fill(at, carry):
            stage[at] = table[plan[ROW_FAR, at], rows, cols]
            return carry

        lax.fori_loop(0, self.far_cap, fill, 0)
        self.remote(
            stage,
            self.far_got[step].at[1 - self.inner],
            self.far_sent,
            self.far_recv.at[step],
            self.relay_dev,
        ).start()

    def launch_near(self, step):
        rows, cols = self.window(step)
        plan, table, stage = self.plan, self.table, self.near_stage.at[step]

        def fill(at, carry):
            stage[at] = table[plan[ROW_NEAR, at], rows, cols]
            return carry

        lax.fori_loop(0, self.near_cap, fill, 0)
        self.remote(
            stage, self.near_got[step], self.near_sent, self.near_recv.at[step], self.near_dev
        ).start()

    def relay(self, step):
        plan, got, stage = self.plan, self.far_got[step], self.pass_stage.at[step]
        part = got.at[:, pl.ds(0, self.near_cap)]

        @pl.when(self.inner == 1)
        def _():
            self.settle(self.far_recv.at[step], got)

            def fill(at, carry):
                for lane in range(2):
                    stage[lane, at] = got[lane, plan[ROW_PASS + lane, at]]
                return carry

            lax.fori_loop(0, self.near_cap, fill, 0)
            self.remote(
                stage, part, self.pass_sent, self.far_recv.at[step], self.near_dev
            ).start()

        @pl.when(self.inner == 0)
        def _():
            self.settle(self.far_recv.at[step], part)

    def serve(self, step, pair):
        rows, cols = self.window(step)
        plan, table, slots, size = self.plan, self.table, self.slots, self.size
        chunk, slot_at = step // PARTS, step % self.ring
        if pair == 0:
            self.settle(self.near_recv.at[step], self.near_got[step])
        if step >= self.ring:
            self.drain(step - self.ring, pair)
        stage = self.serve_stage[pair].at[slot_at]

        def fill(peer, carry):
            taker = self.z * size + peer
            for slot in range(slots):
                first = plan[ROW_SERVE + 2 * pair * slots + slot, taker]
                second = plan[ROW_SERVE + (2 * pair + 1) * slots + slot, taker]
                if pair == 0:
                    stage[peer, 0, slot] = table[first, rows, cols]
                    stage[peer, 1, slot] = self.near_got[step][second]
                else:
                    stage[peer, 0, slot] = self.far_got[step][0, first]
                    stage[peer, 1, slot] = self.far_got[step][1, second]
            return carry

        lax.fori_loop(0, size, fill, 0)
        there = self.out.at[chunk, self.spot, pl.ds(2 * pair, 2), :, :, cols]
        pltpu.make_async_copy(stage.at[self.spot], there, self.serve_recv.at[chunk]).start()

        def send(hop, carry):
            peer = lax.rem(self.spot + hop, size)
            self.remote(
                stage.at[peer],
                there,
                self.serve_sent.at[pair, slot_at],
                self.serve_recv.at[chunk],
                self.z * size + peer,
            ).start()
            return carry

        lax.fori_loop(1, size, send, 0)

    def drain(self, step, pair):
        slot_at = step % self.ring
        held = self.serve_stage[pair].at[slot_at, pl.ds(0, self.size - 1)]
        self.settle(self.serve_sent.at[pair, slot_at], held)

    def run(self, side=None):
        steps = self.steps
        for step in range(min(AHEAD, steps)):
            self.launch_far(step)
            self.launch_near(step)

        @pl.when(self.inner == 1)
        def _():
            for step in range(AHEAD, min(NEAR_AHEAD, steps)):
                self.launch_near(step)

        for step in range(min(LEAD, steps)):
            self.serve(step, 0)
        for step in range(steps):
            if step + AHEAD < steps:
                self.launch_far(step + AHEAD)
                if NEAR_AHEAD == AHEAD:
                    self.launch_near(step + AHEAD)
                else:

                    @pl.when(self.inner == 0)
                    def _():
                        self.launch_near(step + AHEAD)

            if NEAR_AHEAD > AHEAD and step + NEAR_AHEAD < steps:

                @pl.when(self.inner == 1)
                def _():
                    self.launch_near(step + NEAR_AHEAD)

            self.relay(step)
            self.serve(step, 1)
            if step + LEAD < steps:
                self.serve(step + LEAD, 0)
            if side is not None:
                side(step)
        if side is not None:
            side(steps)
        for chunk in range(CHUNKS):
            self.settle(self.serve_recv.at[chunk], self.out.at[chunk])
        def drain(at, carry):
            for pair in range(2):
                self.drain(at, pair)
            return carry

        lax.fori_loop(0, self.ring, drain, 0)
        self.settle(self.far_sent, self.far_stage)
        self.settle(self.near_sent, self.near_stage)

        @pl.when(self.inner == 1)
        def _():
            self.settle(self.pass_sent, self.pass_stage)


def exchange_kernel(moves, plan, table, out, held_table, table_sem, *refs):
    moves.bind(plan, held_table, out, refs)
    fetch = pltpu.make_async_copy(table, held_table, table_sem)
    fetch.start()
    moves.greet()
    fetch.wait()
    moves.run()


def exchange_sum_kernel(
    moves, summer, plan, table, part, out, total, held_table, table_sem, held, sem, *refs
):
    moves.bind(plan, held_table, out, refs[6:])
    fetch_table = pltpu.make_async_copy(table, held_table, table_sem)
    fetch_table.start()
    summer.bind(held, total, refs[:6])
    fetch = pltpu.make_async_copy(part, held, sem)
    fetch.start()
    moves.greet(column=True)
    fetch_table.wait()

    def side(step):
        if step == 0:
            fetch.wait()
        if step in SUM_AT:
            summer.step(SUM_AT.index(step))

    moves.run(side)


def exchange(n, slots, way, far_cap, near_cap, collective, plan, table, part=None):
    moves = Exchange(n, slots, way, far_cap, near_cap, table.shape, table.dtype)
    hbm = pl.BlockSpec(memory_space=pl.ANY)
    vmem = pl.BlockSpec(memory_space=pltpu.VMEM)
    in_specs = [pl.BlockSpec(memory_space=pltpu.SMEM), hbm]
    table_held = [pltpu.VMEM(table.shape, table.dtype), pltpu.SemaphoreType.DMA]
    params = pltpu.CompilerParams(
        collective_id=collective, has_side_effects=True, vmem_limit_bytes=VMEM_MOST
    )
    if part is None:
        return pl.pallas_call(
            functools.partial(exchange_kernel, moves),
            out_shape=moves.out_shape(),
            in_specs=in_specs,
            out_specs=hbm,
            scratch_shapes=table_held + moves.scratch(),
            compiler_params=params,
            name="exchange",
        )(plan, table)
    summer = Summer(n, part.shape)
    return pl.pallas_call(
        functools.partial(exchange_sum_kernel, moves, summer),
        out_shape=(moves.out_shape(), jax.ShapeDtypeStruct(part.shape, jnp.bfloat16)),
        in_specs=in_specs + [hbm],
        out_specs=(hbm, vmem),
        scratch_shapes=table_held
        + [pltpu.VMEM(part.shape, jnp.float32), pltpu.SemaphoreType.DMA]
        + summer.scratch()
        + moves.scratch(),
        compiler_params=params,
        name="exchange_sum",
    )(plan, table, part)


def add_products(flip, slots, first_row, sinks, weights, got, total, at, size):
    z, _, _, near, far_in, far_out = place(lax.axis_index("nodes"), size)
    depth, width = total.shape[1:]
    dims = (((0,), (0,)), ((), ())) if flip else (((1,), (0,)), ((), ()))
    for kind, owner_z in enumerate((z, near, far_in, far_out)):
        for slot in range(slots):
            sink = sinks[first_row + slot, owner_z * size + at]
            rows = got[:, 0, kind, slot].reshape(depth, width)
            total[sink] += lax.dot_general(
                weights[owner_z, 0, slot], rows, dims, preferred_element_type=jnp.float32
            )


def return_sum_kernel(slots, first_row, *refs):
    sinks, weights, got, own, mixer = refs[:5]
    states, head_state, out = refs[5:13], refs[13:17], refs[17]
    updates, head_update, total, mixer_half = refs[18:24], refs[24:27], refs[27], refs[28]
    at = pl.program_id(0)
    blocks, depth, width = out.shape

    @pl.when(at == 0)
    def _():
        total[...] = jnp.zeros_like(total)
        mixer_half[...] = to_half(mixer[0])
        label_width = head_state[0].shape[1]
        head_grad = head_state[1][...].astype(jnp.float32).T[:, :label_width]
        fresh = adam_update(head_state[0][...], head_grad, head_state[2][...], head_state[3][...])
        for to, values in zip(head_update, fresh):
            to[...] = values

    span = own.shape[0] // depth
    base = right_product(own[...], mixer_half[...]).reshape(span, depth, width)
    total[pl.ds(at * span, span)] += base
    for state, update in ((states[:4], updates[:3]), (states[4:], updates[3:])):
        grad = state[1][...].astype(jnp.float32)
        fresh = adam_update(state[0][...], grad, state[2][...], state[3][...])
        for to, values in zip(update, fresh):
            to[...] = values
    size = pl.num_programs(0)
    add_products(True, slots, first_row, sinks, weights, got, total, at, size)

    @pl.when(at == pl.num_programs(0) - 1)
    def _():
        out[...] = to_half(total[:blocks])


def block_specs(weights, got):
    chunks, size, kinds, slots, rows, width = got.shape
    depth = chunks * rows
    edges = weights.reshape(PLANES, size, slots, depth, depth)

    def clip(at):
        return jnp.minimum(at, size - 1)

    specs = [
        pl.BlockSpec((PLANES, 1, slots, depth, depth), lambda at, *_: (0, clip(at), 0, 0, 0)),
        pl.BlockSpec(
            (chunks, 1, kinds, slots, rows, width), lambda at, *_: (0, clip(at), 0, 0, 0, 0)
        ),
    ]
    return edges, specs


def return_sum(first_row, sinks, weights, got, blocks, own, mixer, grads, groups, head):
    chunks, size, _, slots, rows, width = got.shape
    depth = chunks * rows
    edges, specs = block_specs(weights, got)
    tile = blocks * depth // size
    specs = specs + [
        pl.BlockSpec((tile, width), lambda at, sinks: (at, 0)),
        pl.BlockSpec((1, width, width), lambda at, sinks: (0, 0, 0)),
    ]
    states, shapes, out_specs = [], [], []
    for place_at, (weight, first, second) in enumerate(groups):
        part = weight.shape[0] // size
        spec = pl.BlockSpec((part, width), lambda at, sinks: (at, 0))
        moved = pl.BlockSpec((part, width), lambda at, sinks, p=place_at: (at + p * size, 0))
        states += [weight, grads, first, second]
        specs = specs + [spec, moved, spec, spec]
        shapes += [jax.ShapeDtypeStruct(weight.shape, jnp.float32)] * 3
        out_specs += [spec] * 3
    head_at = 2 * groups[0][0].shape[0] // LANES
    still = pl.BlockSpec(head[0].shape, lambda at, sinks: (0, 0))
    states += [head[0], grads, head[1], head[2]]
    specs = specs + [still, pl.BlockSpec((LANES, width), lambda at, sinks: (head_at, 0)), still, still]
    shapes += [jax.ShapeDtypeStruct(head[0].shape, jnp.float32)] * 3
    out_specs += [still] * 3
    found = pl.pallas_call(
        functools.partial(return_sum_kernel, slots, first_row),
        out_shape=[jax.ShapeDtypeStruct((blocks, depth, width), jnp.bfloat16)] + shapes,
        grid_spec=pltpu.PrefetchScalarGridSpec(
            num_scalar_prefetch=1,
            grid=(size,),
            in_specs=specs,
            out_specs=[pl.BlockSpec((blocks, depth, width), lambda at, sinks: (0, 0, 0))]
            + out_specs,
            scratch_shapes=[
                pltpu.VMEM((blocks + 1, depth, width), jnp.float32),
                pltpu.VMEM((width, width), jnp.bfloat16),
            ],
        ),
        compiler_params=pltpu.CompilerParams(vmem_limit_bytes=48 * 2**20),
        name="return_sum",
    )(sinks, edges, got, own, mixer, *states)
    return found[0], found[1:4], found[4:7], found[7:10]


ROW_FAR, ROW_NEAR, ROW_PASS, ROW_SERVE = 0, 1, 2, 4


def plan_rows(slots):
    wishes = ROW_SERVE + KINDS * slots
    return wishes, -(-(wishes + slots) // 8) * 8


def column(values, lane):
    lanes = lax.broadcasted_iota(jnp.int32, values.shape, 1)
    return jnp.sum(jnp.where(lanes == lane, values, 0.0), axis=1, keepdims=True)


def lay_plan(n, slots, blocks, rungs, way, wishes_of, plan, chosen, present):
    size = n // PLANES
    me = lax.axis_index("nodes")
    z, spot, inner, near, far_in, far_out = place(me, size)
    half = z // 2
    row_wish, _ = plan_rows(slots)

    taker = lax.broadcasted_iota(jnp.int32, (LANES, LANES), 0)
    group = lax.broadcasted_iota(jnp.int32, (LANES, LANES), 1)
    plane_of = taker // size
    member = (taker < n) & ((plane_of == group) | (plane_of // 2 + PLANES == group))
    member = jnp.where(member, 1.0, 0.0).astype(jnp.bfloat16)
    hits = jnp.zeros((n * blocks, LANES), jnp.float32)
    for slot in range(slots):
        wish = wishes_of[slot][...]
        ids = lax.broadcasted_iota(jnp.int32, (n, blocks, LANES), 1)
        hot = jnp.where(wish[:, None, :] == ids, 1.0, 0.0).astype(jnp.bfloat16)
        hits = hits + mat_product(hot.reshape(n * blocks, LANES), member)
    here = jnp.where(hits > 0.0, 1.0, 0.0)
    present[...] = here
    counts = jnp.sum(here.reshape(n, blocks, LANES), axis=1)
    owner_plane = lax.broadcasted_iota(jnp.int32, (n, LANES), 0) // size
    lane = lax.broadcasted_iota(jnp.int32, (n, LANES), 1)
    is_near = (lane < PLANES) & (lane != owner_plane)
    is_far = (lane >= PLANES) & (lane < PLANES + 2) & (lane - PLANES != owner_plane // 2)
    near_most = jnp.max(jnp.where(is_near, counts, 0.0), axis=(0, 1), keepdims=True)
    far_most = jnp.max(jnp.where(is_far, counts, 0.0), axis=(0, 1), keepdims=True)
    rung = jnp.zeros((1, 1), jnp.float32)
    for far_cap, near_cap in rungs[:-1]:
        over = (far_most > float(far_cap)) | (near_most > float(near_cap))
        rung = rung + jnp.where(over, 1.0, 0.0)

    def put(row, values):
        plan[way, pl.ds(row, 1), :] = values.astype(jnp.int32)

    chosen[...] = len(rungs) - 1 - rung.astype(jnp.int32)
    block_id = lax.broadcasted_iota(jnp.int32, (blocks, LANES), 0)
    block_lane = lax.broadcasted_iota(jnp.int32, (blocks, LANES), 1)
    ids = block_id.astype(jnp.float32)
    below = lax.broadcasted_iota(jnp.int32, (blocks, blocks), 0) > lax.broadcasted_iota(
        jnp.int32, (blocks, blocks), 1
    )
    below = jnp.where(below, 1.0, 0.0).astype(jnp.bfloat16)

    def listed(chosen, pos, values):
        at = (chosen > 0.0) & (pos.astype(jnp.int32) == block_lane)
        return jnp.sum(jnp.where(at, values, 0.0), axis=0, keepdims=True)

    for kind, owner_z in enumerate((z, near, far_in, far_out)):
        owner = owner_z * size + spot
        mine = present[pl.ds(pl.multiple_of(owner * blocks, 8), blocks), :]
        rank = mat_product(below, mine.astype(jnp.bfloat16))
        if kind == 0:
            where_held = ids
            far = PLANES + 1 - half
            put(ROW_FAR, listed(column(mine, far), column(rank, far), ids))
            put(ROW_NEAR, listed(column(mine, near), column(rank, near), ids))
        elif kind == 1:
            where_held = column(rank, z)
        else:
            where_held = column(rank, z + inner * (PLANES + half - z))
            edge = 3 * half
            put(
                ROW_PASS + kind - 2,
                listed(column(mine, edge), column(rank, edge), column(rank, PLANES + half)),
            )
        for slot in range(slots):
            wish = wishes_of[slot][pl.ds(owner, 1), :]
            held = jnp.where(wish == block_id, where_held, 0.0)
            put(ROW_SERVE + kind * slots + slot, jnp.sum(held, axis=0, keepdims=True))
            if kind == 0:
                put(row_wish + slot, wish)


def prelude_kernel(n, slots, blocks, rungs, tile, *refs):
    need, target, alive, rows, weight, hidden, plan = refs[:7]
    chosen, sunk, mine, taken = refs[7:9], refs[9], refs[10], refs[11]
    wishes = refs[12 : 12 + 2 * slots]
    present, held, held_weight, row_sem, weight_sem, send_sem, recv_sem = refs[12 + 2 * slots :]
    tiles = rows.shape[1] // tile

    def window(at):
        return pl.ds(pl.multiple_of(at * tile, tile), tile)

    def fetch(at):
        part = window(at)
        return pltpu.make_async_copy(rows.at[:, part], held.at[:, part], row_sem.at[at])

    fetch_weight = pltpu.make_async_copy(weight, held_weight, weight_sem)
    fetch_weight.start()
    for at in range(tiles):
        fetch(at).start()
    me = lax.axis_index("nodes")
    barrier = pltpu.get_barrier_semaphore()

    def greet(step, carry):
        pl.semaphore_signal(
            barrier, inc=1, device_id=(lax.rem(me + step, n),), device_id_type=MESH
        )
        return carry

    lax.fori_loop(1, n, greet, 0)
    mine[...] = jnp.full(mine.shape, blocks, jnp.int32)
    sunk[...] = jnp.full(sunk.shape, blocks, jnp.int32)
    for slot in range(slots):
        live = slot < alive[...]
        sunk_row = jnp.where(live, target[pl.ds(slot, 1), :], blocks)
        mine[:, pl.ds(slot * LANES, n)] = jnp.where(live, need[pl.ds(slot, 1), :], blocks)
        mine[:, pl.ds((slots + slot) * LANES, n)] = sunk_row
        sunk[pl.ds(slot, 1), pl.ds(0, n)] = sunk_row
    taken[me] = mine[...]
    fetch_weight.wait()
    half_weight = to_half(held_weight[...])

    def project(at):
        fetch(at).wait()
        hidden[window(at), :] = to_half(left_product(held[:, window(at)], half_weight))

    for at in range(tiles // 2):
        project(at)
    pl.semaphore_wait(barrier, n - 1)

    def send(step, carry):
        pltpu.make_async_remote_copy(
            src_ref=mine,
            dst_ref=taken.at[me],
            send_sem=send_sem,
            recv_sem=recv_sem,
            device_id=(lax.rem(me + step, n),),
            device_id_type=MESH,
        ).start()
        return carry

    lax.fori_loop(1, n, send, 0)
    for at in range(tiles // 2, tiles):
        project(at)
    others = taken.at[pl.ds(0, n - 1)]
    pltpu.make_async_copy(others, others, recv_sem).wait()
    pltpu.make_async_copy(others, others, send_sem).wait()

    every = taken[...].reshape(n, 2 * slots * LANES)
    unit = lax.broadcasted_iota(jnp.int32, (n, LANES), 0) == lax.broadcasted_iota(
        jnp.int32, (n, LANES), 1
    )
    unit = jnp.where(unit, 1.0, 0.0).astype(jnp.bfloat16)
    for slot in range(slots):
        part = every[:, slot * LANES : (slot + 1) * LANES]
        turned = left_product(part.astype(jnp.float32).astype(jnp.bfloat16), unit)
        wishes[slot][...] = turned[:n].astype(jnp.int32)
        wishes[slots + slot][...] = every[:, (slots + slot) * LANES : (slots + slot + 1) * LANES]
    for way in range(2):
        lay_plan(
            n,
            slots,
            blocks,
            rungs,
            way,
            wishes[way * slots : (way + 1) * slots],
            plan,
            chosen[way],
            present,
        )


def prelude(n, slots, blocks, rungs, need, target, alive, rows, weight):
    count, width = rows.shape[1], weight.shape[1]
    vmem = pl.BlockSpec(memory_space=pltpu.VMEM)
    plan_shape = (2, plan_rows(slots)[1], LANES)
    return pl.pallas_call(
        functools.partial(prelude_kernel, n, slots, blocks, rungs, 512),
        out_shape=(
            jax.ShapeDtypeStruct((count, width), jnp.bfloat16),
            jax.ShapeDtypeStruct(plan_shape, jnp.int32),
            jax.ShapeDtypeStruct((1, 1), jnp.int32),
            jax.ShapeDtypeStruct((1, 1), jnp.int32),
            jax.ShapeDtypeStruct((8, LANES), jnp.int32),
        ),
        in_specs=[vmem, vmem, vmem] + [pl.BlockSpec(memory_space=pltpu.HBM)] * 2,
        out_specs=(vmem,) * 5,
        scratch_shapes=[
            pltpu.VMEM((1, 2 * slots * LANES), jnp.int32),
            pltpu.VMEM((n, 1, 2 * slots * LANES), jnp.int32),
        ]
        + [pltpu.VMEM((n, LANES), jnp.int32) for _ in range(2 * slots)]
        + [
            pltpu.VMEM((n * blocks, LANES), jnp.float32),
            pltpu.VMEM(rows.shape, rows.dtype),
            pltpu.VMEM(weight.shape, weight.dtype),
            pltpu.SemaphoreType.DMA((count // 512,)),
            pltpu.SemaphoreType.DMA,
            pltpu.SemaphoreType.DMA,
            pltpu.SemaphoreType.DMA,
        ],
        compiler_params=pltpu.CompilerParams(
            collective_id=0, has_side_effects=True, vmem_limit_bytes=VMEM_MOST
        ),
        name="prelude",
    )(need, target, alive, rows, weight)


def sigmoid(values):
    return 1.0 / (1.0 + jnp.exp(-values))


def dense_kernel(label_width, pieces, slots, first_row, count, sinks, edges, got, *refs):
    marks, truth, own = refs[:3]
    grad_own, grad_taken, part, loss, total = refs[6:11]
    pair, merge, head = refs[11:]
    at = pl.program_id(0)
    gathers = pl.num_programs(0) - total.shape[0] * total.shape[1] // own.shape[0]

    @pl.when(at == 0)
    def _():
        total[...] = jnp.zeros_like(total)
        part[...] = jnp.zeros_like(part)
        loss[...] = jnp.zeros_like(loss)
        for to, weight in zip((pair, merge), refs[3:5]):
            to[...] = to_half(weight[...])
        head[...] = to_half(jnp.pad(refs[5][...], ((0, 0), (0, LANES - label_width))))

    @pl.when(at < gathers)
    def _():
        add_products(False, slots, first_row, sinks, edges, got, total, at, gathers)

    @pl.when(at >= gathers)
    def _():
        span = own.shape[0] // total.shape[1]
        taken = total.at[pl.ds((at - gathers) * span, span)]
        dense_tile(
            label_width,
            pieces,
            (count, marks, truth, own, taken, pair, merge, head),
            (grad_own, grad_taken, part, loss),
        )


def dense_tile(label_width, pieces, given, made):
    count, marks, truth, own, taken, pair, merge, head = given
    grad_own, grad_taken, part, loss = made
    width = own.shape[1]
    tile = own.shape[0] // pieces
    span = taken.shape[0] // pieces
    denom = count[0].astype(jnp.float32) * float(label_width)

    def stages(piece):
        rows = pl.ds(piece * tile, tile)
        hidden = own[rows, :]
        gathered = to_half(taken[pl.ds(piece * span, span)]).reshape(tile, width)
        self_part = to_half(mat_product(hidden, pair[0]))
        neigh_part = to_half(mat_product(gathered, pair[1]))
        yield
        linear = mat_product(self_part, merge[:width]) + mat_product(neigh_part, merge[width:])
        yield
        sig = sigmoid(linear)
        active = linear * sig
        scale = lax.rsqrt(jnp.sum(active * active, axis=1, keepdims=True) + norm_eps)
        output = active * scale
        final = to_half(output)
        yield
        logits = mat_product(final, head[...])
        yield
        labels = truth[rows, :].astype(jnp.float32)
        labels = jnp.pad(labels, ((0, 0), (0, LANES - label_width)))
        marked = marks[0, :, rows].astype(jnp.float32)
        marked = jnp.broadcast_to(marked, (LANES, tile)).T
        column_id = lax.broadcasted_iota(jnp.int32, (tile, LANES), 1)
        marked = jnp.where(column_id < label_width, marked, 0.0)
        decay = jnp.exp(-jnp.abs(logits))
        entry = jnp.maximum(logits, 0.0) - logits * labels + jnp.log1p(decay)
        loss[...] += jnp.sum(entry * marked, axis=(0, 1), keepdims=True) / denom
        grad_logits = to_half((sigmoid(logits) - labels) * marked / denom)
        yield
        part[pl.ds(4 * width, LANES), :] += left_product(grad_logits, final)
        grad_out = right_product(grad_logits, head[...])
        yield
        along = jnp.sum(grad_out * output, axis=1, keepdims=True)
        grad_active = scale * (grad_out - output * along)
        grad_linear = to_half(grad_active * sig * (1.0 + linear * (1.0 - sig)))
        yield
        part[pl.ds(2 * width, width), :] += left_product(self_part, grad_linear)
        part[pl.ds(3 * width, width), :] += left_product(neigh_part, grad_linear)
        grad_self = to_half(right_product(grad_linear, merge[:width]))
        grad_neigh = to_half(right_product(grad_linear, merge[width:]))
        yield
        grad_own[rows, :] = grad_self
        part[pl.ds(0, width), :] += left_product(hidden, grad_self)
        part[pl.ds(width, width), :] += left_product(gathered, grad_neigh)
        grad_taken[rows, :] = to_half(right_product(grad_neigh, pair[1]))
        yield

    running = [stages(piece) for piece in range(pieces)]
    for turn in range(STAGES + SKEW * (pieces - 1)):
        for piece in range(pieces):
            if 0 <= turn - SKEW * piece < STAGES:
                next(running[piece])


def dense(tile, pieces, part_rows, first_row, scalars, edges, got, marks, truth, own, weights):
    rows, width = own.shape
    label_width = truth.shape[1]
    size, slots = got.shape[1], got.shape[3]
    edges, specs = block_specs(edges, got)
    depth = edges.shape[-1]

    def later(at):
        return jnp.maximum(at - size, 0)

    by_rows = pl.BlockSpec((tile, width), lambda at, *_: (later(at), 0))

    def whole(values):
        return pl.BlockSpec(
            values.shape, lambda at, *_: (0,) * values.ndim, pipeline_mode=pl.Buffered(1)
        )

    return pl.pallas_call(
        functools.partial(dense_kernel, label_width, pieces, slots, first_row),
        out_shape=(
            jax.ShapeDtypeStruct((rows, width), jnp.bfloat16),
            jax.ShapeDtypeStruct((rows, width), jnp.bfloat16),
            jax.ShapeDtypeStruct((part_rows, width), jnp.float32),
            jax.ShapeDtypeStruct((1, 1), jnp.float32),
        ),
        grid_spec=pltpu.PrefetchScalarGridSpec(
            num_scalar_prefetch=2,
            grid=(size + rows // tile,),
            in_specs=specs
            + [
                pl.BlockSpec((1, 1, tile), lambda at, *_: (later(at), 0, 0)),
                pl.BlockSpec((tile, label_width), lambda at, *_: (later(at), 0)),
                by_rows,
            ]
            + [whole(values) for values in weights],
            out_specs=(
                by_rows,
                by_rows,
                pl.BlockSpec((part_rows, width), lambda at, *_: (0, 0)),
                pl.BlockSpec((1, 1), lambda at, *_: (0, 0)),
            ),
            scratch_shapes=[pltpu.VMEM((rows // depth + 1, depth, width), jnp.float32)]
            + [pltpu.VMEM(values.shape, jnp.bfloat16) for values in weights[:2]]
            + [pltpu.VMEM((width, LANES), jnp.bfloat16)],
        ),
        compiler_params=pltpu.CompilerParams(vmem_limit_bytes=VMEM_MOST),
        name="dense",
    )(*scalars, edges, got, marks.reshape(rows // tile, 1, tile), truth, own, *weights)


def shards(
    features,
    labels,
    labelled,
    label_count,
    need_blocks,
    need_count,
    target_block,
    adjacency,
    embed_weight,
    pair_weight,
    merge_weight,
    head_weight,
    embed_moment,
    pair_moment,
    merge_moment,
    head_moment,
    embed_variance,
    pair_variance,
    merge_variance,
    head_variance,
):
    row_count = features.shape[0]
    hidden_width = embed_weight.shape[1]
    block_rows = adjacency.shape[1]
    slots = need_blocks.shape[2]
    n = lax.axis_size("nodes")
    size = n // PLANES
    block_count = row_count // block_rows
    near_full = min(block_count, size * slots)
    rungs = [(22, 15), (24, 16), (block_count, near_full)]
    if near_full > 16 or block_count < 24:
        rungs = rungs[-1:]
    hidden_half, plan, *rung_of, sunk = prelude(
        n,
        slots,
        block_count,
        rungs,
        need_blocks[0].T,
        target_block[0].T,
        need_count,
        features.T,
        embed_weight,
    )
    row_wish, _ = plan_rows(slots)

    def swap(way, *held):
        def at(rung):
            far_cap, near_cap = rungs[rung]
            return lambda *held: exchange(
                n, slots, way, far_cap, near_cap, 2 + way * len(rungs) + rung, *held
            )

        if len(rungs) == 1:
            return at(0)(plan, *held)
        branches = [at(rung) for rung in reversed(range(len(rungs)))]
        return lax.switch(rung_of[way].reshape(()), branches, plan, *held)

    got = swap(0, hidden_half.reshape(block_count, block_rows, hidden_width))
    later, got = lax.optimization_barrier((adjacency, got))
    edges_back = lax.all_to_all(later, "nodes", split_axis=0, concat_axis=0, tiled=True)
    label_width = labels.shape[1]
    part_rows = Summer.padded(n, 4 * hidden_width + LANES, hidden_width)
    grad_self, grad_gathered, part, loss_part = dense(
        min(TILE, row_count),
        PIECES,
        part_rows,
        0,
        (label_count, sunk),
        adjacency,
        got,
        labelled,
        labels,
        hidden_half,
        (pair_weight[0], merge_weight[0], head_weight),
    )
    back, total = swap(1, grad_gathered.reshape(block_count, block_rows, hidden_width), part)
    def flat(values):
        return values.reshape(-1, hidden_width)

    grad_hidden, pair_next, merge_next, head_next = return_sum(
        row_wish,
        plan.reshape(-1, LANES),
        edges_back,
        back,
        block_count,
        grad_self,
        pair_weight[0],
        total,
        (
            (flat(pair_weight), flat(pair_moment), flat(pair_variance)),
            (flat(merge_weight), flat(merge_moment), flat(merge_variance)),
        ),
        (head_weight, head_moment, head_variance),
    )
    pair_next = [values.reshape(pair_weight.shape) for values in pair_next]
    merge_next = [values.reshape(merge_weight.shape) for values in merge_next]
    grad_hidden = grad_hidden.reshape(row_count, hidden_width)
    embed_grad, loss_total = finish(n, features.T, grad_hidden, loss_part, 1)
    embed_next = adam_update(embed_weight, embed_grad, embed_moment, embed_variance)
    return (
        loss_total.reshape(1),
        embed_next[0],
        pair_next[0],
        merge_next[0],
        head_next[0],
        embed_next[1],
        pair_next[1],
        merge_next[1],
        head_next[1],
        embed_next[2],
        pair_next[2],
        merge_next[2],
        head_next[2],
    )


def solution(mesh):
    split = ("nodes",)
    return jax.shard_map(
        shards,
        mesh=mesh,
        in_specs=(
            P("nodes", None),
            P("nodes", None),
            P("nodes"),
            P(),
            P("nodes", None, None),
            P("nodes", None),
            P("nodes", None, None),
            P("nodes", None, None),
        )
        + (P(),) * 12,
        out_specs=(P(),) * 13,
        check_vma=False,
    )
```

```python
import functools

import jax
import jax.numpy as jnp
from jax import lax
from jax.experimental import pallas as pl
from jax.experimental.pallas import tpu as pltpu
from jax.sharding import PartitionSpec as P

norm_eps = 1e-06
learn_rate = 0.03
beta_one = 0.9
beta_two = 0.999
adam_eps = 1e-08
decay_rate = 0.01
adam_step = 10.0

PLANES = 4
KINDS = 4
CHUNKS = 8
PARTS = 4
AHEAD = 4
NEAR_AHEAD = 4
LEAD = 2
LANES = 128
VMEM_MOST = 60 * 2**20
TILE = 1024
PIECES = 2
STAGES = 9
SKEW = 2
SUM_AT = (0, 2, 8, 11, 14, 17, 20, 26, 32)
MESH = pl.DeviceIdType.MESH


def to_half(value):
    return value.astype(jnp.bfloat16)


def mat_product(former, latter):
    return jnp.dot(former, latter, preferred_element_type=jnp.float32)


def left_product(former, latter):
    return lax.dot_general(
        former, latter, (((0,), (0,)), ((), ())), preferred_element_type=jnp.float32
    )


def right_product(former, latter):
    return lax.dot_general(
        former, latter, (((1,), (1,)), ((), ())), preferred_element_type=jnp.float32
    )


def adam_update(weight, grad, first, second):
    first_new = beta_one * first + (1.0 - beta_one) * grad
    second_new = beta_two * second + (1.0 - beta_two) * grad * grad
    first_hat = first_new * (1.0 / (1.0 - beta_one**adam_step))
    second_hat = second_new * (1.0 / (1.0 - beta_two**adam_step))
    weight_new = weight - learn_rate * (
        first_hat / (jnp.sqrt(second_hat) + adam_eps) + decay_rate * weight
    )
    return (weight_new, first_new, second_new)


def place(me, plane_size):
    z = me // plane_size
    spot = me % plane_size
    inner = (z % 2 + z // 2) % 2
    near = z + 1 - 2 * (z % 2)
    far_in = 2 - z // 2
    far_out = 3 * (1 - z // 2)
    return z, spot, inner, near, far_in, far_out


class Summer:
    STEPS = 9

    def __init__(self, n, shape, split_row=None, direct=False):
        self.n, (self.rows, self.width) = n, shape
        self.split_row, self.direct = split_row, direct
        self.size = n // PLANES
        self.chips = self.size // 2
        self.half = self.width // 2
        self.cuts = min(self.half // LANES, self.chips)
        self.cut = self.half // self.cuts
        self.bands = self.chips // self.cuts
        self.band = self.rows // self.bands
        self.shard = self.band // PLANES

    @staticmethod
    def padded(n, rows, width):
        summer = Summer(n, (rows, width))
        unit = summer.bands * PLANES * 16
        return -(-rows // unit) * unit

    def scratch(self):
        f32 = jnp.float32
        return [
            pltpu.VMEM((self.rows, self.half), f32),
            pltpu.VMEM((self.chips - 1, self.band, self.cut), f32),
            pltpu.VMEM(((1 if self.direct else 2) * self.shard, self.cut), f32),
            pltpu.VMEM(((PLANES - 1 if self.direct else 1) * self.shard, self.cut), f32),
            pltpu.SemaphoreType.DMA((8,)),
            pltpu.SemaphoreType.DMA((8,)),
        ]

    def bind(self, part, total, refs):
        self.part, self.total = part, total
        self.from_core, self.from_chip, self.from_pair, self.from_far, self.sent, self.got = refs
        me = lax.axis_index("nodes")
        self.z, spot = me // self.size, me % self.size
        self.chip, self.core = spot // 2, spot % 2
        self.low, self.high = self.z % 2, self.z // 2
        self.mine = pl.ds(pl.multiple_of(self.core * self.half, LANES), self.half)
        self.other = pl.ds(pl.multiple_of((1 - self.core) * self.half, LANES), self.half)
        self.across = self.device(self.z, self.chip, 1 - self.core)
        self.pair = self.device(self.high * 2 + 1 - self.low, self.chip, self.core)
        self.far = self.device((1 - self.high) * 2 + self.low, self.chip, self.core)

    def device(self, z, chip, core):
        return z * self.size + chip * 2 + core

    def column(self, hop):
        return self.device(lax.rem(self.z + hop, PLANES), self.chip, self.core)

    def peers(self):
        found = [self.across, self.pair, self.far]
        if self.direct:
            found = [self.across] + [self.column(hop) for hop in range(1, PLANES)]
        for hop in range(1, self.chips):
            found.append(self.device(self.z, lax.rem(self.chip + hop, self.chips), self.core))
        return found

    def patch(self, chip):
        row = pl.multiple_of((chip // self.cuts) * self.band, 8)
        col = self.core * self.half + (chip % self.cuts) * self.cut
        return row, pl.ds(pl.multiple_of(col, LANES), self.cut)

    def copy(self, hop, src, dst, device):
        pltpu.make_async_remote_copy(
            src_ref=src,
            dst_ref=dst,
            send_sem=self.sent.at[hop],
            recv_sem=self.got.at[hop],
            device_id=(device,),
            device_id_type=MESH,
        ).start()

    @staticmethod
    def settle(sem, held):
        pltpu.make_async_copy(held, held, sem).wait()

    def split(self, values, first_row):
        high = values.astype(self.total.dtype).astype(jnp.float32)
        middle = (values - high).astype(self.total.dtype).astype(jnp.float32)
        at = lax.broadcasted_iota(jnp.int32, values.shape, 0) + first_row - self.split_row
        rest = jnp.where(at == 1, values - high, values - high - middle)
        return jnp.where((at == 1) | (at == 2), rest, values)

    def column_step(self, at, band, cols, plane_shard, amount):
        part, total, shard = self.part, self.total, self.shard
        if at == 2:
            self.settle(self.got.at[1], self.from_chip)
            held = part[band, cols]
            for hop in range(1, self.chips):
                held = held + self.from_chip[hop - 1]
            part[band, cols] = held
            for hop in range(1, PLANES):
                src = part.at[plane_shard(lax.rem(self.z + hop, PLANES)), cols]
                dst = self.from_far.at[pl.ds((hop - 1) * shard, shard)]
                self.copy(3, src, dst, self.column(hop))
        elif at == 3:
            self.settle(self.got.at[3], self.from_far)
            held = part[plane_shard(self.z), cols]
            for hop in range(1, PLANES):
                held = held + self.from_far[pl.ds((hop - 1) * shard, shard), :]
            if self.split_row is not None:
                held = self.split(held, self.patch(self.chip)[0] + self.z * shard)
            total[plane_shard(self.z), cols] = held.astype(total.dtype)
            held = total.at[plane_shard(self.z), cols]
            for hop in range(1, PLANES):
                self.copy(4, held, held, self.column(hop))

    def step(self, at):
        part, total, shard = self.part, self.total, self.shard
        row, cols = self.patch(self.chip)
        band = pl.ds(row, self.band)

        def pairs(low):
            return pl.ds(pl.multiple_of(row + low * 2 * shard, 16), 2 * shard)

        def shards(high):
            return pl.ds(pl.multiple_of(row + (self.low * 2 + high) * shard, 16), shard)

        def amount(*shape):
            return total.at[pl.ds(0, shape[0]), pl.ds(0, shape[1])]

        short = self.band * total.dtype.itemsize // part.dtype.itemsize
        every_chip = self.from_chip.at[:, pl.ds(0, short)]

        def chips(hop):
            chip = lax.rem(self.chip + hop, self.chips)
            return chip, self.device(self.z, chip, self.core)

        def plane_shard(z):
            return pl.ds(pl.multiple_of(row + z * shard, 16), shard)

        if self.direct and 2 <= at <= 5:
            self.column_step(at, band, cols, plane_shard, amount)
        elif at == 0:
            self.copy(0, part.at[:, self.other], self.from_core, self.across)
        elif at == 1:
            self.settle(self.got.at[0], self.from_core)
            part[:, self.mine] += self.from_core[...]
            for hop in range(1, self.chips):
                chip, device = chips(hop)
                there, cut = self.patch(chip)
                src = part.at[pl.ds(there, self.band), cut]
                self.copy(1, src, self.from_chip.at[hop - 1], device)
        elif at == 2:
            self.settle(self.got.at[1], self.from_chip)
            held = part[band, cols]
            for hop in range(1, self.chips):
                held = held + self.from_chip[hop - 1]
            part[band, cols] = held
            self.copy(2, part.at[pairs(1 - self.low), cols], self.from_pair, self.pair)
        elif at == 3:
            self.settle(self.got.at[2], self.from_pair)
            part[pairs(self.low), cols] += self.from_pair[...]
            self.copy(3, part.at[shards(1 - self.high), cols], self.from_far, self.far)
        elif at == 4:
            self.settle(self.got.at[3], self.from_far)
            held = part[shards(self.high), cols] + self.from_far[...]
            if self.split_row is not None:
                held = self.split(held, row + (self.low * 2 + self.high) * shard)
            total[shards(self.high), cols] = held.astype(total.dtype)
            held = total.at[shards(self.high), cols]
            self.copy(4, held, held, self.far)
        elif at == 5:
            self.settle(self.got.at[4], amount(shard, self.cut))
            held = total.at[pairs(self.low), cols]
            self.copy(5, held, held, self.pair)
        elif at == 6:
            if self.direct:
                self.settle(self.got.at[4], amount((PLANES - 1) * shard, self.cut))
            else:
                self.settle(self.got.at[5], amount(2 * shard, self.cut))
            held = total.at[band, cols]
            for hop in range(1, self.chips):
                self.copy(6, held, held, chips(hop)[1])
        elif at == 7:
            self.settle(self.got.at[6], every_chip)
            held = total.at[:, self.mine]
            self.copy(7, held, held, self.across)
        else:
            self.settle(self.got.at[7], amount(self.rows, self.half))
            self.settle(self.sent.at[0], self.from_core)
            self.settle(self.sent.at[1], self.from_chip)
            self.settle(self.sent.at[3], self.from_far)
            if self.direct:
                self.settle(self.sent.at[4], amount((PLANES - 1) * shard, self.cut))
            else:
                self.settle(self.sent.at[2], self.from_pair)
                self.settle(self.sent.at[4], amount(shard, self.cut))
                self.settle(self.sent.at[5], amount(2 * shard, self.cut))
            self.settle(self.sent.at[6], every_chip)
            self.settle(self.sent.at[7], amount(self.rows, self.half))


def finish_kernel(n, tile, rows_there, grads, loss, total, part, rows, held, sem, *refs):
    fetches = [
        pltpu.make_async_copy(grads, held, sem.at[0]),
        pltpu.make_async_copy(rows_there, rows, sem.at[1]),
    ]
    for fetch in fetches:
        fetch.start()
    below = -(-rows.shape[0] // 8) * 8
    summer = Summer(n, part.shape, below, direct=True)
    summer.bind(part, total, refs)
    barrier = pltpu.get_barrier_semaphore()
    peers = summer.peers()
    for peer in peers:
        pl.semaphore_signal(barrier, inc=1, device_id=(peer,), device_id_type=MESH)
    count, depth = rows.shape

    def multiply(cols):
        part[:, cols] = jnp.zeros((part.shape[0], summer.half), jnp.float32)

        def add(at, carry):
            window = pl.ds(pl.multiple_of(at * tile, tile), tile)
            part[:count, cols] += mat_product(rows[:, window], held[window, cols])
            return carry

        lax.fori_loop(0, depth // tile, add, 0)
        part[pl.ds(below, 8), cols] = jnp.broadcast_to(loss[...], (8, summer.half))

    for fetch in fetches:
        fetch.wait()
    multiply(summer.other)
    pl.semaphore_wait(barrier, len(peers))
    summer.step(0)
    multiply(summer.mine)
    for at in range(1, Summer.STEPS):
        summer.step(at)


def finish(n, rows, grads, loss, collective):
    count = -(-rows.shape[0] // 8) * 8
    shape = (Summer.padded(n, count + 8, grads.shape[1]), grads.shape[1])
    vmem = pl.BlockSpec(memory_space=pltpu.VMEM)
    total = pl.pallas_call(
        functools.partial(finish_kernel, n, 1024),
        out_shape=jax.ShapeDtypeStruct(shape, jnp.bfloat16),
        in_specs=[
            pl.BlockSpec(memory_space=pltpu.HBM),
            pl.BlockSpec(memory_space=pltpu.HBM),
            vmem,
        ],
        out_specs=vmem,
        scratch_shapes=[
            pltpu.VMEM(shape, jnp.float32),
            pltpu.VMEM(rows.shape, rows.dtype),
            pltpu.VMEM(grads.shape, grads.dtype),
            pltpu.SemaphoreType.DMA((2,)),
        ]
        + Summer(n, shape, direct=True).scratch(),
        compiler_params=pltpu.CompilerParams(
            collective_id=collective, has_side_effects=True, vmem_limit_bytes=VMEM_MOST
        ),
        name="finish",
    )(rows, grads, loss)
    loss = jnp.sum(total[count : count + 3, 0].astype(jnp.float32))
    return total[: rows.shape[0]].astype(jnp.float32), loss


class Exchange:
    def __init__(self, n, slots, way, far_cap, near_cap, shape, kind):
        self.n, self.slots, self.way = n, slots, way
        self.far_cap, self.near_cap = far_cap, near_cap
        self.size = n // PLANES
        self.blocks, self.depth, self.width = shape
        self.kind = kind
        self.rows = self.depth // CHUNKS
        self.cols = self.width // PARTS
        self.steps = CHUNKS * PARTS
        self.ring = self.steps if self.size <= 8 else 2

    def out_shape(self):
        return jax.ShapeDtypeStruct(
            (CHUNKS, self.size, KINDS, self.slots, self.rows, self.width), self.kind
        )

    def scratch(self):
        def piece(*lead):
            return pltpu.VMEM(lead + (self.rows, self.cols), self.kind)

        steps, ring = self.steps, self.ring
        dma = pltpu.SemaphoreType.DMA
        return (
            [piece(self.near_cap) for _ in range(steps)]
            + [piece(2, self.far_cap) for _ in range(steps)]
            + [piece(steps, self.far_cap), piece(steps, self.near_cap)]
            + [piece(steps, 2, self.near_cap)]
            + [piece(ring, self.size, 2, self.slots) for _ in range(2)]
            + [dma, dma, dma, dma((steps,)), dma((steps,)), dma((2, ring)), dma((CHUNKS,))]
        )

    def bind(self, plan, table, out, refs):
        self.plan, self.table, self.out = plan.at[self.way], table, out
        steps = self.steps
        self.near_got, self.far_got = refs[:steps], refs[steps : 2 * steps]
        (
            self.far_stage,
            self.near_stage,
            self.pass_stage,
            first_stage,
            second_stage,
            self.far_sent,
            self.near_sent,
            self.pass_sent,
            self.near_recv,
            self.far_recv,
            self.serve_sent,
            self.serve_recv,
        ) = refs[2 * steps :]
        self.serve_stage = (first_stage, second_stage)
        me = lax.axis_index("nodes")
        self.z, self.spot, self.inner, near, far_in, far_out = place(me, self.size)
        self.near_dev = near * self.size + self.spot
        self.relay_dev = far_in * self.size + self.spot
        self.outer_dev = far_out * self.size + self.spot

    def greet(self, column=False):
        barrier = pltpu.get_barrier_semaphore()

        def hello(device):
            pl.semaphore_signal(barrier, inc=1, device_id=(device,), device_id_type=MESH)

        def in_plane(step, carry):
            hello(self.z * self.size + lax.rem(self.spot + step, self.size))
            return carry

        lax.fori_loop(1, self.size, in_plane, 0)
        hello(self.near_dev)
        if column:
            hello(((1 - self.z // 2) * 2 + self.z % 2) * self.size + self.spot)

            @pl.when(self.inner == 1)
            def _():
                hello(self.relay_dev)

            pl.semaphore_wait(barrier, self.size + 1 + self.inner)
            return

        @pl.when(self.inner == 1)
        def _():
            hello(self.relay_dev)
            hello(self.outer_dev)

        pl.semaphore_wait(barrier, self.size + 1)

    def window(self, step):
        return pl.ds((step // PARTS) * self.rows, self.rows), pl.ds(
            (step % PARTS) * self.cols, self.cols
        )

    def remote(self, src, dst, sent, got, device):
        return pltpu.make_async_remote_copy(
            src_ref=src,
            dst_ref=dst,
            send_sem=sent,
            recv_sem=got,
            device_id=(device,),
            device_id_type=MESH,
        )

    @staticmethod
    def settle(sem, held):
        pltpu.make_async_copy(held, held, sem).wait()

    def launch_far(self, step):
        rows, cols = self.window(step)
        plan, table, stage = self.plan, self.table, self.far_stage.at[step]

        def fill(at, carry):
            stage[at] = table[plan[ROW_FAR, at], rows, cols]
            return carry

        lax.fori_loop(0, self.far_cap, fill, 0)
        self.remote(
            stage,
            self.far_got[step].at[1 - self.inner],
            self.far_sent,
            self.far_recv.at[step],
            self.relay_dev,
        ).start()

    def launch_near(self, step):
        rows, cols = self.window(step)
        plan, table, stage = self.plan, self.table, self.near_stage.at[step]

        def fill(at, carry):
            stage[at] = table[plan[ROW_NEAR, at], rows, cols]
            return carry

        lax.fori_loop(0, self.near_cap, fill, 0)
        self.remote(
            stage, self.near_got[step], self.near_sent, self.near_recv.at[step], self.near_dev
        ).start()

    def relay(self, step):
        plan, got, stage = self.plan, self.far_got[step], self.pass_stage.at[step]
        part = got.at[:, pl.ds(0, self.near_cap)]

        @pl.when(self.inner == 1)
        def _():
            self.settle(self.far_recv.at[step], got)

            def fill(at, carry):
                for lane in range(2):
                    stage[lane, at] = got[lane, plan[ROW_PASS + lane, at]]
                return carry

            lax.fori_loop(0, self.near_cap, fill, 0)
            self.remote(
                stage, part, self.pass_sent, self.far_recv.at[step], self.near_dev
            ).start()

        @pl.when(self.inner == 0)
        def _():
            self.settle(self.far_recv.at[step], part)

    def serve(self, step, pair):
        rows, cols = self.window(step)
        plan, table, slots, size = self.plan, self.table, self.slots, self.size
        chunk, slot_at = step // PARTS, step % self.ring
        if pair == 0:
            self.settle(self.near_recv.at[step], self.near_got[step])
        if step >= self.ring:
            self.drain(step - self.ring, pair)
        stage = self.serve_stage[pair].at[slot_at]

        def fill(peer, carry):
            taker = self.z * size + peer
            for slot in range(slots):
                first = plan[ROW_SERVE + 2 * pair * slots + slot, taker]
                second = plan[ROW_SERVE + (2 * pair + 1) * slots + slot, taker]
                if pair == 0:
                    stage[peer, 0, slot] = table[first, rows, cols]
                    stage[peer, 1, slot] = self.near_got[step][second]
                else:
                    stage[peer, 0, slot] = self.far_got[step][0, first]
                    stage[peer, 1, slot] = self.far_got[step][1, second]
            return carry

        lax.fori_loop(0, size, fill, 0)
        there = self.out.at[chunk, self.spot, pl.ds(2 * pair, 2), :, :, cols]
        pltpu.make_async_copy(stage.at[self.spot], there, self.serve_recv.at[chunk]).start()

        def send(hop, carry):
            peer = lax.rem(self.spot + hop, size)
            self.remote(
                stage.at[peer],
                there,
                self.serve_sent.at[pair, slot_at],
                self.serve_recv.at[chunk],
                self.z * size + peer,
            ).start()
            return carry

        lax.fori_loop(1, size, send, 0)

    def drain(self, step, pair):
        slot_at = step % self.ring
        held = self.serve_stage[pair].at[slot_at, pl.ds(0, self.size - 1)]
        self.settle(self.serve_sent.at[pair, slot_at], held)

    def run(self, side=None):
        steps = self.steps
        for step in range(min(AHEAD, steps)):
            self.launch_far(step)
            self.launch_near(step)

        @pl.when(self.inner == 1)
        def _():
            for step in range(AHEAD, min(NEAR_AHEAD, steps)):
                self.launch_near(step)

        for step in range(min(LEAD, steps)):
            self.serve(step, 0)
        for step in range(steps):
            if step + AHEAD < steps:
                self.launch_far(step + AHEAD)
                if NEAR_AHEAD == AHEAD:
                    self.launch_near(step + AHEAD)
                else:

                    @pl.when(self.inner == 0)
                    def _():
                        self.launch_near(step + AHEAD)

            if NEAR_AHEAD > AHEAD and step + NEAR_AHEAD < steps:

                @pl.when(self.inner == 1)
                def _():
                    self.launch_near(step + NEAR_AHEAD)

            self.relay(step)
            self.serve(step, 1)
            if step + LEAD < steps:
                self.serve(step + LEAD, 0)
            if side is not None:
                side(step)
        if side is not None:
            side(steps)
        for chunk in range(CHUNKS):
            self.settle(self.serve_recv.at[chunk], self.out.at[chunk])
        def drain(at, carry):
            for pair in range(2):
                self.drain(at, pair)
            return carry

        lax.fori_loop(0, self.ring, drain, 0)
        self.settle(self.far_sent, self.far_stage)
        self.settle(self.near_sent, self.near_stage)

        @pl.when(self.inner == 1)
        def _():
            self.settle(self.pass_sent, self.pass_stage)


def exchange_kernel(moves, plan, table, out, held_table, table_sem, *refs):
    moves.bind(plan, held_table, out, refs)
    fetch = pltpu.make_async_copy(table, held_table, table_sem)
    fetch.start()
    moves.greet()
    fetch.wait()
    moves.run()


def exchange_sum_kernel(
    moves, summer, plan, table, part, out, total, held_table, table_sem, held, sem, *refs
):
    moves.bind(plan, held_table, out, refs[6:])
    fetch_table = pltpu.make_async_copy(table, held_table, table_sem)
    fetch_table.start()
    summer.bind(held, total, refs[:6])
    fetch = pltpu.make_async_copy(part, held, sem)
    fetch.start()
    moves.greet(column=True)
    fetch_table.wait()

    def side(step):
        if step == 0:
            fetch.wait()
        if step in SUM_AT:
            summer.step(SUM_AT.index(step))

    moves.run(side)


def exchange(n, slots, way, far_cap, near_cap, collective, plan, table, part=None):
    moves = Exchange(n, slots, way, far_cap, near_cap, table.shape, table.dtype)
    hbm = pl.BlockSpec(memory_space=pl.ANY)
    vmem = pl.BlockSpec(memory_space=pltpu.VMEM)
    in_specs = [pl.BlockSpec(memory_space=pltpu.SMEM), hbm]
    table_held = [pltpu.VMEM(table.shape, table.dtype), pltpu.SemaphoreType.DMA]
    params = pltpu.CompilerParams(
        collective_id=collective, has_side_effects=True, vmem_limit_bytes=VMEM_MOST
    )
    if part is None:
        return pl.pallas_call(
            functools.partial(exchange_kernel, moves),
            out_shape=moves.out_shape(),
            in_specs=in_specs,
            out_specs=hbm,
            scratch_shapes=table_held + moves.scratch(),
            compiler_params=params,
            name="exchange",
        )(plan, table)
    summer = Summer(n, part.shape)
    return pl.pallas_call(
        functools.partial(exchange_sum_kernel, moves, summer),
        out_shape=(moves.out_shape(), jax.ShapeDtypeStruct(part.shape, jnp.bfloat16)),
        in_specs=in_specs + [hbm],
        out_specs=(hbm, vmem),
        scratch_shapes=table_held
        + [pltpu.VMEM(part.shape, jnp.float32), pltpu.SemaphoreType.DMA]
        + summer.scratch()
        + moves.scratch(),
        compiler_params=params,
        name="exchange_sum",
    )(plan, table, part)


def add_products(flip, slots, first_row, sinks, weights, got, total, at, size):
    z, _, _, near, far_in, far_out = place(lax.axis_index("nodes"), size)
    depth, width = total.shape[1:]
    dims = (((0,), (0,)), ((), ())) if flip else (((1,), (0,)), ((), ()))
    for kind, owner_z in enumerate((z, near, far_in, far_out)):
        for slot in range(slots):
            sink = sinks[first_row + slot, owner_z * size + at]
            rows = got[:, 0, kind, slot].reshape(depth, width)
            total[sink] += lax.dot_general(
                weights[owner_z, 0, slot], rows, dims, preferred_element_type=jnp.float32
            )


def return_sum_kernel(slots, first_row, *refs):
    sinks, weights, got, own, mixer = refs[:5]
    states, head_state, out = refs[5:13], refs[13:17], refs[17]
    updates, head_update, total, mixer_half = refs[18:24], refs[24:27], refs[27], refs[28]
    at = pl.program_id(0)
    blocks, depth, width = out.shape

    @pl.when(at == 0)
    def _():
        total[...] = jnp.zeros_like(total)
        mixer_half[...] = to_half(mixer[0])
        label_width = head_state[0].shape[1]
        head_grad = head_state[1][...].astype(jnp.float32).T[:, :label_width]
        fresh = adam_update(head_state[0][...], head_grad, head_state[2][...], head_state[3][...])
        for to, values in zip(head_update, fresh):
            to[...] = values

    span = own.shape[0] // depth
    base = right_product(own[...], mixer_half[...]).reshape(span, depth, width)
    total[pl.ds(at * span, span)] += base
    for state, update in ((states[:4], updates[:3]), (states[4:], updates[3:])):
        grad = state[1][...].astype(jnp.float32)
        fresh = adam_update(state[0][...], grad, state[2][...], state[3][...])
        for to, values in zip(update, fresh):
            to[...] = values
    size = pl.num_programs(0)
    add_products(True, slots, first_row, sinks, weights, got, total, at, size)

    @pl.when(at == pl.num_programs(0) - 1)
    def _():
        out[...] = to_half(total[:blocks])


def block_specs(weights, got):
    chunks, size, kinds, slots, rows, width = got.shape
    depth = chunks * rows
    edges = weights.reshape(PLANES, size, slots, depth, depth)

    def clip(at):
        return jnp.minimum(at, size - 1)

    specs = [
        pl.BlockSpec((PLANES, 1, slots, depth, depth), lambda at, *_: (0, clip(at), 0, 0, 0)),
        pl.BlockSpec(
            (chunks, 1, kinds, slots, rows, width), lambda at, *_: (0, clip(at), 0, 0, 0, 0)
        ),
    ]
    return edges, specs


def return_sum(first_row, sinks, weights, got, blocks, own, mixer, grads, groups, head):
    chunks, size, _, slots, rows, width = got.shape
    depth = chunks * rows
    edges, specs = block_specs(weights, got)
    tile = blocks * depth // size
    specs = specs + [
        pl.BlockSpec((tile, width), lambda at, sinks: (at, 0)),
        pl.BlockSpec((1, width, width), lambda at, sinks: (0, 0, 0)),
    ]
    states, shapes, out_specs = [], [], []
    for place_at, (weight, first, second) in enumerate(groups):
        part = weight.shape[0] // size
        spec = pl.BlockSpec((part, width), lambda at, sinks: (at, 0))
        moved = pl.BlockSpec((part, width), lambda at, sinks, p=place_at: (at + p * size, 0))
        states += [weight, grads, first, second]
        specs = specs + [spec, moved, spec, spec]
        shapes += [jax.ShapeDtypeStruct(weight.shape, jnp.float32)] * 3
        out_specs += [spec] * 3
    head_at = 2 * groups[0][0].shape[0] // LANES
    still = pl.BlockSpec(head[0].shape, lambda at, sinks: (0, 0))
    states += [head[0], grads, head[1], head[2]]
    specs = specs + [still, pl.BlockSpec((LANES, width), lambda at, sinks: (head_at, 0)), still, still]
    shapes += [jax.ShapeDtypeStruct(head[0].shape, jnp.float32)] * 3
    out_specs += [still] * 3
    found = pl.pallas_call(
        functools.partial(return_sum_kernel, slots, first_row),
        out_shape=[jax.ShapeDtypeStruct((blocks, depth, width), jnp.bfloat16)] + shapes,
        grid_spec=pltpu.PrefetchScalarGridSpec(
            num_scalar_prefetch=1,
            grid=(size,),
            in_specs=specs,
            out_specs=[pl.BlockSpec((blocks, depth, width), lambda at, sinks: (0, 0, 0))]
            + out_specs,
            scratch_shapes=[
                pltpu.VMEM((blocks + 1, depth, width), jnp.float32),
                pltpu.VMEM((width, width), jnp.bfloat16),
            ],
        ),
        compiler_params=pltpu.CompilerParams(vmem_limit_bytes=48 * 2**20),
        name="return_sum",
    )(sinks, edges, got, own, mixer, *states)
    return found[0], found[1:4], found[4:7], found[7:10]


ROW_FAR, ROW_NEAR, ROW_PASS, ROW_SERVE = 0, 1, 2, 4


def plan_rows(slots):
    wishes = ROW_SERVE + KINDS * slots
    return wishes, -(-(wishes + slots) // 8) * 8


def column(values, lane):
    lanes = lax.broadcasted_iota(jnp.int32, values.shape, 1)
    return jnp.sum(jnp.where(lanes == lane, values, 0.0), axis=1, keepdims=True)


def lay_plan(n, slots, blocks, rungs, way, wishes_of, plan, chosen, present):
    size = n // PLANES
    me = lax.axis_index("nodes")
    z, spot, inner, near, far_in, far_out = place(me, size)
    half = z // 2
    row_wish, _ = plan_rows(slots)

    taker = lax.broadcasted_iota(jnp.int32, (LANES, LANES), 0)
    group = lax.broadcasted_iota(jnp.int32, (LANES, LANES), 1)
    plane_of = taker // size
    member = (taker < n) & ((plane_of == group) | (plane_of // 2 + PLANES == group))
    member = jnp.where(member, 1.0, 0.0).astype(jnp.bfloat16)
    hits = jnp.zeros((n * blocks, LANES), jnp.float32)
    for slot in range(slots):
        wish = wishes_of[slot][...]
        ids = lax.broadcasted_iota(jnp.int32, (n, blocks, LANES), 1)
        hot = jnp.where(wish[:, None, :] == ids, 1.0, 0.0).astype(jnp.bfloat16)
        hits = hits + mat_product(hot.reshape(n * blocks, LANES), member)
    here = jnp.where(hits > 0.0, 1.0, 0.0)
    present[...] = here
    counts = jnp.sum(here.reshape(n, blocks, LANES), axis=1)
    owner_plane = lax.broadcasted_iota(jnp.int32, (n, LANES), 0) // size
    lane = lax.broadcasted_iota(jnp.int32, (n, LANES), 1)
    is_near = (lane < PLANES) & (lane != owner_plane)
    is_far = (lane >= PLANES) & (lane < PLANES + 2) & (lane - PLANES != owner_plane // 2)
    near_most = jnp.max(jnp.where(is_near, counts, 0.0), axis=(0, 1), keepdims=True)
    far_most = jnp.max(jnp.where(is_far, counts, 0.0), axis=(0, 1), keepdims=True)
    rung = jnp.zeros((1, 1), jnp.float32)
    for far_cap, near_cap in rungs[:-1]:
        over = (far_most > float(far_cap)) | (near_most > float(near_cap))
        rung = rung + jnp.where(over, 1.0, 0.0)

    def put(row, values):
        plan[way, pl.ds(row, 1), :] = values.astype(jnp.int32)

    chosen[...] = len(rungs) - 1 - rung.astype(jnp.int32)
    block_id = lax.broadcasted_iota(jnp.int32, (blocks, LANES), 0)
    block_lane = lax.broadcasted_iota(jnp.int32, (blocks, LANES), 1)
    ids = block_id.astype(jnp.float32)
    below = lax.broadcasted_iota(jnp.int32, (blocks, blocks), 0) > lax.broadcasted_iota(
        jnp.int32, (blocks, blocks), 1
    )
    below = jnp.where(below, 1.0, 0.0).astype(jnp.bfloat16)

    def listed(chosen, pos, values):
        at = (chosen > 0.0) & (pos.astype(jnp.int32) == block_lane)
        return jnp.sum(jnp.where(at, values, 0.0), axis=0, keepdims=True)

    for kind, owner_z in enumerate((z, near, far_in, far_out)):
        owner = owner_z * size + spot
        mine = present[pl.ds(pl.multiple_of(owner * blocks, 8), blocks), :]
        rank = mat_product(below, mine.astype(jnp.bfloat16))
        if kind == 0:
            where_held = ids
            far = PLANES + 1 - half
            put(ROW_FAR, listed(column(mine, far), column(rank, far), ids))
            put(ROW_NEAR, listed(column(mine, near), column(rank, near), ids))
        elif kind == 1:
            where_held = column(rank, z)
        else:
            where_held = column(rank, z + inner * (PLANES + half - z))
            edge = 3 * half
            put(
                ROW_PASS + kind - 2,
                listed(column(mine, edge), column(rank, edge), column(rank, PLANES + half)),
            )
        for slot in range(slots):
            wish = wishes_of[slot][pl.ds(owner, 1), :]
            held = jnp.where(wish == block_id, where_held, 0.0)
            put(ROW_SERVE + kind * slots + slot, jnp.sum(held, axis=0, keepdims=True))
            if kind == 0:
                put(row_wish + slot, wish)


def prelude_kernel(n, slots, blocks, rungs, tile, *refs):
    need, target, alive, rows, weight, hidden, plan = refs[:7]
    chosen, sunk, mine, taken = refs[7:9], refs[9], refs[10], refs[11]
    wishes = refs[12 : 12 + 2 * slots]
    present, held, held_weight, row_sem, weight_sem, send_sem, recv_sem = refs[12 + 2 * slots :]
    tiles = rows.shape[1] // tile

    def window(at):
        return pl.ds(pl.multiple_of(at * tile, tile), tile)

    def fetch(at):
        part = window(at)
        return pltpu.make_async_copy(rows.at[:, part], held.at[:, part], row_sem.at[at])

    fetch_weight = pltpu.make_async_copy(weight, held_weight, weight_sem)
    fetch_weight.start()
    for at in range(tiles):
        fetch(at).start()
    me = lax.axis_index("nodes")
    barrier = pltpu.get_barrier_semaphore()

    def greet(step, carry):
        pl.semaphore_signal(
            barrier, inc=1, device_id=(lax.rem(me + step, n),), device_id_type=MESH
        )
        return carry

    lax.fori_loop(1, n, greet, 0)
    mine[...] = jnp.full(mine.shape, blocks, jnp.int32)
    sunk[...] = jnp.full(sunk.shape, blocks, jnp.int32)
    for slot in range(slots):
        live = slot < alive[...]
        sunk_row = jnp.where(live, target[pl.ds(slot, 1), :], blocks)
        mine[:, pl.ds(slot * LANES, n)] = jnp.where(live, need[pl.ds(slot, 1), :], blocks)
        mine[:, pl.ds((slots + slot) * LANES, n)] = sunk_row
        sunk[pl.ds(slot, 1), pl.ds(0, n)] = sunk_row
    taken[me] = mine[...]
    fetch_weight.wait()
    half_weight = to_half(held_weight[...])

    def project(at):
        fetch(at).wait()
        hidden[window(at), :] = to_half(left_product(held[:, window(at)], half_weight))

    for at in range(tiles // 2):
        project(at)
    pl.semaphore_wait(barrier, n - 1)

    def send(step, carry):
        pltpu.make_async_remote_copy(
            src_ref=mine,
            dst_ref=taken.at[me],
            send_sem=send_sem,
            recv_sem=recv_sem,
            device_id=(lax.rem(me + step, n),),
            device_id_type=MESH,
        ).start()
        return carry

    lax.fori_loop(1, n, send, 0)
    for at in range(tiles // 2, tiles):
        project(at)
    others = taken.at[pl.ds(0, n - 1)]
    pltpu.make_async_copy(others, others, recv_sem).wait()
    pltpu.make_async_copy(others, others, send_sem).wait()

    every = taken[...].reshape(n, 2 * slots * LANES)
    unit = lax.broadcasted_iota(jnp.int32, (n, LANES), 0) == lax.broadcasted_iota(
        jnp.int32, (n, LANES), 1
    )
    unit = jnp.where(unit, 1.0, 0.0).astype(jnp.bfloat16)
    for slot in range(slots):
        part = every[:, slot * LANES : (slot + 1) * LANES]
        turned = left_product(part.astype(jnp.float32).astype(jnp.bfloat16), unit)
        wishes[slot][...] = turned[:n].astype(jnp.int32)
        wishes[slots + slot][...] = every[:, (slots + slot) * LANES : (slots + slot + 1) * LANES]
    for way in range(2):
        lay_plan(
            n,
            slots,
            blocks,
            rungs,
            way,
            wishes[way * slots : (way + 1) * slots],
            plan,
            chosen[way],
            present,
        )


def prelude(n, slots, blocks, rungs, need, target, alive, rows, weight):
    count, width = rows.shape[1], weight.shape[1]
    vmem = pl.BlockSpec(memory_space=pltpu.VMEM)
    plan_shape = (2, plan_rows(slots)[1], LANES)
    return pl.pallas_call(
        functools.partial(prelude_kernel, n, slots, blocks, rungs, 512),
        out_shape=(
            jax.ShapeDtypeStruct((count, width), jnp.bfloat16),
            jax.ShapeDtypeStruct(plan_shape, jnp.int32),
            jax.ShapeDtypeStruct((1, 1), jnp.int32),
            jax.ShapeDtypeStruct((1, 1), jnp.int32),
            jax.ShapeDtypeStruct((8, LANES), jnp.int32),
        ),
        in_specs=[vmem, vmem, vmem] + [pl.BlockSpec(memory_space=pltpu.HBM)] * 2,
        out_specs=(vmem,) * 5,
        scratch_shapes=[
            pltpu.VMEM((1, 2 * slots * LANES), jnp.int32),
            pltpu.VMEM((n, 1, 2 * slots * LANES), jnp.int32),
        ]
        + [pltpu.VMEM((n, LANES), jnp.int32) for _ in range(2 * slots)]
        + [
            pltpu.VMEM((n * blocks, LANES), jnp.float32),
            pltpu.VMEM(rows.shape, rows.dtype),
            pltpu.VMEM(weight.shape, weight.dtype),
            pltpu.SemaphoreType.DMA((count // 512,)),
            pltpu.SemaphoreType.DMA,
            pltpu.SemaphoreType.DMA,
            pltpu.SemaphoreType.DMA,
        ],
        compiler_params=pltpu.CompilerParams(
            collective_id=0, has_side_effects=True, vmem_limit_bytes=VMEM_MOST
        ),
        name="prelude",
    )(need, target, alive, rows, weight)


def sigmoid(values):
    return 1.0 / (1.0 + jnp.exp(-values))


def dense_kernel(label_width, pieces, slots, first_row, count, sinks, edges, got, *refs):
    marks, truth, own = refs[:3]
    grad_own, grad_taken, part, loss, total = refs[6:11]
    pair, merge, head = refs[11:]
    at = pl.program_id(0)
    gathers = pl.num_programs(0) - total.shape[0] * total.shape[1] // own.shape[0]

    @pl.when(at == 0)
    def _():
        total[...] = jnp.zeros_like(total)
        part[...] = jnp.zeros_like(part)
        loss[...] = jnp.zeros_like(loss)
        for to, weight in zip((pair, merge), refs[3:5]):
            to[...] = to_half(weight[...])
        head[...] = to_half(jnp.pad(refs[5][...], ((0, 0), (0, LANES - label_width))))

    @pl.when(at < gathers)
    def _():
        add_products(False, slots, first_row, sinks, edges, got, total, at, gathers)

    @pl.when(at >= gathers)
    def _():
        span = own.shape[0] // total.shape[1]
        taken = total.at[pl.ds((at - gathers) * span, span)]
        dense_tile(
            label_width,
            pieces,
            (count, marks, truth, own, taken, pair, merge, head),
            (grad_own, grad_taken, part, loss),
        )


def dense_tile(label_width, pieces, given, made):
    count, marks, truth, own, taken, pair, merge, head = given
    grad_own, grad_taken, part, loss = made
    width = own.shape[1]
    tile = own.shape[0] // pieces
    span = taken.shape[0] // pieces
    denom = count[0].astype(jnp.float32) * float(label_width)

    def stages(piece):
        rows = pl.ds(piece * tile, tile)
        hidden = own[rows, :]
        gathered = to_half(taken[pl.ds(piece * span, span)]).reshape(tile, width)
        self_part = to_half(mat_product(hidden, pair[0]))
        neigh_part = to_half(mat_product(gathered, pair[1]))
        yield
        linear = mat_product(self_part, merge[:width]) + mat_product(neigh_part, merge[width:])
        yield
        sig = sigmoid(linear)
        active = linear * sig
        scale = lax.rsqrt(jnp.sum(active * active, axis=1, keepdims=True) + norm_eps)
        output = active * scale
        final = to_half(output)
        yield
        logits = mat_product(final, head[...])
        yield
        labels = truth[rows, :].astype(jnp.float32)
        labels = jnp.pad(labels, ((0, 0), (0, LANES - label_width)))
        marked = marks[0, :, rows].astype(jnp.float32)
        marked = jnp.broadcast_to(marked, (LANES, tile)).T
        column_id = lax.broadcasted_iota(jnp.int32, (tile, LANES), 1)
        marked = jnp.where(column_id < label_width, marked, 0.0)
        decay = jnp.exp(-jnp.abs(logits))
        entry = jnp.maximum(logits, 0.0) - logits * labels + jnp.log1p(decay)
        loss[...] += jnp.sum(entry * marked, axis=(0, 1), keepdims=True) / denom
        grad_logits = to_half((sigmoid(logits) - labels) * marked / denom)
        yield
        part[pl.ds(4 * width, LANES), :] += left_product(grad_logits, final)
        grad_out = right_product(grad_logits, head[...])
        yield
        along = jnp.sum(grad_out * output, axis=1, keepdims=True)
        grad_active = scale * (grad_out - output * along)
        grad_linear = to_half(grad_active * sig * (1.0 + linear * (1.0 - sig)))
        yield
        part[pl.ds(2 * width, width), :] += left_product(self_part, grad_linear)
        part[pl.ds(3 * width, width), :] += left_product(neigh_part, grad_linear)
        grad_self = to_half(right_product(grad_linear, merge[:width]))
        grad_neigh = to_half(right_product(grad_linear, merge[width:]))
        yield
        grad_own[rows, :] = grad_self
        part[pl.ds(0, width), :] += left_product(hidden, grad_self)
        part[pl.ds(width, width), :] += left_product(gathered, grad_neigh)
        grad_taken[rows, :] = to_half(right_product(grad_neigh, pair[1]))
        yield

    running = [stages(piece) for piece in range(pieces)]
    for turn in range(STAGES + SKEW * (pieces - 1)):
        for piece in range(pieces):
            if 0 <= turn - SKEW * piece < STAGES:
                next(running[piece])


def dense(tile, pieces, part_rows, first_row, scalars, edges, got, marks, truth, own, weights):
    rows, width = own.shape
    label_width = truth.shape[1]
    size, slots = got.shape[1], got.shape[3]
    edges, specs = block_specs(edges, got)
    depth = edges.shape[-1]

    def later(at):
        return jnp.maximum(at - size, 0)

    by_rows = pl.BlockSpec((tile, width), lambda at, *_: (later(at), 0))

    def whole(values):
        return pl.BlockSpec(
            values.shape, lambda at, *_: (0,) * values.ndim, pipeline_mode=pl.Buffered(1)
        )

    return pl.pallas_call(
        functools.partial(dense_kernel, label_width, pieces, slots, first_row),
        out_shape=(
            jax.ShapeDtypeStruct((rows, width), jnp.bfloat16),
            jax.ShapeDtypeStruct((rows, width), jnp.bfloat16),
            jax.ShapeDtypeStruct((part_rows, width), jnp.float32),
            jax.ShapeDtypeStruct((1, 1), jnp.float32),
        ),
        grid_spec=pltpu.PrefetchScalarGridSpec(
            num_scalar_prefetch=2,
            grid=(size + rows // tile,),
            in_specs=specs
            + [
                pl.BlockSpec((1, 1, tile), lambda at, *_: (later(at), 0, 0)),
                pl.BlockSpec((tile, label_width), lambda at, *_: (later(at), 0)),
                by_rows,
            ]
            + [whole(values) for values in weights],
            out_specs=(
                by_rows,
                by_rows,
                pl.BlockSpec((part_rows, width), lambda at, *_: (0, 0)),
                pl.BlockSpec((1, 1), lambda at, *_: (0, 0)),
            ),
            scratch_shapes=[pltpu.VMEM((rows // depth + 1, depth, width), jnp.float32)]
            + [pltpu.VMEM(values.shape, jnp.bfloat16) for values in weights[:2]]
            + [pltpu.VMEM((width, LANES), jnp.bfloat16)],
        ),
        compiler_params=pltpu.CompilerParams(vmem_limit_bytes=VMEM_MOST),
        name="dense",
    )(*scalars, edges, got, marks.reshape(rows // tile, 1, tile), truth, own, *weights)


def shards(
    features,
    labels,
    labelled,
    label_count,
    need_blocks,
    need_count,
    target_block,
    adjacency,
    embed_weight,
    pair_weight,
    merge_weight,
    head_weight,
    embed_moment,
    pair_moment,
    merge_moment,
    head_moment,
    embed_variance,
    pair_variance,
    merge_variance,
    head_variance,
):
    row_count = features.shape[0]
    hidden_width = embed_weight.shape[1]
    block_rows = adjacency.shape[1]
    slots = need_blocks.shape[2]
    n = lax.axis_size("nodes")
    size = n // PLANES
    block_count = row_count // block_rows
    near_full = min(block_count, size * slots)
    rungs = [(22, 15), (24, 16), (block_count, near_full)]
    if near_full > 16 or block_count < 24:
        rungs = rungs[-1:]
    hidden_half, plan, *rung_of, sunk = prelude(
        n,
        slots,
        block_count,
        rungs,
        need_blocks[0].T,
        target_block[0].T,
        need_count,
        features.T,
        embed_weight,
    )
    row_wish, _ = plan_rows(slots)

    def swap(way, *held):
        def at(rung):
            far_cap, near_cap = rungs[rung]
            return lambda *held: exchange(
                n, slots, way, far_cap, near_cap, 2 + way * len(rungs) + rung, *held
            )

        if len(rungs) == 1:
            return at(0)(plan, *held)
        branches = [at(rung) for rung in reversed(range(len(rungs)))]
        return lax.switch(rung_of[way].reshape(()), branches, plan, *held)

    got = swap(0, hidden_half.reshape(block_count, block_rows, hidden_width))
    later, got = lax.optimization_barrier((adjacency, got))
    edges_back = lax.all_to_all(later, "nodes", split_axis=0, concat_axis=0, tiled=True)
    label_width = labels.shape[1]
    part_rows = Summer.padded(n, 4 * hidden_width + LANES, hidden_width)
    grad_self, grad_gathered, part, loss_part = dense(
        min(TILE, row_count),
        PIECES,
        part_rows,
        0,
        (label_count, sunk),
        adjacency,
        got,
        labelled,
        labels,
        hidden_half,
        (pair_weight[0], merge_weight[0], head_weight),
    )
    back, total = swap(1, grad_gathered.reshape(block_count, block_rows, hidden_width), part)
    def flat(values):
        return values.reshape(-1, hidden_width)

    grad_hidden, pair_next, merge_next, head_next = return_sum(
        row_wish,
        plan.reshape(-1, LANES),
        edges_back,
        back,
        block_count,
        grad_self,
        pair_weight[0],
        total,
        (
            (flat(pair_weight), flat(pair_moment), flat(pair_variance)),
            (flat(merge_weight), flat(merge_moment), flat(merge_variance)),
        ),
        (head_weight, head_moment, head_variance),
    )
    pair_next = [values.reshape(pair_weight.shape) for values in pair_next]
    merge_next = [values.reshape(merge_weight.shape) for values in merge_next]
    grad_hidden = grad_hidden.reshape(row_count, hidden_width)
    embed_grad, loss_total = finish(n, features.T, grad_hidden, loss_part, 1)
    embed_next = adam_update(embed_weight, embed_grad, embed_moment, embed_variance)
    return (
        loss_total.reshape(1),
        embed_next[0],
        pair_next[0],
        merge_next[0],
        head_next[0],
        embed_next[1],
        pair_next[1],
        merge_next[1],
        head_next[1],
        embed_next[2],
        pair_next[2],
        merge_next[2],
        head_next[2],
    )


def solution(mesh):
    split = ("nodes",)
    return jax.shard_map(
        shards,
        mesh=mesh,
        in_specs=(
            P("nodes", None),
            P("nodes", None),
            P("nodes"),
            P(),
            P("nodes", None, None),
            P("nodes", None),
            P("nodes", None, None),
            P("nodes", None, None),
        )
        + (P(),) * 12,
        out_specs=(P(),) * 13,
        check_vma=False,
    )
```

```python
import functools

import jax
import jax.numpy as jnp
from jax import lax
from jax.experimental import pallas as pl
from jax.experimental.pallas import tpu as pltpu
from jax.sharding import PartitionSpec as P

norm_eps = 1e-06
learn_rate = 0.03
beta_one = 0.9
beta_two = 0.999
adam_eps = 1e-08
decay_rate = 0.01
adam_step = 10.0

PLANES = 4
KINDS = 4
CHUNKS = 8
LANES = 128
VMEM_MOST = 60 * 2**20
TILE = 1024
PIECES = 2
STAGES = 9
SKEW = 2
PACE = {
    4: (4, 2, (0, 2, 8, 11, 14, 17, 20, 26, 32)),
    2: (3, 1, (0, 1, 4, 6, 8, 9, 11, 14, 16)),
}
MESH = pl.DeviceIdType.MESH


def to_half(value):
    return value.astype(jnp.bfloat16)


def mat_product(former, latter):
    return jnp.dot(former, latter, preferred_element_type=jnp.float32)


def left_product(former, latter):
    return lax.dot_general(
        former, latter, (((0,), (0,)), ((), ())), preferred_element_type=jnp.float32
    )


def right_product(former, latter):
    return lax.dot_general(
        former, latter, (((1,), (1,)), ((), ())), preferred_element_type=jnp.float32
    )


def adam_update(weight, grad, first, second):
    first_new = beta_one * first + (1.0 - beta_one) * grad
    second_new = beta_two * second + (1.0 - beta_two) * grad * grad
    first_hat = first_new * (1.0 / (1.0 - beta_one**adam_step))
    second_hat = second_new * (1.0 / (1.0 - beta_two**adam_step))
    weight_new = weight - learn_rate * (
        first_hat / (jnp.sqrt(second_hat) + adam_eps) + decay_rate * weight
    )
    return (weight_new, first_new, second_new)


def place(me, plane_size):
    z = me // plane_size
    spot = me % plane_size
    inner = (z % 2 + z // 2) % 2
    near = z + 1 - 2 * (z % 2)
    far_in = 2 - z // 2
    far_out = 3 * (1 - z // 2)
    return z, spot, inner, near, far_in, far_out


class Summer:
    STEPS = 9

    def __init__(self, n, shape, split_row=None, direct=False):
        self.n, (self.rows, self.width) = n, shape
        self.split_row, self.direct = split_row, direct
        self.size = n // PLANES
        self.chips = self.size // 2
        self.half = self.width // 2
        self.cuts = min(self.half // LANES, self.chips)
        self.cut = self.half // self.cuts
        self.bands = self.chips // self.cuts
        self.band = self.rows // self.bands
        self.shard = self.band // PLANES

    @staticmethod
    def padded(n, rows, width):
        summer = Summer(n, (rows, width))
        unit = summer.bands * PLANES * 16
        return -(-rows // unit) * unit

    def scratch(self):
        f32 = jnp.float32
        return [
            pltpu.VMEM((self.rows, self.half), f32),
            pltpu.VMEM((self.chips - 1, self.band, self.cut), f32),
            pltpu.VMEM(((1 if self.direct else 2) * self.shard, self.cut), f32),
            pltpu.VMEM(((PLANES - 1 if self.direct else 1) * self.shard, self.cut), f32),
            pltpu.SemaphoreType.DMA((8,)),
            pltpu.SemaphoreType.DMA((8,)),
        ]

    def bind(self, part, total, refs):
        self.part, self.total = part, total
        self.from_core, self.from_chip, self.from_pair, self.from_far, self.sent, self.got = refs
        me = lax.axis_index("nodes")
        self.z, spot = me // self.size, me % self.size
        self.chip, self.core = spot // 2, spot % 2
        self.low, self.high = self.z % 2, self.z // 2
        self.mine = pl.ds(pl.multiple_of(self.core * self.half, LANES), self.half)
        self.other = pl.ds(pl.multiple_of((1 - self.core) * self.half, LANES), self.half)
        self.across = self.device(self.z, self.chip, 1 - self.core)
        self.pair = self.device(self.high * 2 + 1 - self.low, self.chip, self.core)
        self.far = self.device((1 - self.high) * 2 + self.low, self.chip, self.core)

    def device(self, z, chip, core):
        return z * self.size + chip * 2 + core

    def column(self, hop):
        return self.device(lax.rem(self.z + hop, PLANES), self.chip, self.core)

    def peers(self):
        found = [self.across, self.pair, self.far]
        if self.direct:
            found = [self.across] + [self.column(hop) for hop in range(1, PLANES)]
        for hop in range(1, self.chips):
            found.append(self.device(self.z, lax.rem(self.chip + hop, self.chips), self.core))
        return found

    def patch(self, chip):
        row = pl.multiple_of((chip // self.cuts) * self.band, 8)
        col = self.core * self.half + (chip % self.cuts) * self.cut
        return row, pl.ds(pl.multiple_of(col, LANES), self.cut)

    def copy(self, hop, src, dst, device):
        pltpu.make_async_remote_copy(
            src_ref=src,
            dst_ref=dst,
            send_sem=self.sent.at[hop],
            recv_sem=self.got.at[hop],
            device_id=(device,),
            device_id_type=MESH,
        ).start()

    @staticmethod
    def settle(sem, held):
        pltpu.make_async_copy(held, held, sem).wait()

    def split(self, values, first_row):
        high = values.astype(self.total.dtype).astype(jnp.float32)
        middle = (values - high).astype(self.total.dtype).astype(jnp.float32)
        at = lax.broadcasted_iota(jnp.int32, values.shape, 0) + first_row - self.split_row
        rest = jnp.where(at == 1, values - high, values - high - middle)
        return jnp.where((at == 1) | (at == 2), rest, values)

    def column_step(self, at, band, cols, plane_shard, amount):
        part, total, shard = self.part, self.total, self.shard
        if at == 2:
            self.settle(self.got.at[1], self.from_chip)
            held = part[band, cols]
            for hop in range(1, self.chips):
                held = held + self.from_chip[hop - 1]
            part[band, cols] = held
            for hop in range(1, PLANES):
                src = part.at[plane_shard(lax.rem(self.z + hop, PLANES)), cols]
                dst = self.from_far.at[pl.ds((hop - 1) * shard, shard)]
                self.copy(3, src, dst, self.column(hop))
        elif at == 3:
            self.settle(self.got.at[3], self.from_far)
            held = part[plane_shard(self.z), cols]
            for hop in range(1, PLANES):
                held = held + self.from_far[pl.ds((hop - 1) * shard, shard), :]
            if self.split_row is not None:
                held = self.split(held, self.patch(self.chip)[0] + self.z * shard)
            total[plane_shard(self.z), cols] = held.astype(total.dtype)
            held = total.at[plane_shard(self.z), cols]
            for hop in range(1, PLANES):
                self.copy(4, held, held, self.column(hop))

    def step(self, at):
        part, total, shard = self.part, self.total, self.shard
        row, cols = self.patch(self.chip)
        band = pl.ds(row, self.band)

        def pairs(low):
            return pl.ds(pl.multiple_of(row + low * 2 * shard, 16), 2 * shard)

        def shards(high):
            return pl.ds(pl.multiple_of(row + (self.low * 2 + high) * shard, 16), shard)

        def amount(*shape):
            return total.at[pl.ds(0, shape[0]), pl.ds(0, shape[1])]

        short = self.band * total.dtype.itemsize // part.dtype.itemsize
        every_chip = self.from_chip.at[:, pl.ds(0, short)]

        def chips(hop):
            chip = lax.rem(self.chip + hop, self.chips)
            return chip, self.device(self.z, chip, self.core)

        def plane_shard(z):
            return pl.ds(pl.multiple_of(row + z * shard, 16), shard)

        if self.direct and 2 <= at <= 5:
            self.column_step(at, band, cols, plane_shard, amount)
        elif at == 0:
            self.copy(0, part.at[:, self.other], self.from_core, self.across)
        elif at == 1:
            self.settle(self.got.at[0], self.from_core)
            part[:, self.mine] += self.from_core[...]
            for hop in range(1, self.chips):
                chip, device = chips(hop)
                there, cut = self.patch(chip)
                src = part.at[pl.ds(there, self.band), cut]
                self.copy(1, src, self.from_chip.at[hop - 1], device)
        elif at == 2:
            self.settle(self.got.at[1], self.from_chip)
            held = part[band, cols]
            for hop in range(1, self.chips):
                held = held + self.from_chip[hop - 1]
            part[band, cols] = held
            self.copy(2, part.at[pairs(1 - self.low), cols], self.from_pair, self.pair)
        elif at == 3:
            self.settle(self.got.at[2], self.from_pair)
            part[pairs(self.low), cols] += self.from_pair[...]
            self.copy(3, part.at[shards(1 - self.high), cols], self.from_far, self.far)
        elif at == 4:
            self.settle(self.got.at[3], self.from_far)
            held = part[shards(self.high), cols] + self.from_far[...]
            if self.split_row is not None:
                held = self.split(held, row + (self.low * 2 + self.high) * shard)
            total[shards(self.high), cols] = held.astype(total.dtype)
            held = total.at[shards(self.high), cols]
            self.copy(4, held, held, self.far)
        elif at == 5:
            self.settle(self.got.at[4], amount(shard, self.cut))
            held = total.at[pairs(self.low), cols]
            self.copy(5, held, held, self.pair)
        elif at == 6:
            if self.direct:
                self.settle(self.got.at[4], amount((PLANES - 1) * shard, self.cut))
            else:
                self.settle(self.got.at[5], amount(2 * shard, self.cut))
            held = total.at[band, cols]
            for hop in range(1, self.chips):
                self.copy(6, held, held, chips(hop)[1])
        elif at == 7:
            self.settle(self.got.at[6], every_chip)
            held = total.at[:, self.mine]
            self.copy(7, held, held, self.across)
        else:
            self.settle(self.got.at[7], amount(self.rows, self.half))
            self.settle(self.sent.at[0], self.from_core)
            self.settle(self.sent.at[1], self.from_chip)
            self.settle(self.sent.at[3], self.from_far)
            if self.direct:
                self.settle(self.sent.at[4], amount((PLANES - 1) * shard, self.cut))
            else:
                self.settle(self.sent.at[2], self.from_pair)
                self.settle(self.sent.at[4], amount(shard, self.cut))
                self.settle(self.sent.at[5], amount(2 * shard, self.cut))
            self.settle(self.sent.at[6], every_chip)
            self.settle(self.sent.at[7], amount(self.rows, self.half))


def finish_kernel(n, tile, rows_there, grads, loss, total, part, rows, held, sem, *refs):
    fetches = [
        pltpu.make_async_copy(grads, held, sem.at[0]),
        pltpu.make_async_copy(rows_there, rows, sem.at[1]),
    ]
    for fetch in fetches:
        fetch.start()
    below = -(-rows.shape[0] // 8) * 8
    summer = Summer(n, part.shape, below, direct=True)
    summer.bind(part, total, refs)
    barrier = pltpu.get_barrier_semaphore()
    peers = summer.peers()
    for peer in peers:
        pl.semaphore_signal(barrier, inc=1, device_id=(peer,), device_id_type=MESH)
    count, depth = rows.shape

    def multiply(cols):
        part[:, cols] = jnp.zeros((part.shape[0], summer.half), jnp.float32)

        def add(at, carry):
            window = pl.ds(pl.multiple_of(at * tile, tile), tile)
            part[:count, cols] += mat_product(rows[:, window], held[window, cols])
            return carry

        lax.fori_loop(0, depth // tile, add, 0)
        part[pl.ds(below, 8), cols] = jnp.broadcast_to(loss[...], (8, summer.half))

    for fetch in fetches:
        fetch.wait()
    multiply(summer.other)
    pl.semaphore_wait(barrier, len(peers))
    summer.step(0)
    multiply(summer.mine)
    for at in range(1, Summer.STEPS):
        summer.step(at)


def finish(n, rows, grads, loss, collective):
    count = -(-rows.shape[0] // 8) * 8
    shape = (Summer.padded(n, count + 8, grads.shape[1]), grads.shape[1])
    vmem = pl.BlockSpec(memory_space=pltpu.VMEM)
    total = pl.pallas_call(
        functools.partial(finish_kernel, n, 1024),
        out_shape=jax.ShapeDtypeStruct(shape, jnp.bfloat16),
        in_specs=[
            pl.BlockSpec(memory_space=pltpu.HBM),
            pl.BlockSpec(memory_space=pltpu.HBM),
            vmem,
        ],
        out_specs=vmem,
        scratch_shapes=[
            pltpu.VMEM(shape, jnp.float32),
            pltpu.VMEM(rows.shape, rows.dtype),
            pltpu.VMEM(grads.shape, grads.dtype),
            pltpu.SemaphoreType.DMA((2,)),
        ]
        + Summer(n, shape, direct=True).scratch(),
        compiler_params=pltpu.CompilerParams(
            collective_id=collective, has_side_effects=True, vmem_limit_bytes=VMEM_MOST
        ),
        name="finish",
    )(rows, grads, loss)
    loss = jnp.sum(total[count : count + 3, 0].astype(jnp.float32))
    return total[: rows.shape[0]].astype(jnp.float32), loss


class Exchange:
    def __init__(self, n, slots, way, parts, far_cap, near_cap, shape, kind):
        self.n, self.slots, self.way, self.parts = n, slots, way, parts
        self.ahead, self.lead, self.sum_at = PACE[parts]
        self.far_cap, self.near_cap = far_cap, near_cap
        self.size = n // PLANES
        self.blocks, self.depth, self.width = shape
        self.kind = kind
        self.rows = self.depth // CHUNKS
        self.cols = self.width // self.parts
        self.steps = CHUNKS * self.parts
        self.ring = self.steps if self.size <= 8 else 2

    def out_shape(self):
        return jax.ShapeDtypeStruct(
            (CHUNKS, self.size, KINDS, self.slots, self.rows, self.width), self.kind
        )

    def scratch(self):
        def piece(*lead):
            return pltpu.VMEM(lead + (self.rows, self.cols), self.kind)

        steps, ring = self.steps, self.ring
        dma = pltpu.SemaphoreType.DMA
        return (
            [piece(self.near_cap) for _ in range(steps)]
            + [piece(2, self.far_cap) for _ in range(steps)]
            + [piece(steps, self.far_cap), piece(steps, self.near_cap)]
            + [piece(steps, 2, self.near_cap)]
            + [piece(ring, self.size, 2, self.slots) for _ in range(2)]
            + [dma, dma, dma, dma((steps,)), dma((steps,)), dma((2, ring)), dma((CHUNKS,))]
        )

    def bind(self, plan, table, out, refs):
        self.plan, self.table, self.out = plan.at[self.way], table, out
        steps = self.steps
        self.near_got, self.far_got = refs[:steps], refs[steps : 2 * steps]
        (
            self.far_stage,
            self.near_stage,
            self.pass_stage,
            first_stage,
            second_stage,
            self.far_sent,
            self.near_sent,
            self.pass_sent,
            self.near_recv,
            self.far_recv,
            self.serve_sent,
            self.serve_recv,
        ) = refs[2 * steps :]
        self.serve_stage = (first_stage, second_stage)
        me = lax.axis_index("nodes")
        self.z, self.spot, self.inner, near, far_in, far_out = place(me, self.size)
        self.near_dev = near * self.size + self.spot
        self.relay_dev = far_in * self.size + self.spot
        self.outer_dev = far_out * self.size + self.spot

    def greet(self, column=False):
        barrier = pltpu.get_barrier_semaphore()

        def hello(device):
            pl.semaphore_signal(barrier, inc=1, device_id=(device,), device_id_type=MESH)

        def in_plane(step, carry):
            hello(self.z * self.size + lax.rem(self.spot + step, self.size))
            return carry

        lax.fori_loop(1, self.size, in_plane, 0)
        hello(self.near_dev)
        if column:
            hello(((1 - self.z // 2) * 2 + self.z % 2) * self.size + self.spot)

            @pl.when(self.inner == 1)
            def _():
                hello(self.relay_dev)

            pl.semaphore_wait(barrier, self.size + 1 + self.inner)
            return

        @pl.when(self.inner == 1)
        def _():
            hello(self.relay_dev)
            hello(self.outer_dev)

        pl.semaphore_wait(barrier, self.size + 1)

    def window(self, step):
        return pl.ds((step // self.parts) * self.rows, self.rows), pl.ds(
            (step % self.parts) * self.cols, self.cols
        )

    def remote(self, src, dst, sent, got, device):
        return pltpu.make_async_remote_copy(
            src_ref=src,
            dst_ref=dst,
            send_sem=sent,
            recv_sem=got,
            device_id=(device,),
            device_id_type=MESH,
        )

    @staticmethod
    def settle(sem, held):
        pltpu.make_async_copy(held, held, sem).wait()

    def launch_far(self, step):
        rows, cols = self.window(step)
        plan, table, stage = self.plan, self.table, self.far_stage.at[step]

        def fill(at, carry):
            stage[at] = table[plan[ROW_FAR, at], rows, cols]
            return carry

        lax.fori_loop(0, self.far_cap, fill, 0)
        self.remote(
            stage,
            self.far_got[step].at[1 - self.inner],
            self.far_sent,
            self.far_recv.at[step],
            self.relay_dev,
        ).start()

    def launch_near(self, step):
        rows, cols = self.window(step)
        plan, table, stage = self.plan, self.table, self.near_stage.at[step]

        def fill(at, carry):
            stage[at] = table[plan[ROW_NEAR, at], rows, cols]
            return carry

        lax.fori_loop(0, self.near_cap, fill, 0)
        self.remote(
            stage, self.near_got[step], self.near_sent, self.near_recv.at[step], self.near_dev
        ).start()

    def relay(self, step):
        plan, got, stage = self.plan, self.far_got[step], self.pass_stage.at[step]
        part = got.at[:, pl.ds(0, self.near_cap)]

        @pl.when(self.inner == 1)
        def _():
            self.settle(self.far_recv.at[step], got)

            def fill(at, carry):
                for lane in range(2):
                    stage[lane, at] = got[lane, plan[ROW_PASS + lane, at]]
                return carry

            lax.fori_loop(0, self.near_cap, fill, 0)
            self.remote(
                stage, part, self.pass_sent, self.far_recv.at[step], self.near_dev
            ).start()

        @pl.when(self.inner == 0)
        def _():
            self.settle(self.far_recv.at[step], part)

    def serve(self, step, pair):
        rows, cols = self.window(step)
        plan, table, slots, size = self.plan, self.table, self.slots, self.size
        chunk, slot_at = step // self.parts, step % self.ring
        if pair == 0:
            self.settle(self.near_recv.at[step], self.near_got[step])
        if step >= self.ring:
            self.drain(step - self.ring, pair)
        stage = self.serve_stage[pair].at[slot_at]

        def fill(peer, carry):
            taker = self.z * size + peer
            for slot in range(slots):
                first = plan[ROW_SERVE + 2 * pair * slots + slot, taker]
                second = plan[ROW_SERVE + (2 * pair + 1) * slots + slot, taker]
                if pair == 0:
                    stage[peer, 0, slot] = table[first, rows, cols]
                    stage[peer, 1, slot] = self.near_got[step][second]
                else:
                    stage[peer, 0, slot] = self.far_got[step][0, first]
                    stage[peer, 1, slot] = self.far_got[step][1, second]
            return carry

        lax.fori_loop(0, size, fill, 0)
        there = self.out.at[chunk, self.spot, pl.ds(2 * pair, 2), :, :, cols]
        pltpu.make_async_copy(stage.at[self.spot], there, self.serve_recv.at[chunk]).start()

        def send(hop, carry):
            peer = lax.rem(self.spot + hop, size)
            self.remote(
                stage.at[peer],
                there,
                self.serve_sent.at[pair, slot_at],
                self.serve_recv.at[chunk],
                self.z * size + peer,
            ).start()
            return carry

        lax.fori_loop(1, size, send, 0)

    def drain(self, step, pair):
        slot_at = step % self.ring
        held = self.serve_stage[pair].at[slot_at, pl.ds(0, self.size - 1)]
        self.settle(self.serve_sent.at[pair, slot_at], held)

    def run(self, side=None):
        steps = self.steps
        for step in range(min(self.ahead, steps)):
            self.launch_far(step)
            self.launch_near(step)
        for step in range(min(self.lead, steps)):
            self.serve(step, 0)
        for step in range(steps):
            if step + self.ahead < steps:
                self.launch_far(step + self.ahead)
                self.launch_near(step + self.ahead)
            self.relay(step)
            self.serve(step, 1)
            if step + self.lead < steps:
                self.serve(step + self.lead, 0)
            if side is not None:
                side(step)
        if side is not None:
            side(steps)
        for chunk in range(CHUNKS):
            self.settle(self.serve_recv.at[chunk], self.out.at[chunk])
        def drain(at, carry):
            for pair in range(2):
                self.drain(at, pair)
            return carry

        lax.fori_loop(0, self.ring, drain, 0)
        self.settle(self.far_sent, self.far_stage)
        self.settle(self.near_sent, self.near_stage)

        @pl.when(self.inner == 1)
        def _():
            self.settle(self.pass_sent, self.pass_stage)


def exchange_kernel(moves, plan, table, out, held_table, table_sem, *refs):
    moves.bind(plan, held_table, out, refs)
    fetch = pltpu.make_async_copy(table, held_table, table_sem)
    fetch.start()
    moves.greet()
    fetch.wait()
    moves.run()


def exchange_sum_kernel(
    moves, summer, plan, table, part, out, total, held_table, table_sem, held, sem, *refs
):
    moves.bind(plan, held_table, out, refs[6:])
    fetch_table = pltpu.make_async_copy(table, held_table, table_sem)
    fetch_table.start()
    summer.bind(held, total, refs[:6])
    fetch = pltpu.make_async_copy(part, held, sem)
    fetch.start()
    moves.greet(column=True)
    fetch_table.wait()

    def side(step):
        if step == 0:
            fetch.wait()
        if step in moves.sum_at:
            summer.step(moves.sum_at.index(step))

    moves.run(side)


def exchange(n, slots, way, parts, far_cap, near_cap, collective, plan, table, part=None):
    moves = Exchange(n, slots, way, parts, far_cap, near_cap, table.shape, table.dtype)
    hbm = pl.BlockSpec(memory_space=pl.ANY)
    vmem = pl.BlockSpec(memory_space=pltpu.VMEM)
    in_specs = [pl.BlockSpec(memory_space=pltpu.SMEM), hbm]
    table_held = [pltpu.VMEM(table.shape, table.dtype), pltpu.SemaphoreType.DMA]
    params = pltpu.CompilerParams(
        collective_id=collective, has_side_effects=True, vmem_limit_bytes=VMEM_MOST
    )
    if part is None:
        return pl.pallas_call(
            functools.partial(exchange_kernel, moves),
            out_shape=moves.out_shape(),
            in_specs=in_specs,
            out_specs=hbm,
            scratch_shapes=table_held + moves.scratch(),
            compiler_params=params,
            name="exchange",
        )(plan, table)
    summer = Summer(n, part.shape)
    return pl.pallas_call(
        functools.partial(exchange_sum_kernel, moves, summer),
        out_shape=(moves.out_shape(), jax.ShapeDtypeStruct(part.shape, jnp.bfloat16)),
        in_specs=in_specs + [hbm],
        out_specs=(hbm, vmem),
        scratch_shapes=table_held
        + [pltpu.VMEM(part.shape, jnp.float32), pltpu.SemaphoreType.DMA]
        + summer.scratch()
        + moves.scratch(),
        compiler_params=params,
        name="exchange_sum",
    )(plan, table, part)


def add_products(flip, slots, first_row, sinks, weights, got, total, at, size):
    z, _, _, near, far_in, far_out = place(lax.axis_index("nodes"), size)
    depth, width = total.shape[1:]
    dims = (((0,), (0,)), ((), ())) if flip else (((1,), (0,)), ((), ()))
    for kind, owner_z in enumerate((z, near, far_in, far_out)):
        for slot in range(slots):
            sink = sinks[first_row + slot, owner_z * size + at]
            rows = got[:, 0, kind, slot].reshape(depth, width)
            total[sink] += lax.dot_general(
                weights[owner_z, 0, slot], rows, dims, preferred_element_type=jnp.float32
            )


def return_sum_kernel(slots, first_row, *refs):
    sinks, weights, got, own, mixer = refs[:5]
    states, head_state, out = refs[5:13], refs[13:17], refs[17]
    updates, head_update, total, mixer_half = refs[18:24], refs[24:27], refs[27], refs[28]
    at = pl.program_id(0)
    blocks, depth, width = out.shape

    @pl.when(at == 0)
    def _():
        total[...] = jnp.zeros_like(total)
        mixer_half[...] = to_half(mixer[0])
        label_width = head_state[0].shape[1]
        head_grad = head_state[1][...].astype(jnp.float32).T[:, :label_width]
        fresh = adam_update(head_state[0][...], head_grad, head_state[2][...], head_state[3][...])
        for to, values in zip(head_update, fresh):
            to[...] = values

    span = own.shape[0] // depth
    base = right_product(own[...], mixer_half[...]).reshape(span, depth, width)
    total[pl.ds(at * span, span)] += base
    for state, update in ((states[:4], updates[:3]), (states[4:], updates[3:])):
        grad = state[1][...].astype(jnp.float32)
        fresh = adam_update(state[0][...], grad, state[2][...], state[3][...])
        for to, values in zip(update, fresh):
            to[...] = values
    size = pl.num_programs(0)
    add_products(True, slots, first_row, sinks, weights, got, total, at, size)

    @pl.when(at == pl.num_programs(0) - 1)
    def _():
        out[...] = to_half(total[:blocks])


def block_specs(weights, got):
    chunks, size, kinds, slots, rows, width = got.shape
    depth = chunks * rows
    edges = weights.reshape(PLANES, size, slots, depth, depth)

    def clip(at):
        return jnp.minimum(at, size - 1)

    specs = [
        pl.BlockSpec((PLANES, 1, slots, depth, depth), lambda at, *_: (0, clip(at), 0, 0, 0)),
        pl.BlockSpec(
            (chunks, 1, kinds, slots, rows, width), lambda at, *_: (0, clip(at), 0, 0, 0, 0)
        ),
    ]
    return edges, specs


def return_sum(first_row, sinks, weights, got, blocks, own, mixer, grads, groups, head):
    chunks, size, _, slots, rows, width = got.shape
    depth = chunks * rows
    edges, specs = block_specs(weights, got)
    tile = blocks * depth // size
    specs = specs + [
        pl.BlockSpec((tile, width), lambda at, sinks: (at, 0)),
        pl.BlockSpec((1, width, width), lambda at, sinks: (0, 0, 0)),
    ]
    states, shapes, out_specs = [], [], []
    for place_at, (weight, first, second) in enumerate(groups):
        part = weight.shape[0] // size
        spec = pl.BlockSpec((part, width), lambda at, sinks: (at, 0))
        moved = pl.BlockSpec((part, width), lambda at, sinks, p=place_at: (at + p * size, 0))
        states += [weight, grads, first, second]
        specs = specs + [spec, moved, spec, spec]
        shapes += [jax.ShapeDtypeStruct(weight.shape, jnp.float32)] * 3
        out_specs += [spec] * 3
    head_at = 2 * groups[0][0].shape[0] // LANES
    still = pl.BlockSpec(head[0].shape, lambda at, sinks: (0, 0))
    states += [head[0], grads, head[1], head[2]]
    specs = specs + [still, pl.BlockSpec((LANES, width), lambda at, sinks: (head_at, 0)), still, still]
    shapes += [jax.ShapeDtypeStruct(head[0].shape, jnp.float32)] * 3
    out_specs += [still] * 3
    found = pl.pallas_call(
        functools.partial(return_sum_kernel, slots, first_row),
        out_shape=[jax.ShapeDtypeStruct((blocks, depth, width), jnp.bfloat16)] + shapes,
        grid_spec=pltpu.PrefetchScalarGridSpec(
            num_scalar_prefetch=1,
            grid=(size,),
            in_specs=specs,
            out_specs=[pl.BlockSpec((blocks, depth, width), lambda at, sinks: (0, 0, 0))]
            + out_specs,
            scratch_shapes=[
                pltpu.VMEM((blocks + 1, depth, width), jnp.float32),
                pltpu.VMEM((width, width), jnp.bfloat16),
            ],
        ),
        compiler_params=pltpu.CompilerParams(vmem_limit_bytes=48 * 2**20),
        name="return_sum",
    )(sinks, edges, got, own, mixer, *states)
    return found[0], found[1:4], found[4:7], found[7:10]


ROW_FAR, ROW_NEAR, ROW_PASS, ROW_SERVE = 0, 1, 2, 4


def plan_rows(slots):
    wishes = ROW_SERVE + KINDS * slots
    return wishes, -(-(wishes + slots) // 8) * 8


def column(values, lane):
    lanes = lax.broadcasted_iota(jnp.int32, values.shape, 1)
    return jnp.sum(jnp.where(lanes == lane, values, 0.0), axis=1, keepdims=True)


def lay_plan(n, slots, blocks, rungs, way, wishes_of, plan, chosen, present):
    size = n // PLANES
    me = lax.axis_index("nodes")
    z, spot, inner, near, far_in, far_out = place(me, size)
    half = z // 2
    row_wish, _ = plan_rows(slots)

    taker = lax.broadcasted_iota(jnp.int32, (LANES, LANES), 0)
    group = lax.broadcasted_iota(jnp.int32, (LANES, LANES), 1)
    plane_of = taker // size
    member = (taker < n) & ((plane_of == group) | (plane_of // 2 + PLANES == group))
    member = jnp.where(member, 1.0, 0.0).astype(jnp.bfloat16)
    hits = jnp.zeros((n * blocks, LANES), jnp.float32)
    for slot in range(slots):
        wish = wishes_of[slot][...]
        ids = lax.broadcasted_iota(jnp.int32, (n, blocks, LANES), 1)
        hot = jnp.where(wish[:, None, :] == ids, 1.0, 0.0).astype(jnp.bfloat16)
        hits = hits + mat_product(hot.reshape(n * blocks, LANES), member)
    here = jnp.where(hits > 0.0, 1.0, 0.0)
    present[...] = here
    counts = jnp.sum(here.reshape(n, blocks, LANES), axis=1)
    owner_plane = lax.broadcasted_iota(jnp.int32, (n, LANES), 0) // size
    lane = lax.broadcasted_iota(jnp.int32, (n, LANES), 1)
    is_near = (lane < PLANES) & (lane != owner_plane)
    is_far = (lane >= PLANES) & (lane < PLANES + 2) & (lane - PLANES != owner_plane // 2)
    near_most = jnp.max(jnp.where(is_near, counts, 0.0), axis=(0, 1), keepdims=True)
    far_most = jnp.max(jnp.where(is_far, counts, 0.0), axis=(0, 1), keepdims=True)
    rung = jnp.zeros((1, 1), jnp.float32)
    for far_cap, near_cap in rungs[:-1]:
        over = (far_most > float(far_cap)) | (near_most > float(near_cap))
        rung = rung + jnp.where(over, 1.0, 0.0)

    def put(row, values):
        plan[way, pl.ds(row, 1), :] = values.astype(jnp.int32)

    chosen[...] = len(rungs) - 1 - rung.astype(jnp.int32)
    block_id = lax.broadcasted_iota(jnp.int32, (blocks, LANES), 0)
    block_lane = lax.broadcasted_iota(jnp.int32, (blocks, LANES), 1)
    ids = block_id.astype(jnp.float32)
    below = lax.broadcasted_iota(jnp.int32, (blocks, blocks), 0) > lax.broadcasted_iota(
        jnp.int32, (blocks, blocks), 1
    )
    below = jnp.where(below, 1.0, 0.0).astype(jnp.bfloat16)

    def listed(chosen, pos, values):
        at = (chosen > 0.0) & (pos.astype(jnp.int32) == block_lane)
        return jnp.sum(jnp.where(at, values, 0.0), axis=0, keepdims=True)

    for kind, owner_z in enumerate((z, near, far_in, far_out)):
        owner = owner_z * size + spot
        mine = present[pl.ds(pl.multiple_of(owner * blocks, 8), blocks), :]
        rank = mat_product(below, mine.astype(jnp.bfloat16))
        if kind == 0:
            where_held = ids
            far = PLANES + 1 - half
            put(ROW_FAR, listed(column(mine, far), column(rank, far), ids))
            put(ROW_NEAR, listed(column(mine, near), column(rank, near), ids))
        elif kind == 1:
            where_held = column(rank, z)
        else:
            where_held = column(rank, z + inner * (PLANES + half - z))
            edge = 3 * half
            put(
                ROW_PASS + kind - 2,
                listed(column(mine, edge), column(rank, edge), column(rank, PLANES + half)),
            )
        for slot in range(slots):
            wish = wishes_of[slot][pl.ds(owner, 1), :]
            held = jnp.where(wish == block_id, where_held, 0.0)
            put(ROW_SERVE + kind * slots + slot, jnp.sum(held, axis=0, keepdims=True))
            if kind == 0:
                put(row_wish + slot, wish)


def prelude_kernel(n, slots, blocks, rungs, tile, *refs):
    need, target, alive, rows, weight, hidden, plan = refs[:7]
    chosen, sunk, mine, taken = refs[7:9], refs[9], refs[10], refs[11]
    wishes = refs[12 : 12 + 2 * slots]
    present, held, held_weight, row_sem, weight_sem, send_sem, recv_sem = refs[12 + 2 * slots :]
    tiles = rows.shape[1] // tile

    def window(at):
        return pl.ds(pl.multiple_of(at * tile, tile), tile)

    def fetch(at):
        part = window(at)
        return pltpu.make_async_copy(rows.at[:, part], held.at[:, part], row_sem.at[at])

    fetch_weight = pltpu.make_async_copy(weight, held_weight, weight_sem)
    fetch_weight.start()
    for at in range(tiles):
        fetch(at).start()
    me = lax.axis_index("nodes")
    barrier = pltpu.get_barrier_semaphore()

    def greet(step, carry):
        pl.semaphore_signal(
            barrier, inc=1, device_id=(lax.rem(me + step, n),), device_id_type=MESH
        )
        return carry

    lax.fori_loop(1, n, greet, 0)
    mine[...] = jnp.full(mine.shape, blocks, jnp.int32)
    sunk[...] = jnp.full(sunk.shape, blocks, jnp.int32)
    for slot in range(slots):
        live = slot < alive[...]
        sunk_row = jnp.where(live, target[pl.ds(slot, 1), :], blocks)
        mine[:, pl.ds(slot * LANES, n)] = jnp.where(live, need[pl.ds(slot, 1), :], blocks)
        mine[:, pl.ds((slots + slot) * LANES, n)] = sunk_row
        sunk[pl.ds(slot, 1), pl.ds(0, n)] = sunk_row
    taken[me] = mine[...]
    fetch_weight.wait()
    half_weight = to_half(held_weight[...])

    def project(at):
        fetch(at).wait()
        hidden[window(at), :] = to_half(left_product(held[:, window(at)], half_weight))

    for at in range(tiles // 2):
        project(at)
    pl.semaphore_wait(barrier, n - 1)

    def send(step, carry):
        pltpu.make_async_remote_copy(
            src_ref=mine,
            dst_ref=taken.at[me],
            send_sem=send_sem,
            recv_sem=recv_sem,
            device_id=(lax.rem(me + step, n),),
            device_id_type=MESH,
        ).start()
        return carry

    lax.fori_loop(1, n, send, 0)
    for at in range(tiles // 2, tiles):
        project(at)
    others = taken.at[pl.ds(0, n - 1)]
    pltpu.make_async_copy(others, others, recv_sem).wait()
    pltpu.make_async_copy(others, others, send_sem).wait()

    every = taken[...].reshape(n, 2 * slots * LANES)
    unit = lax.broadcasted_iota(jnp.int32, (n, LANES), 0) == lax.broadcasted_iota(
        jnp.int32, (n, LANES), 1
    )
    unit = jnp.where(unit, 1.0, 0.0).astype(jnp.bfloat16)
    for slot in range(slots):
        part = every[:, slot * LANES : (slot + 1) * LANES]
        turned = left_product(part.astype(jnp.float32).astype(jnp.bfloat16), unit)
        wishes[slot][...] = turned[:n].astype(jnp.int32)
        wishes[slots + slot][...] = every[:, (slots + slot) * LANES : (slots + slot + 1) * LANES]
    for way in range(2):
        lay_plan(
            n,
            slots,
            blocks,
            rungs,
            way,
            wishes[way * slots : (way + 1) * slots],
            plan,
            chosen[way],
            present,
        )


def prelude(n, slots, blocks, rungs, need, target, alive, rows, weight):
    count, width = rows.shape[1], weight.shape[1]
    vmem = pl.BlockSpec(memory_space=pltpu.VMEM)
    plan_shape = (2, plan_rows(slots)[1], LANES)
    return pl.pallas_call(
        functools.partial(prelude_kernel, n, slots, blocks, rungs, 512),
        out_shape=(
            jax.ShapeDtypeStruct((count, width), jnp.bfloat16),
            jax.ShapeDtypeStruct(plan_shape, jnp.int32),
            jax.ShapeDtypeStruct((1, 1), jnp.int32),
            jax.ShapeDtypeStruct((1, 1), jnp.int32),
            jax.ShapeDtypeStruct((8, LANES), jnp.int32),
        ),
        in_specs=[vmem, vmem, vmem] + [pl.BlockSpec(memory_space=pltpu.HBM)] * 2,
        out_specs=(vmem,) * 5,
        scratch_shapes=[
            pltpu.VMEM((1, 2 * slots * LANES), jnp.int32),
            pltpu.VMEM((n, 1, 2 * slots * LANES), jnp.int32),
        ]
        + [pltpu.VMEM((n, LANES), jnp.int32) for _ in range(2 * slots)]
        + [
            pltpu.VMEM((n * blocks, LANES), jnp.float32),
            pltpu.VMEM(rows.shape, rows.dtype),
            pltpu.VMEM(weight.shape, weight.dtype),
            pltpu.SemaphoreType.DMA((count // 512,)),
            pltpu.SemaphoreType.DMA,
            pltpu.SemaphoreType.DMA,
            pltpu.SemaphoreType.DMA,
        ],
        compiler_params=pltpu.CompilerParams(
            collective_id=0, has_side_effects=True, vmem_limit_bytes=VMEM_MOST
        ),
        name="prelude",
    )(need, target, alive, rows, weight)


def sigmoid(values):
    return 1.0 / (1.0 + jnp.exp(-values))


def dense_kernel(label_width, pieces, slots, first_row, count, sinks, edges, got, *refs):
    marks, truth, own = refs[:3]
    grad_own, grad_taken, part, loss, total = refs[6:11]
    pair, merge, head = refs[11:]
    at = pl.program_id(0)
    gathers = pl.num_programs(0) - total.shape[0] * total.shape[1] // own.shape[0]

    @pl.when(at == 0)
    def _():
        total[...] = jnp.zeros_like(total)
        part[...] = jnp.zeros_like(part)
        loss[...] = jnp.zeros_like(loss)
        for to, weight in zip((pair, merge), refs[3:5]):
            to[...] = to_half(weight[...])
        head[...] = to_half(jnp.pad(refs[5][...], ((0, 0), (0, LANES - label_width))))

    @pl.when(at < gathers)
    def _():
        add_products(False, slots, first_row, sinks, edges, got, total, at, gathers)

    @pl.when(at >= gathers)
    def _():
        span = own.shape[0] // total.shape[1]
        taken = total.at[pl.ds((at - gathers) * span, span)]
        dense_tile(
            label_width,
            pieces,
            (count, marks, truth, own, taken, pair, merge, head),
            (grad_own, grad_taken, part, loss),
        )


def dense_tile(label_width, pieces, given, made):
    count, marks, truth, own, taken, pair, merge, head = given
    grad_own, grad_taken, part, loss = made
    width = own.shape[1]
    tile = own.shape[0] // pieces
    span = taken.shape[0] // pieces
    denom = count[0].astype(jnp.float32) * float(label_width)

    def stages(piece):
        rows = pl.ds(piece * tile, tile)
        hidden = own[rows, :]
        gathered = to_half(taken[pl.ds(piece * span, span)]).reshape(tile, width)
        self_part = to_half(mat_product(hidden, pair[0]))
        neigh_part = to_half(mat_product(gathered, pair[1]))
        yield
        linear = mat_product(self_part, merge[:width]) + mat_product(neigh_part, merge[width:])
        yield
        sig = sigmoid(linear)
        active = linear * sig
        scale = lax.rsqrt(jnp.sum(active * active, axis=1, keepdims=True) + norm_eps)
        output = active * scale
        final = to_half(output)
        yield
        logits = mat_product(final, head[...])
        yield
        labels = truth[rows, :].astype(jnp.float32)
        labels = jnp.pad(labels, ((0, 0), (0, LANES - label_width)))
        marked = marks[0, :, rows].astype(jnp.float32)
        marked = jnp.broadcast_to(marked, (LANES, tile)).T
        column_id = lax.broadcasted_iota(jnp.int32, (tile, LANES), 1)
        marked = jnp.where(column_id < label_width, marked, 0.0)
        decay = jnp.exp(-jnp.abs(logits))
        entry = jnp.maximum(logits, 0.0) - logits * labels + jnp.log1p(decay)
        loss[...] += jnp.sum(entry * marked, axis=(0, 1), keepdims=True) / denom
        grad_logits = to_half((sigmoid(logits) - labels) * marked / denom)
        yield
        part[pl.ds(4 * width, LANES), :] += left_product(grad_logits, final)
        grad_out = right_product(grad_logits, head[...])
        yield
        along = jnp.sum(grad_out * output, axis=1, keepdims=True)
        grad_active = scale * (grad_out - output * along)
        grad_linear = to_half(grad_active * sig * (1.0 + linear * (1.0 - sig)))
        yield
        part[pl.ds(2 * width, width), :] += left_product(self_part, grad_linear)
        part[pl.ds(3 * width, width), :] += left_product(neigh_part, grad_linear)
        grad_self = to_half(right_product(grad_linear, merge[:width]))
        grad_neigh = to_half(right_product(grad_linear, merge[width:]))
        yield
        grad_own[rows, :] = grad_self
        part[pl.ds(0, width), :] += left_product(hidden, grad_self)
        part[pl.ds(width, width), :] += left_product(gathered, grad_neigh)
        grad_taken[rows, :] = to_half(right_product(grad_neigh, pair[1]))
        yield

    running = [stages(piece) for piece in range(pieces)]
    for turn in range(STAGES + SKEW * (pieces - 1)):
        for piece in range(pieces):
            if 0 <= turn - SKEW * piece < STAGES:
                next(running[piece])


def dense(tile, pieces, part_rows, first_row, scalars, edges, got, marks, truth, own, weights):
    rows, width = own.shape
    label_width = truth.shape[1]
    size, slots = got.shape[1], got.shape[3]
    edges, specs = block_specs(edges, got)
    depth = edges.shape[-1]

    def later(at):
        return jnp.maximum(at - size, 0)

    by_rows = pl.BlockSpec((tile, width), lambda at, *_: (later(at), 0))

    def whole(values):
        return pl.BlockSpec(
            values.shape, lambda at, *_: (0,) * values.ndim, pipeline_mode=pl.Buffered(1)
        )

    return pl.pallas_call(
        functools.partial(dense_kernel, label_width, pieces, slots, first_row),
        out_shape=(
            jax.ShapeDtypeStruct((rows, width), jnp.bfloat16),
            jax.ShapeDtypeStruct((rows, width), jnp.bfloat16),
            jax.ShapeDtypeStruct((part_rows, width), jnp.float32),
            jax.ShapeDtypeStruct((1, 1), jnp.float32),
        ),
        grid_spec=pltpu.PrefetchScalarGridSpec(
            num_scalar_prefetch=2,
            grid=(size + rows // tile,),
            in_specs=specs
            + [
                pl.BlockSpec((1, 1, tile), lambda at, *_: (later(at), 0, 0)),
                pl.BlockSpec((tile, label_width), lambda at, *_: (later(at), 0)),
                by_rows,
            ]
            + [whole(values) for values in weights],
            out_specs=(
                by_rows,
                by_rows,
                pl.BlockSpec((part_rows, width), lambda at, *_: (0, 0)),
                pl.BlockSpec((1, 1), lambda at, *_: (0, 0)),
            ),
            scratch_shapes=[pltpu.VMEM((rows // depth + 1, depth, width), jnp.float32)]
            + [pltpu.VMEM(values.shape, jnp.bfloat16) for values in weights[:2]]
            + [pltpu.VMEM((width, LANES), jnp.bfloat16)],
        ),
        compiler_params=pltpu.CompilerParams(vmem_limit_bytes=VMEM_MOST),
        name="dense",
    )(*scalars, edges, got, marks.reshape(rows // tile, 1, tile), truth, own, *weights)


def shards(
    features,
    labels,
    labelled,
    label_count,
    need_blocks,
    need_count,
    target_block,
    adjacency,
    embed_weight,
    pair_weight,
    merge_weight,
    head_weight,
    embed_moment,
    pair_moment,
    merge_moment,
    head_moment,
    embed_variance,
    pair_variance,
    merge_variance,
    head_variance,
):
    row_count = features.shape[0]
    hidden_width = embed_weight.shape[1]
    block_rows = adjacency.shape[1]
    slots = need_blocks.shape[2]
    n = lax.axis_size("nodes")
    size = n // PLANES
    block_count = row_count // block_rows
    near_full = min(block_count, size * slots)
    rungs = [(22, 15), (24, 16), (block_count, near_full)]
    if near_full > 16 or block_count < 24:
        rungs = rungs[-1:]
    hidden_half, plan, *rung_of, sunk = prelude(
        n,
        slots,
        block_count,
        rungs,
        need_blocks[0].T,
        target_block[0].T,
        need_count,
        features.T,
        embed_weight,
    )
    row_wish, _ = plan_rows(slots)

    def swap(way, *held):
        def at(rung):
            far_cap, near_cap = rungs[rung]
            parts = 4 if rung == 0 else 2
            return lambda *held: exchange(
                n, slots, way, parts, far_cap, near_cap, 2 + way * len(rungs) + rung, *held
            )

        if len(rungs) == 1:
            return at(0)(plan, *held)
        branches = [at(rung) for rung in reversed(range(len(rungs)))]
        return lax.switch(rung_of[way].reshape(()), branches, plan, *held)

    got = swap(0, hidden_half.reshape(block_count, block_rows, hidden_width))
    later, got = lax.optimization_barrier((adjacency, got))
    edges_back = lax.all_to_all(later, "nodes", split_axis=0, concat_axis=0, tiled=True)
    label_width = labels.shape[1]
    part_rows = Summer.padded(n, 4 * hidden_width + LANES, hidden_width)
    grad_self, grad_gathered, part, loss_part = dense(
        min(TILE, row_count),
        PIECES,
        part_rows,
        0,
        (label_count, sunk),
        adjacency,
        got,
        labelled,
        labels,
        hidden_half,
        (pair_weight[0], merge_weight[0], head_weight),
    )
    back, total = swap(1, grad_gathered.reshape(block_count, block_rows, hidden_width), part)
    def flat(values):
        return values.reshape(-1, hidden_width)

    grad_hidden, pair_next, merge_next, head_next = return_sum(
        row_wish,
        plan.reshape(-1, LANES),
        edges_back,
        back,
        block_count,
        grad_self,
        pair_weight[0],
        total,
        (
            (flat(pair_weight), flat(pair_moment), flat(pair_variance)),
            (flat(merge_weight), flat(merge_moment), flat(merge_variance)),
        ),
        (head_weight, head_moment, head_variance),
    )
    pair_next = [values.reshape(pair_weight.shape) for values in pair_next]
    merge_next = [values.reshape(merge_weight.shape) for values in merge_next]
    grad_hidden = grad_hidden.reshape(row_count, hidden_width)
    embed_grad, loss_total = finish(n, features.T, grad_hidden, loss_part, 1)
    embed_next = adam_update(embed_weight, embed_grad, embed_moment, embed_variance)
    return (
        loss_total.reshape(1),
        embed_next[0],
        pair_next[0],
        merge_next[0],
        head_next[0],
        embed_next[1],
        pair_next[1],
        merge_next[1],
        head_next[1],
        embed_next[2],
        pair_next[2],
        merge_next[2],
        head_next[2],
    )


def solution(mesh):
    split = ("nodes",)
    return jax.shard_map(
        shards,
        mesh=mesh,
        in_specs=(
            P("nodes", None),
            P("nodes", None),
            P("nodes"),
            P(),
            P("nodes", None, None),
            P("nodes", None),
            P("nodes", None, None),
            P("nodes", None, None),
        )
        + (P(),) * 12,
        out_specs=(P(),) * 13,
        check_vma=False,
    )
```
